32 devices in a mesh: row: 8 (over z, core), col: 4 (over y, x).
Axes of the slice: x: 2, y: 2, z: 4, core: 2. Of those that a mesh axis runs over, the one named last changes fastest.
Arguments:
- tokens: bfloat16 [2, 2048, 2048], P(None, 'row', 'col'), may hold values from -6 to 6
- routes: int32 [2, 2048, 4], P(None, 'row'), may hold values from 0 to 7, all different within a row; in each aligned block of 256 rows (0 to 255, 256 to 511, ..., all dimensions but the last counted through in order) at most 170 rows name the same one
- route_weights: float32 [2, 2048, 4], P(None, 'row'), may hold values from 0.1 to 0.6
- group_ids: int32 [2, 16], P(None, 'row'), may hold values from 0 to 1
- first_gain: bfloat16 [2048], P('row'), may hold values from 0.099609375 to 1.8984375
- query_weight: bfloat16 [2048, 2048], P('row', 'col'), may hold values from -0.125 to 0.125
- key_weight: bfloat16 [2048, 2048], P('row', 'col'), may hold values from -0.125 to 0.125
- value_weight: bfloat16 [2048, 2048], P('row', 'col'), may hold values from -0.125 to 0.125
- output_weight: bfloat16 [2048, 2048], P('col', 'row'), may hold values from -0.5 to 0.5
- second_gain: bfloat16 [2048], P('row'), may hold values from 0.099609375 to 1.8984375
- shared_gate: bfloat16 [2048, 5632], P('row', 'col'), may hold values from -0.125 to 0.125
- shared_up: bfloat16 [2048, 5632], P('row', 'col'), may hold values from -0.125 to 0.125
- shared_down: bfloat16 [5632, 2048], P('col', 'row'), may hold values from -0.15625 to 0.15625
- shared_logit: bfloat16 [2048], P('row'), may hold values from -0.125 to 0.125
- expert_gate: bfloat16 [2048, 8, 1408], P('row', 'col'), may hold values from -0.125 to 0.125
- expert_up: bfloat16 [2048, 8, 1408], P('row', 'col'), may hold values from -0.125 to 0.125
- expert_down: bfloat16 [8, 1408, 2048], P('col', None, 'row'), may hold values from -0.3125 to 0.3125
- cotangent: bfloat16 [2, 2048, 2048], P(None, 'row', 'col'), may hold values from -6 to 6
Outputs:
- result: bfloat16 [2, 2048, 2048], P(None, 'row', 'col')
- token_grad: float32 [2, 2048, 2048], P(None, 'row', 'col')
- first_gain_grad: float32 [2048], P('row')
- query_grad: float32 [2048, 2048], P('row', 'col')
- key_grad: float32 [2048, 2048], P('row', 'col')
- value_grad: float32 [2048, 2048], P('row', 'col')
- output_grad: float32 [2048, 2048], P('col', 'row')
- second_gain_grad: float32 [2048], P('row')
- shared_gate_grad: float32 [2048, 5632], P('row', 'col')
- shared_up_grad: float32 [2048, 5632], P('row', 'col')
- shared_down_grad: float32 [5632, 2048], P('col', 'row')
- shared_logit_grad: float32 [2048], P('row')
- expert_gate_grad: float32 [2048, 8, 1408], P('row', 'col')
- expert_up_grad: float32 [2048, 8, 1408], P('row', 'col')
- expert_down_grad: float32 [8, 1408, 2048], P('col', None, 'row')
The draws below stay inside these ranges and needn't reach their ends.
Inputs may be any that keep to these rules, and one draw needn't show every extreme that they name: `routes`: within the 256 rows of one device in one micro-batch no expert is named by more than 170 rows, and in every draw some expert is named by exactly 170 rows of some device; each row names 4 different experts. `group_ids`: each continuation follows one of the 2 prompts of its own device block and micro-batch.
All inputs are finite; a program needn't handle non-finite values.
Results may differ from the reference program's by a relative error of at most 0.025.
Values may be sent and summed in bfloat16 or wider, within the bound.
No kernel may reach another device: no remote copies, remote signals or barrier semaphores. Data moves between devices by JAX's collectives and lax.ppermute only.
A program may use at most 256 MiB of HBM per device.

```python
import math
import jax
import jax.numpy as jnp
import numpy as np
from jax import lax

D = 2048
HEADS = 16
HEAD_DIM = 128
EXPERT_FF = 1408
SHARED_FF = 5632
TOPK = 4
EXPERTS = 8
MICRO = 2
PROMPTS = 2
CONTS = 2
CONT_LEN = 64
PROMPT_LEN = 64
TOK_DEV = 256
TOKENS = 2048
CAP = 170
N_ROW = 8


def with_ends(values, rng, smallest, high):
    shape = values.shape
    index_at = [jax.random.randint(jax.random.fold_in(rng, axis), (), 0, shape[axis]) for axis in range(len(shape))]
    values = values.at[tuple(index_at)].set(smallest)
    longest = shape.index(max(shape))
    index_at[longest] = (index_at[longest] + 1) % shape[longest]
    return values.at[tuple(index_at)].set(high)


def raised(array, own_key, source, target, parts, factor):
    owner, partner = [(jnp.arange(array.shape[dim]) // (array.shape[dim] // parts)).reshape([-1 if axis == dim else 1 for axis in range(array.ndim)]) for dim in (source, target)]
    chosen = jax.random.permutation(own_key, parts)[partner]
    strong = (owner == chosen) | (owner == (partner + parts // 2) % parts)
    return jnp.where(strong, factor * array, array)


def shard_levels(rng, dims, cuts, smallest, high):
    level, own = 1.0, jax.random.fold_in(rng, 6)
    for axis_at, blocks in cuts:
        steps = jnp.exp(jax.random.uniform(jax.random.fold_in(own, axis_at), (blocks,), jnp.float32, smallest / len(cuts), high / len(cuts)))
        level = level * jnp.repeat(steps, dims[axis_at] // blocks).reshape([-1 if axis == axis_at else 1 for axis in range(len(dims))])
    return level


def assign_block(key, own, number, rows, number_of, top, most, lean):
    order = jax.random.permutation(key, number_of)
    heavy_load, ordinary = load_shares(number_of, rows * top, most, lean, True), load_shares(number_of, rows * top, most, lean, False)
    places = jnp.arange(number_of)

    def named(sizes, rotation):
        used = int((sizes > 0).sum())
        fixed = max(1, used // 4)
        moved = fixed + (places - fixed + rotation * (used - fixed)) % max(1, number_of - fixed)
        return jnp.zeros((number_of,), jnp.int32).at[order[jnp.where(places < fixed, places, moved)]].set(jnp.asarray(sizes, jnp.int32))

    sizes = jnp.where(number % 4 == 0, named(heavy_load, number // 4), named(ordinary, number - number // 4 - 1))
    mixed = jax.random.permutation(jax.random.fold_in(own, 3), number_of)
    giver, receiver = mixed[0:number_of // 2 * 2:2], mixed[1:number_of // 2 * 2:2]
    room = jnp.minimum(sizes[giver] - 1, most - sizes[receiver]) // 2
    room = jnp.where((giver == order[0]) | (receiver == order[0]) | (sizes[receiver] == 0), 0, jnp.maximum(room, 0))
    moved = jax.random.randint(jax.random.fold_in(own, 4), (number_of // 2,), 0, 1 << 20) % (room + 1)
    sizes = sizes.at[giver].add(-moved).at[receiver].add(moved)
    items = jnp.searchsorted(jnp.cumsum(sizes), jnp.arange(rows * top), side="right").astype(jnp.int32)
    grid = items.reshape(top, rows).T
    grid = grid[jax.random.permutation(jax.random.fold_in(own, 1), rows)]
    rotation = jax.random.randint(jax.random.fold_in(own, 2), (rows, 1), 0, top)
    return jnp.take_along_axis(grid, (jnp.arange(top)[None, :] + rotation) % top, axis=1)


def load_shares(amount, total, limit, lean, full):
    loads = [(1 << 20) // math.isqrt(rank ** lean) + 1 for rank in range(1, amount + 1)]
    largest = limit if full else min(limit, max(-(-total // amount), total * loads[0] // sum(loads)))
    least = 1 if total - largest >= amount - 1 else 0
    given, rest = [largest] + [least] * (amount - 1), total - largest - least * (amount - 1)
    while rest > 0:
        movable = [i for i in range(1, amount) if given[i] < largest] or [i for i in range(1, amount) if given[i] < limit]
        mass, budget = sum([loads[i] for i in movable]), rest
        for i in movable:
            addition = min(limit - given[i], max(1, budget * loads[i] // mass), rest)
            given[i] = given[i] + addition
            rest = rest - addition
    return np.array(given)


def noise(rng, shape, spread, limit, shards=(), kind=jnp.bfloat16):
    drawn = spread * jax.random.normal(rng, shape, jnp.float32)
    if shards:
        drawn = drawn * shard_levels(rng, shape, shards, -0.22, 0.18)
    return jnp.clip(drawn, -limit, limit).astype(kind)


def noise_with(rng, dims, deviation, bound, split, heavy, held_as=jnp.bfloat16):
    result = deviation * jax.random.normal(rng, dims, jnp.float32)
    if split:
        result = result * shard_levels(rng, dims, split, -0.22, 0.18)
    return jnp.clip(raised(result, jax.random.fold_in(rng, 3), *heavy), -bound, bound).astype(held_as)


def setup_inputs(seed: int = 0) -> dict:
    key_list = jax.random.split(jax.random.key(seed), 19)
    tokens = noise(key_list[0], (MICRO, TOKENS, D), 1.0, 6.0, ((1, 8), (2, 4)))
    routes_keys = jax.random.split(jax.random.fold_in(key_list[1], 1), MICRO * TOKENS // TOK_DEV)
    routes_turns = jax.random.permutation(jax.random.fold_in(key_list[1], 3), MICRO * TOKENS // TOK_DEV)
    routes = jax.vmap(lambda own, number: assign_block(jax.random.fold_in(key_list[1], 2), own, number, TOK_DEV, EXPERTS, TOPK, CAP, 1))(routes_keys, routes_turns).reshape((MICRO, TOKENS, TOPK))
    route_weights = jnp.clip(jnp.exp(math.log(0.6) - 1.7917595 * jax.random.uniform(key_list[2], (MICRO, TOKENS, TOPK), jnp.float32) ** shard_levels(key_list[2], (MICRO, TOKENS, TOPK), ((1, 8),), -0.2, 0.2)), 0.1, 0.6)
    group_ids = with_ends(jax.random.randint(key_list[3], (MICRO, CONTS * N_ROW), 0, PROMPTS), jax.random.fold_in(key_list[3], 1), 0, PROMPTS - 1).astype(jnp.int32)
    first_gain = jnp.clip(1.0 + 0.18 * jax.random.normal(key_list[4], (D,), jnp.float32), 0.099609375, 1.8984375).astype(jnp.bfloat16)
    query_weight = noise(key_list[5], (D, D), D ** -0.5, 0.125, ((0, 8), (1, 4)))
    key_weight = noise(key_list[6], (D, D), D ** -0.5, 0.125, ((0, 8), (1, 4)))
    value_weight = noise(key_list[7], (D, D), D ** -0.5, 0.125, ((0, 8), (1, 4)))
    output_weight = noise(key_list[8], (D, D), (D // 16) ** -0.5, 0.5, ((0, 4), (1, 8)))
    second_gain = jnp.clip(1.0 + 0.18 * jax.random.normal(key_list[9], (D,), jnp.float32), 0.099609375, 1.8984375).astype(jnp.bfloat16)
    shared_gate = noise(key_list[10], (D, SHARED_FF), D ** -0.5, 0.125, ((0, 8), (1, 4)))
    shared_up = noise(key_list[11], (D, SHARED_FF), D ** -0.5, 0.125, ((0, 8), (1, 4)))
    shared_down = noise(key_list[12], (SHARED_FF, D), (SHARED_FF // 4) ** -0.5, 0.15625, ((0, 4), (1, 8)))
    shared_logit = noise(key_list[13], (D,), D ** -0.5, 0.125, ((0, 8),))
    expert_gate = noise(key_list[14], (D, EXPERTS, EXPERT_FF), D ** -0.5, 0.125, ((0, 8), (1, 4)))
    expert_up = noise(key_list[15], (D, EXPERTS, EXPERT_FF), D ** -0.5, 0.125, ((0, 8), (1, 4)))
    expert_down = noise(key_list[16], (EXPERTS, EXPERT_FF, D), (EXPERT_FF // 4) ** -0.5, 0.3125, ((0, 4), (2, 8)))
    cotangent = noise_with(key_list[17], (MICRO, TOKENS, D), 1.0, 6.0, ((1, 8), (2, 4)), (1, 2, 8, 2.0))
    return {"tokens": tokens, "routes": routes, "route_weights": route_weights, "group_ids": group_ids, "first_gain": first_gain, "query_weight": query_weight, "key_weight": key_weight, "value_weight": value_weight, "output_weight": output_weight, "second_gain": second_gain, "shared_gate": shared_gate, "shared_up": shared_up, "shared_down": shared_down, "shared_logit": shared_logit, "expert_gate": expert_gate, "expert_up": expert_up, "expert_down": expert_down, "cotangent": cotangent}


@jax.custom_vjp
def low(v):
    return lax.optimization_barrier(v.astype(jnp.bfloat16)).astype(jnp.float32)

@jax.custom_vjp
def low_back(v):
    return v

def low_keep(v):
    return (low(v), None)

def low_pass(kept, grad):
    return (grad,)

def back_keep(v):
    return (v, None)

def back_low(kept, grad):
    return (low(grad),)
low.defvjp(low_keep, low_pass)
low_back.defvjp(back_keep, back_low)
epsilon = 1e-06
rope_base = 1000000.0
masked_score = -1000000000.0

def matmul(left, right):
    return jnp.dot(left, right, precision=lax.Precision.HIGHEST, preferred_element_type=jnp.float32)

def block_layout(groups):
    token_index = jnp.arange(TOK_DEV, dtype=jnp.int32)
    prompt_rows = PROMPTS * PROMPT_LEN
    is_prompt = token_index < prompt_rows
    cont_offset = jnp.maximum(token_index - prompt_rows, 0)
    cont_number = cont_offset // CONT_LEN
    segment = jnp.where(is_prompt, token_index // PROMPT_LEN, PROMPTS + cont_number)
    position = jnp.where(is_prompt, token_index % PROMPT_LEN, PROMPT_LEN + cont_offset % CONT_LEN)
    cont_picks = (cont_number[:, None] == jnp.arange(CONTS, dtype=jnp.int32)[None, :]).astype(jnp.int32)
    source = jnp.where(is_prompt, segment, lax.optimization_barrier(jnp.sum(cont_picks * groups[None, :], axis=1)))
    same_segment = (segment[:, None] == segment[None, :]) & (position[None, :] <= position[:, None])
    context = jnp.logical_not(is_prompt)[:, None] & is_prompt[None, :] & (source[:, None] == segment[None, :])
    return (same_segment | context, position)

def rotary_tables(position):
    half_dim = HEAD_DIM // 2
    frequency = rope_base ** (-(2.0 * jnp.arange(half_dim, dtype=jnp.float32)) / HEAD_DIM)
    angles = position.astype(jnp.float32)[:, None] * frequency[None, :]
    return (jnp.cos(angles), jnp.sin(angles))

def rotate(values, cosine, sine_rows):
    half_dim = HEAD_DIM // 2
    first_half = values[..., :half_dim]
    second = values[..., half_dim:]
    cos_rows = cosine[:, None, :]
    sin_rows = sine_rows[:, None, :]
    return jnp.concatenate([first_half * cos_rows - second * sin_rows, second * cos_rows + first_half * sin_rows], axis=-1)

def attend(pieces):
    queries, key_rows, value_rows, groups = pieces
    allowed, position = block_layout(groups)
    cosine, sine_rows = rotary_tables(position)
    head_shape = (TOK_DEV, HEADS, HEAD_DIM)
    query_rot = low(rotate(queries.reshape(head_shape), cosine, sine_rows))
    key_rot = low(rotate(key_rows.reshape(head_shape), cosine, sine_rows))
    value_low = low(value_rows.reshape(head_shape))
    raw_scores = jnp.einsum('qhd,khd->hqk', query_rot, key_rot, precision=lax.Precision.HIGHEST)
    scores = jnp.where(allowed[None], low_back(raw_scores) * (1.0 / math.sqrt(HEAD_DIM)), masked_score)
    probabilities = jax.nn.softmax(scores, axis=-1)
    mixed_heads = jnp.einsum('hqk,khd->qhd', low(probabilities), value_low, precision=lax.Precision.HIGHEST)
    return low(low_back(mixed_heads)).reshape(TOK_DEV, D)

def forward(inputs, groups, route_rows, route_share, weights):
    first_gain, query_weight, key_weight, value_weight, output_weight, second_gain, shared_gate, shared_up, shared_down, shared_logit, expert_gate, expert_up, expert_down = weights
    first_scale = lax.rsqrt(lax.optimization_barrier(jnp.mean(inputs * inputs, axis=-1, keepdims=True)) + epsilon)
    first_normed = low(inputs * first_scale * first_gain)
    queries = low_back(matmul(first_normed, query_weight))
    key_rows = low_back(matmul(first_normed, key_weight))
    value_rows = low_back(matmul(first_normed, value_weight))
    block_shape = (N_ROW, TOK_DEV, D)
    mixed_heads = lax.map(jax.checkpoint(attend), (queries.reshape(block_shape), key_rows.reshape(block_shape), value_rows.reshape(block_shape), groups.reshape(N_ROW, CONTS)))
    attention = low_back(matmul(mixed_heads.reshape(TOKENS, D), output_weight))
    hidden = inputs + attention
    second_scale = lax.rsqrt(lax.optimization_barrier(jnp.mean(hidden * hidden, axis=-1, keepdims=True)) + epsilon)
    second_normed = low(hidden * second_scale * second_gain)
    gate_pre = low_back(matmul(second_normed, shared_gate))
    up_pre = low_back(matmul(second_normed, shared_up))
    shared_act = low(jax.nn.silu(gate_pre) * up_pre)
    shared_out = low_back(matmul(shared_act, shared_down))
    shared_prob = jax.nn.sigmoid(matmul(second_normed, shared_logit))
    expert_hits = route_rows[:, :, None] == jnp.arange(EXPERTS, dtype=jnp.int32)[None, None, :]
    mixing = lax.optimization_barrier(jnp.sum(jnp.where(expert_hits, route_share[:, :, None], 0.0), axis=1))

    def expert_step(running, pieces):
        gate_block, up_block, down_block, share_column = pieces
        expert_gate_pre = low_back(matmul(second_normed, gate_block))
        expert_up_pre = low_back(matmul(second_normed, up_block))
        expert_act = low(jax.nn.silu(expert_gate_pre) * expert_up_pre)
        expert_out = low_back(matmul(expert_act, down_block))
        return (running + share_column[:, None] * expert_out, None)
    routed, _ = lax.scan(jax.checkpoint(expert_step), jnp.zeros((TOKENS, D), jnp.float32), (jnp.transpose(expert_gate, (1, 0, 2)), jnp.transpose(expert_up, (1, 0, 2)), expert_down, mixing.T))
    return hidden + shared_prob[:, None] * shared_out + routed

def reference(tokens, routes, route_weights, group_ids, first_gain, query_weight, key_weight, value_weight, output_weight, second_gain, shared_gate, shared_up, shared_down, shared_logit, expert_gate, expert_up, expert_down, cotangent):
    float_weights = tuple((weight.astype(jnp.float32) for weight in (first_gain, query_weight, key_weight, value_weight, output_weight, second_gain, shared_gate, shared_up, shared_down, shared_logit, expert_gate, expert_up, expert_down)))
    totals = tuple((jnp.zeros_like(weight) for weight in float_weights))
    results = []
    input_grads = []
    for batch_index in range(MICRO):

        def single_batch(inputs, weights):
            return forward(inputs, group_ids[batch_index], routes[batch_index], route_weights[batch_index], weights)
        outputs, pull_back = jax.vjp(single_batch, tokens[batch_index].astype(jnp.float32), float_weights)
        inputs_grad, weight_grads = pull_back(cotangent[batch_index].astype(jnp.float32))
        totals = tuple((left_term + right_term for left_term, right_term in zip(totals, weight_grads)))
        results.append(outputs.astype(jnp.bfloat16))
        input_grads.append(inputs_grad)
    return (jnp.stack(results), jnp.stack(input_grads), totals[0], totals[1], totals[2], totals[3], totals[4], totals[5], totals[6], totals[7], totals[8], totals[9], totals[10], totals[11], totals[12])
```

```python
import functools
import math

import jax
import jax.numpy as jnp
from jax import lax
from jax.experimental import pallas as pl
from jax.experimental.pallas import tpu as pltpu
from jax.sharding import Mesh, PartitionSpec as P

HEAD_DIM = 128
EXPERTS = 8
PROMPTS = 2
CONTS = 2
CONT_LEN = 64
PROMPT_LEN = 64

epsilon = 1e-06
rope_base = 1000000.0
masked_score = -1000000000.0

F32 = jnp.float32
BF16 = jnp.bfloat16
COL = ("y", "x")
ROW = ("g", "k")
ALL = ("g", "k", "y", "x")


def block_layout(groups, row_count):
    token_index = jnp.arange(row_count, dtype=jnp.int32)
    prompt_rows = PROMPTS * PROMPT_LEN
    is_prompt = token_index < prompt_rows
    cont_offset = jnp.maximum(token_index - prompt_rows, 0)
    cont_number = cont_offset // CONT_LEN
    segment = jnp.where(is_prompt, token_index // PROMPT_LEN, PROMPTS + cont_number)
    position = jnp.where(is_prompt, token_index % PROMPT_LEN, PROMPT_LEN + cont_offset % CONT_LEN)
    cont_picks = (cont_number[:, None] == jnp.arange(CONTS, dtype=jnp.int32)[None, :]).astype(
        jnp.int32
    )
    source = jnp.where(
        is_prompt[None], segment[None], jnp.sum(cont_picks[None] * groups[:, None, :], axis=2)
    )
    same_segment = (segment[:, None] == segment[None, :]) & (position[None, :] <= position[:, None])
    context = (
        jnp.logical_not(is_prompt)[None, :, None]
        & is_prompt[None, None, :]
        & (source[:, :, None] == segment[None, None, :])
    )
    return (same_segment[None] | context, position)


def rotary_tables(position):
    half_dim = HEAD_DIM // 2
    frequency = rope_base ** (-(2.0 * jnp.arange(half_dim, dtype=F32)) / HEAD_DIM)
    angles = position.astype(F32)[:, None] * frequency[None, :]
    cosine = jnp.cos(angles)
    sine = jnp.sin(angles)
    return (cosine[None, :, None, :], sine[None, :, None, :])


def rotate(values, cosine, sine):
    first, second = jnp.split(values, 2, axis=-1)
    return jnp.concatenate([first * cosine - second * sine, second * cosine + first * sine], -1)


def dot(left, right, dims):
    return lax.dot_general(left, right, (dims, ((), ())), preferred_element_type=F32)


TILE = 256
PARTS = 2
EXTRA = 16


def ffn_kernel(sizes, meta, rows_ref, cot_ref, mix_ref, logit_ref, *refs):
    n_g, f_pad, f_shared, f_routed, local_experts, d_own = sizes
    blocks = refs[: 2 * n_g]
    out_ref, normed_ref, act_ref, gate_ref, up_ref = refs[2 * n_g : 2 * n_g + 5]
    w_gu, w_down, sems = refs[2 * n_g + 5 :]
    g_at, k_at = meta[0], meta[1]

    @pl.when((pl.program_id(0) == 0) & (pl.program_id(1) == 0))
    def _():
        copies = []
        for half in range(2):
            for shift in range(n_g):
                column = 2 * (g_at ^ shift) + (k_at ^ half)
                lanes = pl.ds(pl.multiple_of(column * d_own, d_own), d_own)
                source = blocks[half * n_g + shift]
                for kind, target in enumerate(
                    (w_gu.at[:f_pad, lanes], w_gu.at[f_pad : 2 * f_pad, lanes], w_down.at[:, lanes])
                ):
                    copies.append(
                        pltpu.make_async_copy(
                            source.at[kind], target, sems.at[(half * n_g + shift) * 3 + kind]
                        )
                    )
        for copy in copies:
            copy.start()
        w_gu[2 * f_pad :, :] = logit_ref[...]
        for copy in copies:
            copy.wait()

    rows = rows_ref[...]
    count = rows.shape[0]
    cot = jnp.concatenate(
        [cot_ref[c, 0, :, 0].reshape(count, -1) for c in range(cot_ref.shape[0])], axis=1
    )
    minor = ((1,), (1,))
    pre = dot(w_gu[...], rows, minor)
    down_back = dot(w_down[...], cot, minor)
    gate_pre, up_pre = pre[:f_pad], pre[f_pad : 2 * f_pad]
    prob = jax.nn.sigmoid(pre[2 * f_pad : 2 * f_pad + 1])
    pieces = [jnp.broadcast_to(prob, (f_shared, count))]
    for e in range(local_experts):
        pieces.append(jnp.broadcast_to(mix_ref[0, e : e + 1, :], (f_routed, count)))
    rest = f_pad - f_shared - local_experts * f_routed
    if rest:
        pieces.append(jnp.zeros((rest, count), F32))
    scale = jnp.concatenate(pieces, axis=0)
    sigma = jax.nn.sigmoid(gate_pre)
    silu = gate_pre * sigma
    act = silu * up_pre
    prob_part = jnp.sum(act[:f_shared] * down_back[:f_shared], axis=0, keepdims=True)
    act_grad = down_back * scale
    act_low = (act * scale).astype(BF16)
    gate_low = (act_grad * up_pre * sigma * (1.0 + gate_pre * (1.0 - sigma))).astype(BF16)
    up_low = (act_grad * silu).astype(BF16)
    logit_part = prob_part * prob * (1.0 - prob)
    logit_high = logit_part.astype(BF16).astype(F32)
    logit_rows = jnp.concatenate(
        [logit_high, logit_part - logit_high, jnp.zeros((EXTRA - 2, count), F32)], axis=0
    ).astype(BF16)
    act_ref[...] = act_low
    gate_ref[:f_pad, :] = gate_low
    gate_ref[f_pad:, :] = logit_rows
    up_ref[...] = up_low
    major = ((0,), (0,))
    out_ref[...] = dot(act_low, w_down[...], major).astype(BF16)
    both = jnp.concatenate([gate_low, up_low, logit_rows], axis=0)
    normed_ref[...] = dot(both, w_gu[...], major).astype(BF16)


def ffn_pass(sizes, meta, rows, cot, mix, logit, blocks, part):
    n_g, f_pad, _, _, local_experts, d_own = sizes
    total, dim = rows.shape
    n_c, _, _, parts, sub, cw = cot.shape
    take = min(TILE // sub, n_c)
    tile = take * sub
    steps = n_c // take
    flat = lambda i, j, m: (i * steps + j, 0)
    wide = lambda i, j, m: (0, i * steps + j)
    any_spec = pl.BlockSpec(memory_space=pl.ANY)
    return pl.pallas_call(
        functools.partial(ffn_kernel, sizes),
        grid_spec=pltpu.PrefetchScalarGridSpec(
            num_scalar_prefetch=1,
            grid=(n_g, steps),
            in_specs=[
                pl.BlockSpec((tile, dim), flat),
                pl.BlockSpec((n_c, 1, take, 1, sub, cw), lambda i, j, m: (0, i, j, part, 0, 0)),
                pl.BlockSpec((1, 8, tile), lambda i, j, m: (i * steps + j, 0, 0)),
                pl.BlockSpec((EXTRA, dim), lambda i, j, m: (0, 0)),
            ]
            + [any_spec] * (2 * n_g),
            out_specs=[
                pl.BlockSpec((tile, dim), flat),
                pl.BlockSpec((tile, dim), flat),
                pl.BlockSpec((f_pad, tile), wide),
                pl.BlockSpec((f_pad + EXTRA, tile), wide),
                pl.BlockSpec((f_pad, tile), wide),
            ],
            scratch_shapes=[
                pltpu.VMEM((2 * f_pad + EXTRA, dim), BF16),
                pltpu.VMEM((f_pad, dim), BF16),
                pltpu.SemaphoreType.DMA((6 * n_g,)),
            ],
        ),
        out_shape=[
            jax.ShapeDtypeStruct((total, dim), BF16),
            jax.ShapeDtypeStruct((total, dim), BF16),
            jax.ShapeDtypeStruct((f_pad, total), BF16),
            jax.ShapeDtypeStruct((f_pad + EXTRA, total), BF16),
            jax.ShapeDtypeStruct((f_pad, total), BF16),
        ],
        compiler_params=pltpu.CompilerParams(
            dimension_semantics=("arbitrary", "arbitrary"), vmem_limit_bytes=60 * 1024 * 1024
        ),
        cost_estimate=pl.CostEstimate(
            flops=12 * total * dim * f_pad,
            bytes_accessed=8 * total * dim + 6 * total * f_pad + 6 * f_pad * dim,
            transcendentals=total * f_pad,
        ),
        name="ffn_pass",
    )(meta, rows, cot, mix.reshape(-1, tile, 8).transpose(0, 2, 1), logit, *blocks)


def grad_kernel(parts, f_pad, meta, *refs):
    total = None
    for left, right in zip(refs[:parts], refs[parts : 2 * parts]):
        value = right[...].reshape(left.shape[1], -1)
        term = dot(left[...], value, ((1,), (0,)))
        total = term if total is None else total + term
    refs[2 * parts][0, 0] = total[:f_pad].astype(BF16)
    if len(refs) > 2 * parts + 1:
        refs[2 * parts + 1][...] = jnp.broadcast_to(
            total[f_pad : f_pad + 1] + total[f_pad + 1 : f_pad + 2], refs[2 * parts + 1].shape
        )


def weight_grad(sizes, meta, lefts, rights, cot):
    n_g, f_pad, _, _, _, d_own = sizes
    parts = len(lefts)
    f_rows, part_rows = lefts[0].shape
    dim = 2 * n_g * d_own
    if cot:
        n_c, _, _, _, sub, cw = rights[0].shape
        per = cw // d_own
        right_specs = [
            pl.BlockSpec(
                (1, n_g, n_c, 1, sub, d_own),
                functools.partial(lambda part, j, m: (j // per, 0, 0, part, 0, j % per), part),
            )
            for part in range(parts)
        ]
    else:
        right_specs = [pl.BlockSpec((part_rows, d_own), lambda j, m: (0, j))] * parts
    out_specs = [
        pl.BlockSpec(
            (1, 1, f_pad, d_own), lambda j, m: ((j % 2) ^ m[1], (j // 2) ^ m[0], 0, 0)
        )
    ]
    out_shape = [jax.ShapeDtypeStruct((2, n_g, f_pad, d_own), BF16)]
    if f_rows > f_pad:
        out_specs.append(pl.BlockSpec((8, d_own), lambda j, m: (0, j)))
        out_shape.append(jax.ShapeDtypeStruct((8, dim), F32))
    return pl.pallas_call(
        functools.partial(grad_kernel, parts, f_pad),
        grid_spec=pltpu.PrefetchScalarGridSpec(
            num_scalar_prefetch=1,
            grid=(2 * n_g,),
            in_specs=[pl.BlockSpec((f_rows, part_rows), lambda j, m: (0, 0))] * parts + right_specs,
            out_specs=out_specs,
        ),
        out_shape=out_shape,
        compiler_params=pltpu.CompilerParams(
            dimension_semantics=("arbitrary",), vmem_limit_bytes=48 * 1024 * 1024
        ),
        cost_estimate=pl.CostEstimate(
            flops=2 * parts * part_rows * dim * f_rows,
            bytes_accessed=2 * parts * part_rows * (dim + f_rows) + 2 * f_pad * dim,
            transcendentals=0,
        ),
        name="weight_grad",
    )(meta, *lefts, *rights)


def norm_back(normed_grad, unit_rows, scale, gain):
    weighted = normed_grad * gain
    rows_grad = scale * (
        weighted - unit_rows * jnp.mean(weighted * unit_rows, axis=-1, keepdims=True)
    )
    return (rows_grad, jnp.sum(normed_grad * unit_rows, axis=0))


def swap(value, axis):
    return lax.ppermute(value, axis, [(0, 1), (1, 0)])


def shift_chips(value, shift, n_g):
    if shift == 0:
        return value
    return lax.ppermute(value, "g", [(i, i ^ shift) for i in range(n_g)])


def col_gather(value, count):
    spread = jnp.broadcast_to(value[None], (count,) + value.shape)
    return lax.all_to_all(spread, COL, 0, 0, tiled=True)


def col_sum(partial, count):
    parts = partial.astype(BF16).reshape((count, -1) + partial.shape[1:])
    return jnp.sum(lax.all_to_all(parts, COL, 0, 0, tiled=True).astype(F32), axis=0)


def rows_to_features(rows, count):
    row_count, width = rows.shape
    parts = rows.reshape(row_count, count, width // count).transpose(1, 0, 2)
    moved = lax.all_to_all(parts, COL, 0, 0, tiled=True)
    blocks = moved.reshape(2, row_count * count // 2, width // count)
    return lax.all_to_all(blocks, "k", 0, 0, tiled=True)


def shards(
    tokens,
    routes,
    route_weights,
    group_ids,
    first_gain,
    query_weight,
    key_weight,
    value_weight,
    output_weight,
    second_gain,
    shared_gate,
    shared_up,
    shared_down,
    shared_logit,
    expert_gate,
    expert_up,
    expert_down,
    cotangent,
):
    n_g = lax.axis_size("g")
    n_c = lax.axis_size("y") * lax.axis_size("x")
    n_row = 2 * n_g
    at_g, at_k = lax.axis_index("g"), lax.axis_index("k")
    at_c = lax.axis_index(COL)
    block = tokens.shape[1]
    dim = query_weight.shape[0] * n_row
    d_own = query_weight.shape[0]
    width = query_weight.shape[1]
    heads = width // HEAD_DIM
    local_experts = expert_gate.shape[1]
    span = 2 * block
    total = n_g * span
    own_rows = span // n_c
    pick = lambda array, index, axis=0: lax.dynamic_index_in_dim(array, index, axis, keepdims=False)

    labels = jnp.arange(EXPERTS, dtype=jnp.int32)
    mixing = jnp.sum(
        jnp.where(
            routes[:, None] == labels[None, :, None, None], route_weights[:, None], 0.0
        ),
        axis=-1,
    )
    small = jnp.concatenate(
        [
            mixing.reshape(2 * EXPERTS, block),
            jnp.zeros((8, block), F32)
            .at[0, :d_own].set(first_gain.astype(F32))
            .at[1, :d_own].set(second_gain.astype(F32))
            .at[2, :d_own].set(shared_logit.astype(F32))
            .at[3, : 2 * CONTS].set(group_ids.astype(F32).reshape(-1)),
        ],
        axis=0,
    )
    small_all = lax.all_gather(small, ROW, axis=0, tiled=False)
    gain_1 = small_all[:, 16, :d_own].reshape(dim)
    gain_2 = small_all[:, 17, :d_own].reshape(dim)
    logit_w = small_all[:, 18, :d_own].reshape(dim)
    groups_all = small_all[:, 19, : 2 * CONTS].reshape(n_g, 2, 2, CONTS)
    groups = pick(pick(groups_all, at_g), at_k, 1).astype(jnp.int32)
    mixing_all = small_all[:, : 2 * EXPERTS].reshape(n_row, 2, EXPERTS, block)
    mixing_own = lax.dynamic_slice_in_dim(
        pick(mixing_all, at_k, 1), at_c * local_experts, local_experts, 1
    )
    mixing_own = mixing_own.transpose(0, 2, 1).reshape(total, local_experts)

    token_part = lax.all_to_all(tokens, "k", 0, 0, tiled=True).reshape(span, -1)
    cot_part = lax.all_to_all(cotangent, "k", 0, 0, tiled=True).reshape(span, -1)

    qkv = lax.all_gather(
        jnp.concatenate([query_weight, key_weight, value_weight], axis=1), ROW, axis=0, tiled=True
    )
    out_w = lax.all_gather(output_weight, ROW, axis=1, tiled=True)
    inputs = col_gather(token_part, n_c).reshape(n_c, span, -1).transpose(1, 0, 2)
    inputs = inputs.reshape(span, dim).astype(F32)

    f_shared = shared_gate.shape[1] // n_g
    f_routed = expert_gate.shape[2] // n_g
    f_all = f_shared + local_experts * f_routed
    f_pad = -(-f_all // 16) * 16
    sizes = (n_g, f_pad, f_shared, f_routed, local_experts, d_own)
    meta = jnp.stack([at_g, at_k]).astype(jnp.int32)

    def slices(shared, routed):
        parts = [
            shared.reshape(n_g, f_shared, d_own),
            routed.reshape(local_experts, n_g, f_routed, d_own)
            .transpose(1, 0, 2, 3)
            .reshape(n_g, -1, d_own),
        ]
        if f_pad > f_all:
            parts.append(jnp.zeros((n_g, f_pad - f_all, d_own), BF16))
        return jnp.concatenate(parts, axis=1)

    weight_slices = jnp.stack(
        [
            slices(shared_gate.T, expert_gate.transpose(1, 2, 0)),
            slices(shared_up.T, expert_up.transpose(1, 2, 0)),
            slices(shared_down, expert_down),
        ],
        axis=1,
    )
    own_blocks = [
        shift_chips(pick(weight_slices, at_g ^ shift), shift, n_g) for shift in range(n_g)
    ]
    weight_blocks = own_blocks + [swap(value, "k") for value in own_blocks]

    first_scale = lax.rsqrt(jnp.mean(inputs * inputs, axis=-1, keepdims=True) + epsilon)
    normed_1 = (inputs * first_scale * gain_1).astype(BF16)
    projected = dot(normed_1, qkv, ((1,), (0,)))
    allowed, position = block_layout(groups, block)
    cosine, sine = rotary_tables(position)
    head_shape = (2, block, heads, HEAD_DIM)
    query_rot = rotate(projected[:, :width].reshape(head_shape), cosine, sine).astype(BF16)
    key_rot = rotate(projected[:, width : 2 * width].reshape(head_shape), cosine, sine).astype(BF16)
    value_low = projected[:, 2 * width :].reshape(head_shape).astype(BF16)

    def einsum(form, left, right):
        return jnp.einsum(form, left, right, preferred_element_type=F32)

    scores = jnp.where(
        allowed[:, None],
        einsum("bqhd,bkhd->bhqk", query_rot, key_rot) * (1.0 / math.sqrt(HEAD_DIM)),
        masked_score,
    )
    peak = jnp.max(scores, axis=-1, keepdims=True)
    exp_scores = jnp.exp(scores - peak)
    probabilities = exp_scores / jnp.sum(exp_scores, axis=-1, keepdims=True)
    prob_low = probabilities.astype(BF16)
    mixed = einsum("bhqk,bkhd->bqhd", prob_low, value_low).astype(BF16).reshape(span, width)
    attention = col_sum(dot(mixed, out_w, ((1,), (0,))), n_c)

    own_inputs = lax.dynamic_slice_in_dim(inputs, at_c * own_rows, own_rows, 0)
    hidden = own_inputs + attention
    second_scale = lax.rsqrt(jnp.mean(hidden * hidden, axis=-1, keepdims=True) + epsilon)
    unit_2 = hidden * second_scale
    normed_own = (unit_2 * gain_2).astype(BF16)
    sub = own_rows // PARTS
    normed_parts = [
        lax.all_gather(
            normed_own[part * sub : (part + 1) * sub], ("g",) + COL, axis=0, tiled=True
        )
        for part in range(PARTS)
    ]

    cot_rows = lax.all_gather(cot_part, "g", axis=0, tiled=True)
    cot_all = col_gather(cot_rows, n_c).reshape(n_c, n_g, n_c, PARTS, sub, dim // n_c)
    own_cot = pick(pick(cot_all, at_g, 1), at_c, 1).reshape(n_c, own_rows, -1)
    own_cot = own_cot.transpose(1, 0, 2).reshape(own_rows, dim)

    logit_low = jnp.zeros((EXTRA, dim), BF16).at[:2].set(logit_w.astype(BF16)[None])
    mixing_parts = mixing_own.reshape(n_g, n_c, PARTS, sub, local_experts)
    mixing_parts = jnp.pad(mixing_parts, ((0, 0),) * 4 + ((0, 8 - local_experts),))
    passes = [
        ffn_pass(
            sizes,
            meta,
            normed_parts[part],
            cot_all,
            mixing_parts[:, :, part].reshape(-1, 8),
            logit_low,
            weight_blocks,
            part,
        )
        for part in range(PARTS)
    ]

    def scatter_axis(value, axis, at):
        size = lax.axis_size(axis)
        index = lax.axis_index(axis)
        if size == 2:
            other = swap(pick(value, 1 - index, at), axis)
            return (pick(value, index, at).astype(F32) + other.astype(F32)).astype(BF16)
        moved = lax.all_to_all(value, axis, at, at, tiled=True)
        return jnp.sum(moved.astype(F32), axis=at).astype(BF16)

    def scatter_cols(partial):
        part = partial.reshape(n_g, lax.axis_size("y"), 2, sub, dim)
        left, right = part[..., : dim // 2], part[..., dim // 2 :]
        left, right = scatter_axis(left, "x", 2), scatter_axis(right, "y", 1)
        left, right = scatter_axis(left, "y", 1), scatter_axis(right, "x", 1)
        return jnp.concatenate([left, right], axis=-1)

    def scatter_rows(partial):
        part = scatter_cols(partial)
        return jnp.sum(lax.all_to_all(part, "g", 0, 0, tiled=True).astype(F32), axis=0)

    normed_grad_2 = jnp.concatenate([scatter_rows(parts[1]) for parts in passes], axis=0)
    hidden_part, gain_2_sum = norm_back(normed_grad_2, unit_2, second_scale, gain_2)
    hidden_grad = own_cot.astype(F32) + hidden_part
    attn_grad = col_gather(hidden_grad.astype(BF16), n_c).reshape(span, dim)

    def return_slices(grad):
        other = swap(grad[1], "k")
        both = (grad[0].astype(F32) + other.astype(F32)).astype(BF16)
        moved = [shift_chips(both[shift], shift, n_g) for shift in range(n_g)]
        moved = jnp.stack(moved)
        moved = jnp.stack([pick(moved, at_g ^ source) for source in range(n_g)])
        shared = moved[:, :f_shared].reshape(n_g * f_shared, d_own)
        routed = moved[:, f_shared:f_all].reshape(n_g, local_experts, f_routed, d_own)
        routed = routed.transpose(1, 0, 2, 3).reshape(local_experts, n_g * f_routed, d_own)
        return (shared, routed)

    gate_blocks, logit_sum = weight_grad(
        sizes, meta, [parts[3] for parts in passes], normed_parts, False
    )
    (up_blocks,) = weight_grad(sizes, meta, [parts[4] for parts in passes], normed_parts, False)
    (down_blocks,) = weight_grad(
        sizes, meta, [parts[2] for parts in passes], [cot_all] * PARTS, True
    )
    gate_s, gate_e = return_slices(gate_blocks)
    up_s, up_e = return_slices(up_blocks)
    down_s, down_e = return_slices(down_blocks)
    logit_sum = logit_sum[0]

    out_rows = jnp.concatenate([scatter_rows(parts[0]) for parts in passes], axis=0)
    result = rows_to_features((hidden + out_rows).astype(BF16), n_c)

    out_grad = dot(attn_grad, mixed, ((0,), (0,)))
    mixed_grad = dot(attn_grad, out_w, ((1,), (1,))).astype(BF16).reshape(head_shape)
    prob_grad = einsum("bqhd,bkhd->bhqk", mixed_grad, value_low)
    value_grad = einsum("bhqk,bqhd->bkhd", prob_low, mixed_grad).astype(BF16)
    center = jnp.sum(prob_grad * probabilities, axis=-1, keepdims=True)
    score_grad = (probabilities * (prob_grad - center) * (1.0 / math.sqrt(HEAD_DIM))).astype(BF16)
    query_grad = rotate(einsum("bhqk,bkhd->bqhd", score_grad, key_rot), cosine, -sine).astype(BF16)
    key_grad = rotate(einsum("bhqk,bqhd->bkhd", score_grad, query_rot), cosine, -sine).astype(BF16)
    qkv_grad = jnp.concatenate(
        [part.reshape(span, width) for part in (query_grad, key_grad, value_grad)], axis=1
    )
    qkv_sum = dot(normed_1, qkv_grad, ((0,), (0,)))
    normed_grad_1 = col_sum(dot(qkv_grad, qkv, ((1,), (1,))), n_c)
    own_scale = lax.dynamic_slice_in_dim(first_scale, at_c * own_rows, own_rows, 0)
    rows_part, gain_1_sum = norm_back(normed_grad_1, own_inputs * own_scale, own_scale, gain_1)
    token_grad = rows_to_features((hidden_grad + rows_part).astype(BF16), n_c).astype(F32)

    sums = jnp.stack([gain_1_sum, gain_2_sum, logit_sum]).reshape(3, n_row, d_own)
    sums = jnp.broadcast_to(sums.transpose(1, 0, 2)[:, None], (n_row, n_c, 3, d_own))
    sums = lax.all_to_all(sums.reshape(n_row * n_c, 3, d_own), ALL, 0, 0, tiled=True)
    sums = jnp.sum(sums, axis=0)

    out_w_grad = lax.psum_scatter(out_grad.astype(BF16), ROW, scatter_dimension=0, tiled=True)
    qkv_own = lax.psum_scatter(qkv_sum.astype(BF16), ROW, scatter_dimension=0, tiled=True)
    qkv_own = qkv_own.astype(F32)
    return (
        result,
        token_grad,
        sums[0],
        qkv_own[:, :width],
        qkv_own[:, width : 2 * width],
        qkv_own[:, 2 * width :],
        out_w_grad.T.astype(F32),
        sums[1],
        gate_s.T.astype(F32),
        up_s.T.astype(F32),
        down_s.astype(F32),
        sums[2],
        gate_e.transpose(2, 0, 1).astype(F32),
        up_e.transpose(2, 0, 1).astype(F32),
        down_e.astype(F32),
    )


def solution(mesh):
    n_row, n_col = mesh.shape["row"], mesh.shape["col"]
    inner = Mesh(mesh.devices.reshape(n_row // 2, 2, n_col // 2, 2), ALL)
    return jax.shard_map(
        shards,
        mesh=inner,
        in_specs=(
            P(None, ROW, COL),
            P(None, ROW, None),
            P(None, ROW, None),
            P(None, ROW),
            P(ROW),
            P(ROW, COL),
            P(ROW, COL),
            P(ROW, COL),
            P(COL, ROW),
            P(ROW),
            P(ROW, COL),
            P(ROW, COL),
            P(COL, ROW),
            P(ROW),
            P(ROW, COL, None),
            P(ROW, COL, None),
            P(COL, None, ROW),
            P(None, ROW, COL),
        ),
        out_specs=(
            P(None, ROW, COL),
            P(None, ROW, COL),
            P(ROW),
            P(ROW, COL),
            P(ROW, COL),
            P(ROW, COL),
            P(COL, ROW),
            P(ROW),
            P(ROW, COL),
            P(ROW, COL),
            P(COL, ROW),
            P(ROW),
            P(ROW, COL, None),
            P(ROW, COL, None),
            P(COL, None, ROW),
        ),
        check_vma=False,
    )
```

```python
import functools
import math

import jax
import jax.numpy as jnp
from jax import lax
from jax.experimental import pallas as pl
from jax.experimental.pallas import tpu as pltpu
from jax.sharding import Mesh, PartitionSpec as P

HEAD_DIM = 128
EXPERTS = 8
PROMPTS = 2
CONTS = 2
CONT_LEN = 64
PROMPT_LEN = 64

epsilon = 1e-06
rope_base = 1000000.0
masked_score = -1000000000.0

F32 = jnp.float32
BF16 = jnp.bfloat16
COL = ("y", "x")
ROW = ("g", "k")
ALL = ("g", "k", "y", "x")


def block_layout(groups, row_count):
    token_index = jnp.arange(row_count, dtype=jnp.int32)
    prompt_rows = PROMPTS * PROMPT_LEN
    is_prompt = token_index < prompt_rows
    cont_offset = jnp.maximum(token_index - prompt_rows, 0)
    cont_number = cont_offset // CONT_LEN
    segment = jnp.where(is_prompt, token_index // PROMPT_LEN, PROMPTS + cont_number)
    position = jnp.where(is_prompt, token_index % PROMPT_LEN, PROMPT_LEN + cont_offset % CONT_LEN)
    cont_picks = (cont_number[:, None] == jnp.arange(CONTS, dtype=jnp.int32)[None, :]).astype(
        jnp.int32
    )
    source = jnp.where(
        is_prompt[None], segment[None], jnp.sum(cont_picks[None] * groups[:, None, :], axis=2)
    )
    same_segment = (segment[:, None] == segment[None, :]) & (position[None, :] <= position[:, None])
    context = (
        jnp.logical_not(is_prompt)[None, :, None]
        & is_prompt[None, None, :]
        & (source[:, :, None] == segment[None, None, :])
    )
    return (same_segment[None] | context, position)


def rotary_tables(position):
    half_dim = HEAD_DIM // 2
    frequency = rope_base ** (-(2.0 * jnp.arange(half_dim, dtype=F32)) / HEAD_DIM)
    angles = position.astype(F32)[:, None] * frequency[None, :]
    cosine = jnp.cos(angles)
    sine = jnp.sin(angles)
    return (cosine[None, :, None, :], sine[None, :, None, :])


def rotate(values, cosine, sine):
    first, second = jnp.split(values, 2, axis=-1)
    return jnp.concatenate([first * cosine - second * sine, second * cosine + first * sine], -1)


def dot(left, right, dims):
    return lax.dot_general(left, right, (dims, ((), ())), preferred_element_type=F32)


TILE = 256
PARTS = 2
EXTRA = 16


def ffn_kernel(sizes, meta, rows_ref, cot_ref, mix_ref, logit_ref, *refs):
    n_g, f_pad, f_shared, f_routed, local_experts, d_own = sizes
    blocks = refs[: 6 * n_g]
    out_ref, normed_ref, act_ref, gate_ref, up_ref = refs[6 * n_g : 6 * n_g + 5]
    w_gu, w_down, sems = refs[6 * n_g + 5 :]
    g_at, k_at = meta[0], meta[1]

    @pl.when((pl.program_id(0) == 0) & (pl.program_id(1) == 0))
    def _():
        copies = []
        for half in range(2):
            for shift in range(n_g):
                column = 2 * (g_at ^ shift) + (k_at ^ half)
                lanes = pl.ds(pl.multiple_of(column * d_own, d_own), d_own)
                first = (half * n_g + shift) * 3
                for kind, target in enumerate(
                    (w_gu.at[:f_pad, lanes], w_gu.at[f_pad : 2 * f_pad, lanes], w_down.at[:, lanes])
                ):
                    copies.append(
                        pltpu.make_async_copy(
                            blocks[first + kind], target, sems.at[first + kind]
                        )
                    )
        for copy in copies:
            copy.start()
        w_gu[2 * f_pad :, :] = logit_ref[...]
        for copy in copies:
            copy.wait()

    rows = rows_ref[...]
    count = rows.shape[0]
    cot = jnp.concatenate(
        [cot_ref[c, 0].reshape(count, -1) for c in range(cot_ref.shape[0])], axis=1
    )
    minor = ((1,), (1,))
    pre = dot(w_gu[...], rows, minor)
    down_back = dot(w_down[...], cot, minor)
    gate_pre, up_pre = pre[:f_pad], pre[f_pad : 2 * f_pad]
    prob = jax.nn.sigmoid(pre[2 * f_pad : 2 * f_pad + 1])
    pieces = [jnp.broadcast_to(prob, (f_shared, count))]
    for e in range(local_experts):
        pieces.append(jnp.broadcast_to(mix_ref[0, e : e + 1, :], (f_routed, count)))
    rest = f_pad - f_shared - local_experts * f_routed
    if rest:
        pieces.append(jnp.zeros((rest, count), F32))
    scale = jnp.concatenate(pieces, axis=0)
    sigma = jax.nn.sigmoid(gate_pre)
    silu = gate_pre * sigma
    act = silu * up_pre
    prob_part = jnp.sum(act[:f_shared] * down_back[:f_shared], axis=0, keepdims=True)
    act_grad = down_back * scale
    act_low = (act * scale).astype(BF16)
    gate_low = (act_grad * up_pre * sigma * (1.0 + gate_pre * (1.0 - sigma))).astype(BF16)
    up_low = (act_grad * silu).astype(BF16)
    logit_part = prob_part * prob * (1.0 - prob)
    logit_high = logit_part.astype(BF16).astype(F32)
    logit_rows = jnp.concatenate(
        [logit_high, logit_part - logit_high, jnp.zeros((EXTRA - 2, count), F32)], axis=0
    ).astype(BF16)
    act_ref[...] = act_low
    gate_ref[:f_pad, :] = gate_low
    gate_ref[f_pad:, :] = logit_rows
    up_ref[...] = up_low
    major = ((0,), (0,))
    out_ref[...] = dot(act_low, w_down[...], major).astype(BF16)
    both = jnp.concatenate([gate_low, up_low, logit_rows], axis=0)
    normed_ref[...] = dot(both, w_gu[...], major).astype(BF16)


def ffn_pass(sizes, meta, rows, cot, mix, logit, blocks):
    n_g, f_pad, _, _, local_experts, d_own = sizes
    total, dim = rows.shape
    n_c, _, _, sub, cw = cot.shape
    take = min(TILE // sub, n_c)
    tile = take * sub
    steps = n_c // take
    flat = lambda i, j, m: (i * steps + j, 0)
    wide = lambda i, j, m: (0, i * steps + j)
    any_spec = pl.BlockSpec(memory_space=pl.ANY)
    return pl.pallas_call(
        functools.partial(ffn_kernel, sizes),
        grid_spec=pltpu.PrefetchScalarGridSpec(
            num_scalar_prefetch=1,
            grid=(n_g, steps),
            in_specs=[
                pl.BlockSpec((tile, dim), flat),
                pl.BlockSpec((n_c, 1, take, sub, cw), lambda i, j, m: (0, i, j, 0, 0)),
                pl.BlockSpec((1, 8, tile), lambda i, j, m: (i * steps + j, 0, 0)),
                pl.BlockSpec((EXTRA, dim), lambda i, j, m: (0, 0)),
            ]
            + [any_spec] * (6 * n_g),
            out_specs=[
                pl.BlockSpec((tile, dim), flat),
                pl.BlockSpec((tile, dim), flat),
                pl.BlockSpec((f_pad, tile), wide),
                pl.BlockSpec((f_pad + EXTRA, tile), wide),
                pl.BlockSpec((f_pad, tile), wide),
            ],
            scratch_shapes=[
                pltpu.VMEM((2 * f_pad + EXTRA, dim), BF16),
                pltpu.VMEM((f_pad, dim), BF16),
                pltpu.SemaphoreType.DMA((6 * n_g,)),
            ],
        ),
        out_shape=[
            jax.ShapeDtypeStruct((total, dim), BF16),
            jax.ShapeDtypeStruct((total, dim), BF16),
            jax.ShapeDtypeStruct((f_pad, total), BF16),
            jax.ShapeDtypeStruct((f_pad + EXTRA, total), BF16),
            jax.ShapeDtypeStruct((f_pad, total), BF16),
        ],
        compiler_params=pltpu.CompilerParams(
            dimension_semantics=("arbitrary", "arbitrary"), vmem_limit_bytes=60 * 1024 * 1024
        ),
        cost_estimate=pl.CostEstimate(
            flops=12 * total * dim * f_pad,
            bytes_accessed=8 * total * dim + 6 * total * f_pad + 6 * f_pad * dim,
            transcendentals=total * f_pad,
        ),
        name="ffn_pass",
    )(meta, rows, cot, mix.reshape(-1, tile, 8).transpose(0, 2, 1), logit, *blocks)


def grad_kernel(parts, f_pad, meta, *refs):
    total = None
    for left, right in zip(refs[:parts], refs[parts : 2 * parts]):
        value = right[...].reshape(left.shape[1], -1)
        term = dot(left[...], value, ((1,), (0,)))
        total = term if total is None else total + term
    refs[2 * parts][0, 0] = total[:f_pad].astype(BF16)
    if len(refs) > 2 * parts + 1:
        refs[2 * parts + 1][...] = jnp.broadcast_to(
            total[f_pad : f_pad + 1] + total[f_pad + 1 : f_pad + 2], refs[2 * parts + 1].shape
        )


def weight_grad(sizes, meta, lefts, rights, cot):
    n_g, f_pad, _, _, _, d_own = sizes
    parts = len(lefts)
    f_rows, part_rows = lefts[0].shape
    dim = 2 * n_g * d_own
    if cot:
        n_c, _, _, sub, cw = rights[0].shape
        per = cw // d_own
        right_specs = [
            pl.BlockSpec(
                (1, n_g, n_c, sub, d_own), lambda j, m: (j // per, 0, 0, 0, j % per)
            )
        ] * parts
    else:
        right_specs = [pl.BlockSpec((part_rows, d_own), lambda j, m: (0, j))] * parts
    out_specs = [
        pl.BlockSpec(
            (1, 1, f_pad, d_own), lambda j, m: ((j % 2) ^ m[1], (j // 2) ^ m[0], 0, 0)
        )
    ]
    out_shape = [jax.ShapeDtypeStruct((2, n_g, f_pad, d_own), BF16)]
    if f_rows > f_pad:
        out_specs.append(pl.BlockSpec((8, d_own), lambda j, m: (0, j)))
        out_shape.append(jax.ShapeDtypeStruct((8, dim), F32))
    return pl.pallas_call(
        functools.partial(grad_kernel, parts, f_pad),
        grid_spec=pltpu.PrefetchScalarGridSpec(
            num_scalar_prefetch=1,
            grid=(2 * n_g,),
            in_specs=[pl.BlockSpec((f_rows, part_rows), lambda j, m: (0, 0))] * parts + right_specs,
            out_specs=out_specs,
        ),
        out_shape=out_shape,
        compiler_params=pltpu.CompilerParams(
            dimension_semantics=("arbitrary",), vmem_limit_bytes=48 * 1024 * 1024
        ),
        cost_estimate=pl.CostEstimate(
            flops=2 * parts * part_rows * dim * f_rows,
            bytes_accessed=2 * parts * part_rows * (dim + f_rows) + 2 * f_pad * dim,
            transcendentals=0,
        ),
        name="weight_grad",
    )(meta, *lefts, *rights)


def tie(*values):
    return lax.optimization_barrier(values)


def norm_back(normed_grad, unit_rows, scale, gain):
    weighted = normed_grad * gain
    rows_grad = scale * (
        weighted - unit_rows * jnp.mean(weighted * unit_rows, axis=-1, keepdims=True)
    )
    return (rows_grad, jnp.sum(normed_grad * unit_rows, axis=0))


def swap(value, axis):
    return lax.ppermute(value, axis, [(0, 1), (1, 0)])


def shift_chips(value, shift, n_g):
    if shift == 0:
        return value
    return lax.ppermute(value, "g", [(i, i ^ shift) for i in range(n_g)])


def col_gather(value, count):
    spread = jnp.broadcast_to(value[None], (count,) + value.shape)
    return lax.all_to_all(spread, COL, 0, 0, tiled=True)


def col_sum(partial, count):
    parts = partial.astype(BF16).reshape((count, -1) + partial.shape[1:])
    return jnp.sum(lax.all_to_all(parts, COL, 0, 0, tiled=True).astype(F32), axis=0)


def rows_to_features(rows, count):
    row_count, width = rows.shape
    parts = rows.reshape(row_count, count, width // count).transpose(1, 0, 2)
    moved = lax.all_to_all(parts, COL, 0, 0, tiled=True)
    blocks = moved.reshape(2, row_count * count // 2, width // count)
    return lax.all_to_all(blocks, "k", 0, 0, tiled=True)


def shards(
    tokens,
    routes,
    route_weights,
    group_ids,
    first_gain,
    query_weight,
    key_weight,
    value_weight,
    output_weight,
    second_gain,
    shared_gate,
    shared_up,
    shared_down,
    shared_logit,
    expert_gate,
    expert_up,
    expert_down,
    cotangent,
):
    n_g = lax.axis_size("g")
    n_c = lax.axis_size("y") * lax.axis_size("x")
    n_row = 2 * n_g
    at_g, at_k = lax.axis_index("g"), lax.axis_index("k")
    at_c = lax.axis_index(COL)
    block = tokens.shape[1]
    dim = query_weight.shape[0] * n_row
    d_own = query_weight.shape[0]
    width = query_weight.shape[1]
    heads = width // HEAD_DIM
    local_experts = expert_gate.shape[1]
    span = 2 * block
    total = n_g * span
    own_rows = span // n_c
    pick = lambda array, index, axis=0: lax.dynamic_index_in_dim(array, index, axis, keepdims=False)

    labels = jnp.arange(EXPERTS, dtype=jnp.int32)
    mixing = jnp.sum(
        jnp.where(
            routes[:, None] == labels[None, :, None, None], route_weights[:, None], 0.0
        ),
        axis=-1,
    )
    small = jnp.concatenate(
        [
            mixing.reshape(2 * EXPERTS, block),
            jnp.zeros((8, block), F32)
            .at[0, :d_own].set(first_gain.astype(F32))
            .at[1, :d_own].set(second_gain.astype(F32))
            .at[2, :d_own].set(shared_logit.astype(F32))
            .at[3, : 2 * CONTS].set(group_ids.astype(F32).reshape(-1)),
        ],
        axis=0,
    )
    small_all = lax.all_gather(small, ROW, axis=0, tiled=False)
    gain_1 = small_all[:, 16, :d_own].reshape(dim)
    gain_2 = small_all[:, 17, :d_own].reshape(dim)
    logit_w = small_all[:, 18, :d_own].reshape(dim)
    groups_all = small_all[:, 19, : 2 * CONTS].reshape(n_g, 2, 2, CONTS)
    groups = pick(pick(groups_all, at_g), at_k, 1).astype(jnp.int32)
    mixing_all = small_all[:, : 2 * EXPERTS].reshape(n_row, 2, EXPERTS, block)
    mixing_own = lax.dynamic_slice_in_dim(
        pick(mixing_all, at_k, 1), at_c * local_experts, local_experts, 1
    )
    mixing_own = mixing_own.transpose(0, 2, 1).reshape(total, local_experts)

    f_shared = shared_gate.shape[1] // n_g
    f_routed = expert_gate.shape[2] // n_g
    f_all = f_shared + local_experts * f_routed
    f_pad = -(-f_all // 16) * 16
    sizes = (n_g, f_pad, f_shared, f_routed, local_experts, d_own)
    meta = jnp.stack([at_g, at_k]).astype(jnp.int32)

    def slices(shared, routed):
        parts = [
            shared.reshape(n_g, f_shared, d_own),
            routed.reshape(local_experts, n_g, f_routed, d_own)
            .transpose(1, 0, 2, 3)
            .reshape(n_g, -1, d_own),
        ]
        if f_pad > f_all:
            parts.append(jnp.zeros((n_g, f_pad - f_all, d_own), BF16))
        return jnp.concatenate(parts, axis=1)

    weight_slices = [
        slices(shared_gate.T, expert_gate.transpose(1, 2, 0)),
        slices(shared_up.T, expert_up.transpose(1, 2, 0)),
        slices(shared_down, expert_down),
    ]
    picked = [[pick(value, at_g ^ shift) for shift in range(n_g)] for value in weight_slices]
    picked[0], tokens = tie(picked[0], tokens)
    own_blocks = [
        [shift_chips(value, shift, n_g) for shift, value in enumerate(values)] for values in picked
    ]

    token_part = lax.all_to_all(tokens, "k", 0, 0, tiled=True).reshape(span, -1)
    cot_part = lax.all_to_all(cotangent, "k", 0, 0, tiled=True).reshape(span, -1)

    qkv = lax.all_gather(
        jnp.concatenate([query_weight, key_weight, value_weight], axis=1), ROW, axis=0, tiled=True
    )
    out_w = lax.all_gather(output_weight, ROW, axis=1, tiled=True)
    inputs = col_gather(token_part, n_c).reshape(n_c, span, -1).transpose(1, 0, 2)
    inputs = inputs.reshape(span, dim).astype(F32)

    own_blocks[0], inputs = tie(own_blocks[0], inputs)
    first_scale = lax.rsqrt(jnp.mean(inputs * inputs, axis=-1, keepdims=True) + epsilon)
    normed_1 = (inputs * first_scale * gain_1).astype(BF16)
    projected = dot(normed_1, qkv, ((1,), (0,)))
    allowed, position = block_layout(groups, block)
    cosine, sine = rotary_tables(position)
    head_shape = (2, block, heads, HEAD_DIM)
    query_rot = rotate(projected[:, :width].reshape(head_shape), cosine, sine).astype(BF16)
    key_rot = rotate(projected[:, width : 2 * width].reshape(head_shape), cosine, sine).astype(BF16)
    value_low = projected[:, 2 * width :].reshape(head_shape).astype(BF16)

    def einsum(form, left, right):
        return jnp.einsum(form, left, right, preferred_element_type=F32)

    scores = jnp.where(
        allowed[:, None],
        einsum("bqhd,bkhd->bhqk", query_rot, key_rot) * (1.0 / math.sqrt(HEAD_DIM)),
        masked_score,
    )
    peak = jnp.max(scores, axis=-1, keepdims=True)
    exp_scores = jnp.exp(scores - peak)
    probabilities = exp_scores / jnp.sum(exp_scores, axis=-1, keepdims=True)
    prob_low = probabilities.astype(BF16)
    mixed = einsum("bhqk,bkhd->bqhd", prob_low, value_low).astype(BF16).reshape(span, width)
    attention = col_sum(dot(mixed, out_w, ((1,), (0,))), n_c)

    own_inputs = lax.dynamic_slice_in_dim(inputs, at_c * own_rows, own_rows, 0)
    own_blocks[1], attention = tie(own_blocks[1], attention)
    hidden = own_inputs + attention
    second_scale = lax.rsqrt(jnp.mean(hidden * hidden, axis=-1, keepdims=True) + epsilon)
    unit_2 = hidden * second_scale
    normed_own = (unit_2 * gain_2).astype(BF16)
    sub = own_rows // PARTS
    normed_parts = [
        lax.all_gather(
            normed_own[part * sub : (part + 1) * sub], ("g",) + COL, axis=0, tiled=True
        )
        for part in range(PARTS)
    ]

    cot_rows = lax.all_gather(cot_part, "g", axis=0, tiled=True)
    cot_rows = cot_rows.reshape(n_g, n_c, PARTS, sub, dim // n_c)
    cot_all = [
        col_gather(cot_rows[:, :, part], n_c).reshape(n_c, n_g, n_c, sub, dim // n_c)
        for part in range(PARTS)
    ]
    own_cot = [
        pick(pick(cot, at_g, 1), at_c, 1).transpose(1, 0, 2).reshape(sub, dim) for cot in cot_all
    ]
    own_cot = jnp.concatenate(own_cot, axis=0)

    logit_low = jnp.zeros((EXTRA, dim), BF16).at[:2].set(logit_w.astype(BF16)[None])
    mixing_parts = mixing_own.reshape(n_g, n_c, PARTS, sub, local_experts)
    mixing_parts = jnp.pad(mixing_parts, ((0, 0),) * 4 + ((0, 8 - local_experts),))
    swapped = [[swap(value, "k") for value in values] for values in own_blocks]
    weight_blocks = [
        values[shift]
        for half in (own_blocks, swapped)
        for shift in range(n_g)
        for values in half
    ]
    passes = [
        ffn_pass(
            sizes,
            meta,
            normed_parts[part],
            cot_all[part],
            mixing_parts[:, :, part].reshape(-1, 8),
            logit_low,
            weight_blocks,
        )
        for part in range(PARTS)
    ]

    def scatter_axis(value, axis, at):
        size = lax.axis_size(axis)
        index = lax.axis_index(axis)
        if size == 2:
            other = swap(pick(value, 1 - index, at), axis)
            return (pick(value, index, at).astype(F32) + other.astype(F32)).astype(BF16)
        moved = lax.all_to_all(value, axis, at, at, tiled=True)
        return jnp.sum(moved.astype(F32), axis=at).astype(BF16)

    def scatter_cols(partial):
        part = partial.reshape(n_g, lax.axis_size("y"), 2, sub, dim)
        left, right = part[..., : dim // 2], part[..., dim // 2 :]
        left, right = scatter_axis(left, "x", 2), scatter_axis(right, "y", 1)
        left, right = scatter_axis(left, "y", 1), scatter_axis(right, "x", 1)
        return jnp.concatenate([left, right], axis=-1)

    def scatter_chips(part):
        return jnp.sum(lax.all_to_all(part, "g", 0, 0, tiled=True).astype(F32), axis=0)

    def own_core(grad):
        other = swap(grad[1], "k")
        return (grad[0].astype(F32) + other.astype(F32)).astype(BF16)

    def send_slices(both):
        return [shift_chips(both[shift], shift, n_g) for shift in range(n_g)]

    def place_slices(moved):
        moved = jnp.stack(moved)
        moved = jnp.stack([pick(moved, at_g ^ source) for source in range(n_g)])
        shared = moved[:, :f_shared].reshape(n_g * f_shared, d_own)
        routed = moved[:, f_shared:f_all].reshape(n_g, local_experts, f_routed, d_own)
        routed = routed.transpose(1, 0, 2, 3).reshape(local_experts, n_g * f_routed, d_own)
        return (shared, routed)

    (down_blocks,) = weight_grad(sizes, meta, [parts[2] for parts in passes], cot_all, True)
    gate_blocks, logit_sum = weight_grad(
        sizes, meta, [parts[3] for parts in passes], normed_parts, False
    )
    (up_blocks,) = weight_grad(sizes, meta, [parts[4] for parts in passes], normed_parts, False)
    logit_sum = logit_sum[0]
    down_both = own_core(down_blocks)

    normed_cols = [scatter_cols(parts[1]) for parts in passes]
    normed_cols[1], down_both, gate_blocks = tie(normed_cols[1], down_both, gate_blocks)
    normed_grad_2 = jnp.concatenate([scatter_chips(part) for part in normed_cols], axis=0)
    down_moved = send_slices(down_both)
    gate_both, up_both = own_core(gate_blocks), own_core(up_blocks)
    normed_grad_2, down_moved, gate_both, up_both = tie(
        normed_grad_2, down_moved, gate_both, up_both
    )
    hidden_part, gain_2_sum = norm_back(normed_grad_2, unit_2, second_scale, gain_2)
    hidden_grad = own_cot.astype(F32) + hidden_part
    gate_moved = send_slices(gate_both)
    up_moved = send_slices(up_both)
    attn_grad = col_gather(hidden_grad.astype(BF16), n_c).reshape(span, dim)
    out_parts, attn_grad = tie([parts[0] for parts in passes], attn_grad)
    down_s, down_e = place_slices(down_moved)

    out_grad = dot(attn_grad, mixed, ((0,), (0,)))
    mixed_grad = dot(attn_grad, out_w, ((1,), (1,))).astype(BF16).reshape(head_shape)
    prob_grad = einsum("bqhd,bkhd->bhqk", mixed_grad, value_low)
    value_grad = einsum("bhqk,bqhd->bkhd", prob_low, mixed_grad).astype(BF16)
    center = jnp.sum(prob_grad * probabilities, axis=-1, keepdims=True)
    score_grad = (probabilities * (prob_grad - center) * (1.0 / math.sqrt(HEAD_DIM))).astype(BF16)
    query_grad = rotate(einsum("bhqk,bkhd->bqhd", score_grad, key_rot), cosine, -sine).astype(BF16)
    key_grad = rotate(einsum("bhqk,bqhd->bkhd", score_grad, query_rot), cosine, -sine).astype(BF16)
    qkv_grad = jnp.concatenate(
        [part.reshape(span, width) for part in (query_grad, key_grad, value_grad)], axis=1
    )
    qkv_grad, gate_moved = tie(qkv_grad, gate_moved)
    gate_s, gate_e = place_slices(gate_moved)
    qkv_sum = dot(normed_1, qkv_grad, ((0,), (0,)))
    normed_grad_1 = col_sum(dot(qkv_grad, qkv, ((1,), (1,))), n_c)
    normed_grad_1, up_moved = tie(normed_grad_1, up_moved)
    up_s, up_e = place_slices(up_moved)
    own_scale = lax.dynamic_slice_in_dim(first_scale, at_c * own_rows, own_rows, 0)
    rows_part, gain_1_sum = norm_back(normed_grad_1, own_inputs * own_scale, own_scale, gain_1)
    token_grad = rows_to_features((hidden_grad + rows_part).astype(BF16), n_c).astype(F32)

    out_rows = jnp.concatenate([scatter_chips(scatter_cols(part)) for part in out_parts], axis=0)
    result = rows_to_features((hidden + out_rows).astype(BF16), n_c)

    sums = jnp.stack([gain_1_sum, gain_2_sum, logit_sum]).reshape(3, n_row, d_own)
    sums = jnp.broadcast_to(sums.transpose(1, 0, 2)[:, None], (n_row, n_c, 3, d_own))
    sums = lax.all_to_all(sums.reshape(n_row * n_c, 3, d_own), ALL, 0, 0, tiled=True)
    sums = jnp.sum(sums, axis=0)

    out_w_grad = lax.psum_scatter(out_grad.astype(BF16), ROW, scatter_dimension=0, tiled=True)
    qkv_own = lax.psum_scatter(qkv_sum.astype(BF16), ROW, scatter_dimension=0, tiled=True)
    qkv_own = qkv_own.astype(F32)
    return (
        result,
        token_grad,
        sums[0],
        qkv_own[:, :width],
        qkv_own[:, width : 2 * width],
        qkv_own[:, 2 * width :],
        out_w_grad.T.astype(F32),
        sums[1],
        gate_s.T.astype(F32),
        up_s.T.astype(F32),
        down_s.astype(F32),
        sums[2],
        gate_e.transpose(2, 0, 1).astype(F32),
        up_e.transpose(2, 0, 1).astype(F32),
        down_e.astype(F32),
    )


def solution(mesh):
    n_row, n_col = mesh.shape["row"], mesh.shape["col"]
    inner = Mesh(mesh.devices.reshape(n_row // 2, 2, n_col // 2, 2), ALL)
    return jax.shard_map(
        shards,
        mesh=inner,
        in_specs=(
            P(None, ROW, COL),
            P(None, ROW, None),
            P(None, ROW, None),
            P(None, ROW),
            P(ROW),
            P(ROW, COL),
            P(ROW, COL),
            P(ROW, COL),
            P(COL, ROW),
            P(ROW),
            P(ROW, COL),
            P(ROW, COL),
            P(COL, ROW),
            P(ROW),
            P(ROW, COL, None),
            P(ROW, COL, None),
            P(COL, None, ROW),
            P(None, ROW, COL),
        ),
        out_specs=(
            P(None, ROW, COL),
            P(None, ROW, COL),
            P(ROW),
            P(ROW, COL),
            P(ROW, COL),
            P(ROW, COL),
            P(COL, ROW),
            P(ROW),
            P(ROW, COL),
            P(ROW, COL),
            P(COL, ROW),
            P(ROW),
            P(ROW, COL, None),
            P(ROW, COL, None),
            P(COL, None, ROW),
        ),
        check_vma=False,
    )
```

```python
import functools
import math

import jax
import jax.numpy as jnp
from jax import lax
from jax.experimental import pallas as pl
from jax.experimental.pallas import tpu as pltpu
from jax.sharding import Mesh, PartitionSpec as P

HEAD_DIM = 128
EXPERTS = 8
PROMPTS = 2
CONTS = 2
CONT_LEN = 64
PROMPT_LEN = 64

epsilon = 1e-06
rope_base = 1000000.0
masked_score = -1000000000.0

F32 = jnp.float32
BF16 = jnp.bfloat16
COL = ("y", "x")
ROW = ("g", "k")
ALL = ("g", "k", "y", "x")


def block_layout(groups, row_count):
    token_index = jnp.arange(row_count, dtype=jnp.int32)
    prompt_rows = PROMPTS * PROMPT_LEN
    is_prompt = token_index < prompt_rows
    cont_offset = jnp.maximum(token_index - prompt_rows, 0)
    cont_number = cont_offset // CONT_LEN
    segment = jnp.where(is_prompt, token_index // PROMPT_LEN, PROMPTS + cont_number)
    position = jnp.where(is_prompt, token_index % PROMPT_LEN, PROMPT_LEN + cont_offset % CONT_LEN)
    cont_picks = (cont_number[:, None] == jnp.arange(CONTS, dtype=jnp.int32)[None, :]).astype(
        jnp.int32
    )
    source = jnp.where(
        is_prompt[None], segment[None], jnp.sum(cont_picks[None] * groups[:, None, :], axis=2)
    )
    same_segment = (segment[:, None] == segment[None, :]) & (position[None, :] <= position[:, None])
    context = (
        jnp.logical_not(is_prompt)[None, :, None]
        & is_prompt[None, None, :]
        & (source[:, :, None] == segment[None, None, :])
    )
    return (same_segment[None] | context, position)


def rotary_tables(position):
    half_dim = HEAD_DIM // 2
    frequency = rope_base ** (-(2.0 * jnp.arange(half_dim, dtype=F32)) / HEAD_DIM)
    angles = position.astype(F32)[:, None] * frequency[None, :]
    cosine = jnp.cos(angles)
    sine = jnp.sin(angles)
    return (cosine[None, :, None, :], sine[None, :, None, :])


def rotate(values, cosine, sine):
    first, second = jnp.split(values, 2, axis=-1)
    return jnp.concatenate([first * cosine - second * sine, second * cosine + first * sine], -1)


def dot(left, right, dims):
    return lax.dot_general(left, right, (dims, ((), ())), preferred_element_type=F32)


PARTS = 2
EXTRA = 16


def ffn_kernel(sizes, meta, rows_ref, cot_ref, mix_ref, logit_ref, *refs):
    n_g, f_pad, f_shared, f_routed, local_experts, d_own = sizes
    blocks = refs[: 6 * n_g]
    out_ref, normed_ref, act_ref, gate_ref, up_ref = refs[6 * n_g : 6 * n_g + 5]
    w_gu, w_down, sems = refs[6 * n_g + 5 :]
    g_at, k_at, c_at = meta[0], meta[1], meta[2]

    @pl.when(pl.program_id(0) == 0)
    def _():
        copies = []
        for half in range(2):
            for shift in range(n_g):
                column = 2 * (g_at ^ shift) + (k_at ^ half)
                lanes = pl.ds(pl.multiple_of(column * d_own, d_own), d_own)
                first = (half * n_g + shift) * 3
                for kind, target in enumerate(
                    (w_gu.at[:f_pad, lanes], w_gu.at[f_pad : 2 * f_pad, lanes], w_down.at[:, lanes])
                ):
                    copies.append(
                        pltpu.make_async_copy(
                            blocks[first + kind], target, sems.at[first + kind]
                        )
                    )
        for copy in copies:
            copy.start()
        w_gu[2 * f_pad :, :] = logit_ref[...]
        for copy in copies:
            copy.wait()

    rows = rows_ref[...]
    count = rows.shape[0]
    n_c = cot_ref.shape[0]
    cot = jnp.concatenate(
        [
            jnp.concatenate([cot_ref[c ^ c_at, 0, row ^ c_at] for row in range(n_c)], axis=0)
            for c in range(n_c)
        ],
        axis=1,
    )
    minor = ((1,), (1,))
    pre = dot(w_gu[...], rows, minor)
    down_back = dot(w_down[...], cot, minor)
    gate_pre, up_pre = pre[:f_pad], pre[f_pad : 2 * f_pad]
    prob = jax.nn.sigmoid(pre[2 * f_pad : 2 * f_pad + 1])
    pieces = [jnp.broadcast_to(prob, (f_shared, count))]
    for e in range(local_experts):
        pieces.append(jnp.broadcast_to(mix_ref[0, e : e + 1, :], (f_routed, count)))
    rest = f_pad - f_shared - local_experts * f_routed
    if rest:
        pieces.append(jnp.zeros((rest, count), F32))
    scale = jnp.concatenate(pieces, axis=0)
    sigma = jax.nn.sigmoid(gate_pre)
    silu = gate_pre * sigma
    act = silu * up_pre
    prob_part = jnp.sum(act[:f_shared] * down_back[:f_shared], axis=0, keepdims=True)
    act_grad = down_back * scale
    act_low = (act * scale).astype(BF16)
    gate_low = (act_grad * up_pre * sigma * (1.0 + gate_pre * (1.0 - sigma))).astype(BF16)
    up_low = (act_grad * silu).astype(BF16)
    logit_part = prob_part * prob * (1.0 - prob)
    logit_high = logit_part.astype(BF16).astype(F32)
    logit_rows = jnp.concatenate(
        [logit_high, logit_part - logit_high, jnp.zeros((EXTRA - 2, count), F32)], axis=0
    ).astype(BF16)
    act_ref[...] = act_low
    gate_ref[:f_pad, :] = gate_low
    gate_ref[f_pad:, :] = logit_rows
    up_ref[...] = up_low
    major = ((0,), (0,))
    out_ref[...] = dot(act_low, w_down[...], major).astype(BF16)
    both = jnp.concatenate([gate_low, up_low, logit_rows], axis=0)
    normed_ref[...] = dot(both, w_gu[...], major).astype(BF16)


def ffn_pass(sizes, meta, rows, cot, mix, logit, blocks):
    n_g, f_pad, _, _, local_experts, d_own = sizes
    total, dim = rows.shape
    n_c, _, _, sub, cw = cot.shape
    tile = n_c * sub
    flat = lambda i, m: (i, 0)
    wide = lambda i, m: (0, i)
    any_spec = pl.BlockSpec(memory_space=pl.ANY)
    return pl.pallas_call(
        functools.partial(ffn_kernel, sizes),
        grid_spec=pltpu.PrefetchScalarGridSpec(
            num_scalar_prefetch=1,
            grid=(n_g,),
            in_specs=[
                pl.BlockSpec((tile, dim), flat),
                pl.BlockSpec((n_c, 1, n_c, sub, cw), lambda i, m: (0, i, 0, 0, 0)),
                pl.BlockSpec((1, 8, tile), lambda i, m: (i, 0, 0)),
                pl.BlockSpec((EXTRA, dim), lambda i, m: (0, 0)),
            ]
            + [any_spec] * (6 * n_g),
            out_specs=[
                pl.BlockSpec((tile, dim), flat),
                pl.BlockSpec((tile, dim), flat),
                pl.BlockSpec((f_pad, tile), wide),
                pl.BlockSpec((f_pad + EXTRA, tile), wide),
                pl.BlockSpec((f_pad, tile), wide),
            ],
            scratch_shapes=[
                pltpu.VMEM((2 * f_pad + EXTRA, dim), BF16),
                pltpu.VMEM((f_pad, dim), BF16),
                pltpu.SemaphoreType.DMA((6 * n_g,)),
            ],
        ),
        out_shape=[
            jax.ShapeDtypeStruct((total, dim), BF16),
            jax.ShapeDtypeStruct((total, dim), BF16),
            jax.ShapeDtypeStruct((f_pad, total), BF16),
            jax.ShapeDtypeStruct((f_pad + EXTRA, total), BF16),
            jax.ShapeDtypeStruct((f_pad, total), BF16),
        ],
        compiler_params=pltpu.CompilerParams(
            dimension_semantics=("arbitrary",), vmem_limit_bytes=60 * 1024 * 1024
        ),
        cost_estimate=pl.CostEstimate(
            flops=12 * total * dim * f_pad,
            bytes_accessed=8 * total * dim + 6 * total * f_pad + 6 * f_pad * dim,
            transcendentals=total * f_pad,
        ),
        name="ffn_pass",
    )(meta, rows, cot, mix.reshape(-1, tile, 8).transpose(0, 2, 1), logit, *blocks)


def grad_kernel(parts, f_pad, meta, *refs):
    total = None
    for left, right in zip(refs[:parts], refs[parts : 2 * parts]):
        value = right[...]
        if len(value.shape) > 2:
            _, n_g, n_c, sub, _ = right.shape
            value = jnp.concatenate(
                [right[0, g, row ^ meta[2]] for g in range(n_g) for row in range(n_c)], axis=0
            )
        term = dot(left[...], value, ((1,), (0,)))
        total = term if total is None else total + term
    refs[2 * parts][0, 0] = total[:f_pad].astype(BF16)
    if len(refs) > 2 * parts + 1:
        refs[2 * parts + 1][...] = jnp.broadcast_to(
            total[f_pad : f_pad + 1] + total[f_pad + 1 : f_pad + 2], refs[2 * parts + 1].shape
        )


def weight_grad(sizes, meta, lefts, rights, cot):
    n_g, f_pad, _, _, _, d_own = sizes
    parts = len(lefts)
    f_rows, part_rows = lefts[0].shape
    dim = 2 * n_g * d_own
    if cot:
        n_c, _, _, sub, cw = rights[0].shape
        per = cw // d_own
        right_specs = [
            pl.BlockSpec(
                (1, n_g, n_c, sub, d_own), lambda j, m: ((j // per) ^ m[2], 0, 0, 0, j % per)
            )
        ] * parts
    else:
        right_specs = [pl.BlockSpec((part_rows, d_own), lambda j, m: (0, j))] * parts
    out_specs = [
        pl.BlockSpec(
            (1, 1, f_pad, d_own), lambda j, m: ((j % 2) ^ m[1], (j // 2) ^ m[0], 0, 0)
        )
    ]
    out_shape = [jax.ShapeDtypeStruct((2, n_g, f_pad, d_own), BF16)]
    if f_rows > f_pad:
        out_specs.append(pl.BlockSpec((8, d_own), lambda j, m: (0, j)))
        out_shape.append(jax.ShapeDtypeStruct((8, dim), F32))
    return pl.pallas_call(
        functools.partial(grad_kernel, parts, f_pad),
        grid_spec=pltpu.PrefetchScalarGridSpec(
            num_scalar_prefetch=1,
            grid=(2 * n_g,),
            in_specs=[pl.BlockSpec((f_rows, part_rows), lambda j, m: (0, 0))] * parts + right_specs,
            out_specs=out_specs,
        ),
        out_shape=out_shape,
        compiler_params=pltpu.CompilerParams(
            dimension_semantics=("arbitrary",), vmem_limit_bytes=48 * 1024 * 1024
        ),
        cost_estimate=pl.CostEstimate(
            flops=2 * parts * part_rows * dim * f_rows,
            bytes_accessed=2 * parts * part_rows * (dim + f_rows) + 2 * f_pad * dim,
            transcendentals=0,
        ),
        name="weight_grad",
    )(meta, *lefts, *rights)


def tie(*values):
    return lax.optimization_barrier(values)


def norm_back(normed_grad, unit_rows, scale, gain):
    weighted = normed_grad * gain
    rows_grad = scale * (
        weighted - unit_rows * jnp.mean(weighted * unit_rows, axis=-1, keepdims=True)
    )
    return (rows_grad, jnp.sum(normed_grad * unit_rows, axis=0))


def swap(value, axis):
    return lax.ppermute(value, axis, [(0, 1), (1, 0)])


def shift_by(value, axis, shift):
    if shift == 0:
        return value
    return lax.ppermute(value, axis, [(i, i ^ shift) for i in range(lax.axis_size(axis))])


def gather_joined(value, axis, at):
    bit = lax.axis_size(axis) // 2
    while bit:
        shape = value.shape[:at] + (2 * value.shape[at],) + value.shape[at + 1 :]
        value = jnp.stack([value, shift_by(value, axis, bit)], axis=at + 1).reshape(shape)
        bit //= 2
    return value


def halve(value, axis, at, bit):
    size = value.shape[at]
    shape = value.shape[:at] + (size // 2, 2) + value.shape[at + 1 :]
    pair = value.reshape(shape)
    keep, send = (lax.index_in_dim(pair, i, at + 1, keepdims=False) for i in range(2))
    other = shift_by(send, axis, bit)
    return (keep.astype(F32) + other.astype(F32)).astype(BF16)


def col_gather(value, count):
    spread = jnp.broadcast_to(value[None], (count,) + value.shape)
    return lax.all_to_all(spread, COL, 0, 0, tiled=True)


def col_sum(partial, count):
    parts = partial.astype(BF16).reshape((count, -1) + partial.shape[1:])
    return jnp.sum(lax.all_to_all(parts, COL, 0, 0, tiled=True).astype(F32), axis=0)


def rows_to_features(rows, count):
    row_count, width = rows.shape
    parts = rows.reshape(row_count, count, width // count).transpose(1, 0, 2)
    moved = lax.all_to_all(parts, COL, 0, 0, tiled=True)
    blocks = moved.reshape(2, row_count * count // 2, width // count)
    return lax.all_to_all(blocks, "k", 0, 0, tiled=True)


def shards(
    tokens,
    routes,
    route_weights,
    group_ids,
    first_gain,
    query_weight,
    key_weight,
    value_weight,
    output_weight,
    second_gain,
    shared_gate,
    shared_up,
    shared_down,
    shared_logit,
    expert_gate,
    expert_up,
    expert_down,
    cotangent,
):
    n_g = lax.axis_size("g")
    n_c = lax.axis_size("y") * lax.axis_size("x")
    n_y, n_x = lax.axis_size("y"), lax.axis_size("x")
    n_row = 2 * n_g
    at_g, at_k = lax.axis_index("g"), lax.axis_index("k")
    at_c = lax.axis_index(COL)
    block = tokens.shape[1]
    dim = query_weight.shape[0] * n_row
    d_own = query_weight.shape[0]
    width = query_weight.shape[1]
    heads = width // HEAD_DIM
    local_experts = expert_gate.shape[1]
    span = 2 * block
    total = n_g * span
    own_rows = span // n_c
    pick = lambda array, index, axis=0: lax.dynamic_index_in_dim(array, index, axis, keepdims=False)

    labels = jnp.arange(EXPERTS, dtype=jnp.int32)
    mixing = jnp.sum(
        jnp.where(
            routes[:, None] == labels[None, :, None, None], route_weights[:, None], 0.0
        ),
        axis=-1,
    )
    small = jnp.concatenate(
        [
            mixing.reshape(2 * EXPERTS, block),
            jnp.zeros((8, block), F32)
            .at[0, :d_own].set(first_gain.astype(F32))
            .at[1, :d_own].set(second_gain.astype(F32))
            .at[2, :d_own].set(shared_logit.astype(F32))
            .at[3, : 2 * CONTS].set(group_ids.astype(F32).reshape(-1)),
        ],
        axis=0,
    )
    small_all = lax.all_to_all(
        jnp.broadcast_to(small[None], (n_row,) + small.shape), ROW, 0, 0, tiled=True
    )
    f_shared = shared_gate.shape[1] // n_g
    f_routed = expert_gate.shape[2] // n_g
    f_all = f_shared + local_experts * f_routed
    f_pad = -(-f_all // 16) * 16
    sizes = (n_g, f_pad, f_shared, f_routed, local_experts, d_own)
    meta = jnp.stack([at_g, at_k, at_c]).astype(jnp.int32)

    def slices(shared, routed):
        parts = [
            shared.reshape(n_g, f_shared, d_own),
            routed.reshape(local_experts, n_g, f_routed, d_own)
            .transpose(1, 0, 2, 3)
            .reshape(n_g, -1, d_own),
        ]
        if f_pad > f_all:
            parts.append(jnp.zeros((n_g, f_pad - f_all, d_own), BF16))
        return jnp.concatenate(parts, axis=1)

    weight_slices = [
        slices(shared_gate.T, expert_gate.transpose(1, 2, 0)),
        slices(shared_up.T, expert_up.transpose(1, 2, 0)),
        slices(shared_down, expert_down),
    ]
    picked = [[pick(value, at_g ^ shift) for shift in range(n_g)] for value in weight_slices]
    picked[0], small_all = tie(picked[0], small_all)
    own_blocks = [
        [shift_by(value, "g", shift) for shift, value in enumerate(values)] for values in picked
    ]

    gain_1 = small_all[:, 16, :d_own].reshape(dim)
    gain_2 = small_all[:, 17, :d_own].reshape(dim)
    logit_w = small_all[:, 18, :d_own].reshape(dim)
    groups_all = small_all[:, 19, : 2 * CONTS].reshape(n_g, 2, 2, CONTS)
    groups = pick(pick(groups_all, at_g), at_k, 1).astype(jnp.int32)
    mixing_all = small_all[:, : 2 * EXPERTS].reshape(n_row, 2, EXPERTS, block)
    mixing_own = lax.dynamic_slice_in_dim(
        pick(mixing_all, at_k, 1), at_c * local_experts, local_experts, 1
    )
    mixing_own = mixing_own.transpose(0, 2, 1).reshape(total, local_experts)

    token_part = lax.all_to_all(tokens, "k", 0, 0, tiled=True).reshape(span, -1)
    cot_part = lax.all_to_all(cotangent, "k", 0, 0, tiled=True).reshape(span, -1)

    sub = own_rows // PARTS
    cot_rows = cot_part.reshape(1, n_c, PARTS, sub, dim // n_c)
    cot_rows = gather_joined(cot_rows, "g", 0)
    cot_all = []
    for part in range(PARTS):
        value = cot_rows[:, :, part][None, None]
        for axis in ("x", "y") if part % 2 else ("y", "x"):
            value = gather_joined(value, axis, ("y", "x").index(axis))
        cot_all.append(value.reshape(n_c, n_g, n_c, sub, dim // n_c))

    qkv = lax.all_gather(
        jnp.concatenate([query_weight, key_weight, value_weight], axis=1), ROW, axis=0, tiled=True
    )
    out_w = lax.all_gather(output_weight, ROW, axis=1, tiled=True)
    inputs = col_gather(token_part, n_c).reshape(n_c, span, -1).transpose(1, 0, 2)
    inputs = inputs.reshape(span, dim).astype(F32)

    own_blocks[0], inputs = tie(own_blocks[0], inputs)
    first_scale = lax.rsqrt(jnp.mean(inputs * inputs, axis=-1, keepdims=True) + epsilon)
    normed_1 = (inputs * first_scale * gain_1).astype(BF16)
    projected = dot(normed_1, qkv, ((1,), (0,)))
    allowed, position = block_layout(groups, block)
    cosine, sine = rotary_tables(position)
    head_shape = (2, block, heads, HEAD_DIM)
    query_rot = rotate(projected[:, :width].reshape(head_shape), cosine, sine).astype(BF16)
    key_rot = rotate(projected[:, width : 2 * width].reshape(head_shape), cosine, sine).astype(BF16)
    value_low = projected[:, 2 * width :].reshape(head_shape).astype(BF16)

    def einsum(form, left, right):
        return jnp.einsum(form, left, right, preferred_element_type=F32)

    scores = jnp.where(
        allowed[:, None],
        einsum("bqhd,bkhd->bhqk", query_rot, key_rot) * (1.0 / math.sqrt(HEAD_DIM)),
        masked_score,
    )
    peak = jnp.max(scores, axis=-1, keepdims=True)
    exp_scores = jnp.exp(scores - peak)
    probabilities = exp_scores / jnp.sum(exp_scores, axis=-1, keepdims=True)
    prob_low = probabilities.astype(BF16)
    mixed = einsum("bhqk,bkhd->bqhd", prob_low, value_low).astype(BF16).reshape(span, width)
    own_blocks[1], mixed = tie(own_blocks[1], mixed)
    attention = col_sum(dot(mixed, out_w, ((1,), (0,))), n_c)

    own_inputs = lax.dynamic_slice_in_dim(inputs, at_c * own_rows, own_rows, 0)
    cot_all, attention = tie(cot_all, attention)
    hidden = own_inputs + attention
    second_scale = lax.rsqrt(jnp.mean(hidden * hidden, axis=-1, keepdims=True) + epsilon)
    unit_2 = hidden * second_scale
    normed_own = (unit_2 * gain_2).astype(BF16)
    own_blocks[2], normed_own = tie(own_blocks[2], normed_own)

    def gather_rows(rows):
        value = gather_joined(rows[None], "g", 0)[:, None, None]
        sides = []
        for side, order in enumerate((("y", "x"), ("x", "y"))):
            half = value[..., side * (dim // 2) : (side + 1) * (dim // 2)]
            for axis in order:
                half = gather_joined(half, axis, 1 + ("y", "x").index(axis))
            sides.append(half)
        return jnp.concatenate(sides, axis=-1).reshape(-1, dim)

    normed_parts = [gather_rows(normed_own[part * sub : (part + 1) * sub]) for part in range(PARTS)]
    own_cot = [
        lax.dynamic_index_in_dim(cot[:, 0], at_c, 1, keepdims=False) for cot in cot_all
    ]
    own_cot = jnp.concatenate(own_cot, axis=1)
    own_cot = jnp.stack([pick(own_cot, at_c ^ c) for c in range(n_c)], axis=1)
    own_cot = own_cot.reshape(own_rows, dim)

    logit_low = jnp.zeros((EXTRA, dim), BF16).at[:2].set(logit_w.astype(BF16)[None])
    mixing_parts = mixing_own.reshape(n_g, n_c, PARTS, sub, local_experts)
    mixing_parts = jnp.stack([pick(mixing_parts, at_g ^ shift) for shift in range(n_g)])
    mixing_parts = jnp.stack([pick(mixing_parts, at_c ^ c, 1) for c in range(n_c)], axis=1)
    mixing_parts = jnp.pad(mixing_parts, ((0, 0),) * 4 + ((0, 8 - local_experts),))
    swapped = [[swap(value, "k") for value in values] for values in own_blocks]
    weight_blocks = [
        values[shift]
        for half in (own_blocks, swapped)
        for shift in range(n_g)
        for values in half
    ]
    passes = [
        ffn_pass(
            sizes,
            meta,
            normed_parts[part],
            cot_all[part],
            mixing_parts[:, :, part].reshape(-1, 8),
            logit_low,
            weight_blocks,
        )
        for part in range(PARTS)
    ]

    def split_sides(partial):
        part = partial.reshape(n_g, n_y, n_x, sub, dim)
        return [part[..., : dim // 2], part[..., dim // 2 :]]

    def scatter_axis(value, axis, at):
        bit = 1
        while bit < lax.axis_size(axis):
            value = halve(value, axis, at, bit)
            bit *= 2
        return lax.index_in_dim(value, 0, at, keepdims=False)

    def cols_first(sides):
        return [scatter_axis(sides[0], "x", 2), scatter_axis(sides[1], "y", 1)]

    def cols_second(sides):
        sides = [scatter_axis(sides[0], "y", 1), scatter_axis(sides[1], "x", 1)]
        return jnp.concatenate(sides, axis=-1)

    def chips_steps(value):
        bit = 1
        while 2 * bit < n_g:
            value = halve(value, "g", 0, bit)
            bit *= 2
        return value

    def chips_last(value):
        other = shift_by(value[1], "g", n_g // 2)
        return value[0].astype(F32) + other.astype(F32)

    def own_core(grad):
        other = swap(grad[1], "k")
        return (grad[0].astype(F32) + other.astype(F32)).astype(BF16)

    def send_slices(both):
        return [shift_by(both[shift], "g", shift) for shift in range(n_g)]

    def place_slices(moved):
        moved = jnp.stack(moved)
        moved = jnp.stack([pick(moved, at_g ^ source) for source in range(n_g)])
        shared = moved[:, :f_shared].reshape(n_g * f_shared, d_own)
        routed = moved[:, f_shared:f_all].reshape(n_g, local_experts, f_routed, d_own)
        routed = routed.transpose(1, 0, 2, 3).reshape(local_experts, n_g * f_routed, d_own)
        return (shared, routed)

    acts, gates, ups = ([parts[i] for parts in passes] for i in (2, 3, 4))
    first = cols_first(split_sides(passes[0][1]))
    first, acts = tie(first, acts)
    (down_blocks,) = weight_grad(sizes, meta, acts, cot_all, True)
    first = cols_second(first)
    second = cols_first(split_sides(passes[1][1]))
    first, second, gates, down_blocks = tie(first, second, gates, down_blocks)
    gate_blocks, logit_sum = weight_grad(sizes, meta, gates, normed_parts, False)
    logit_sum = logit_sum[0]
    first = chips_steps(first)
    second = cols_second(second)
    down_both = own_core(down_blocks)
    first, second, down_both, ups, gate_blocks = tie(first, second, down_both, ups, gate_blocks)
    down_moved = send_slices(down_both)
    (up_blocks,) = weight_grad(sizes, meta, ups, normed_parts, False)
    first = chips_last(first)
    second = chips_steps(second)
    gate_both = own_core(gate_blocks)
    first, second, gate_both, up_blocks = tie(first, second, gate_both, up_blocks)
    second = chips_last(second)
    up_both = own_core(up_blocks)
    out_sides = [cols_first(split_sides(parts[0])) for parts in passes]
    normed_grad_2 = jnp.concatenate([first, second], axis=0)
    normed_grad_2, up_both = tie(normed_grad_2, up_both)
    hidden_part, gain_2_sum = norm_back(normed_grad_2, unit_2, second_scale, gain_2)
    hidden_grad = own_cot.astype(F32) + hidden_part
    gate_moved = send_slices(gate_both)
    up_moved = send_slices(up_both)
    attn_grad = col_gather(hidden_grad.astype(BF16), n_c).reshape(span, dim)
    out_sides, attn_grad, down_moved = tie(out_sides, attn_grad, down_moved)
    out_parts = [cols_second(sides) for sides in out_sides]
    down_s, down_e = place_slices(down_moved)

    out_grad = dot(attn_grad, mixed, ((0,), (0,)))
    mixed_grad = dot(attn_grad, out_w, ((1,), (1,))).astype(BF16).reshape(head_shape)
    out_parts, mixed_grad = tie(out_parts, mixed_grad)
    out_parts = [chips_steps(part) for part in out_parts]
    prob_grad = einsum("bqhd,bkhd->bhqk", mixed_grad, value_low)
    value_grad = einsum("bhqk,bqhd->bkhd", prob_low, mixed_grad).astype(BF16)
    center = jnp.sum(prob_grad * probabilities, axis=-1, keepdims=True)
    score_grad = (probabilities * (prob_grad - center) * (1.0 / math.sqrt(HEAD_DIM))).astype(BF16)
    query_grad = rotate(einsum("bhqk,bkhd->bqhd", score_grad, key_rot), cosine, -sine).astype(BF16)
    key_grad = rotate(einsum("bhqk,bqhd->bkhd", score_grad, query_rot), cosine, -sine).astype(BF16)
    qkv_grad = jnp.concatenate(
        [part.reshape(span, width) for part in (query_grad, key_grad, value_grad)], axis=1
    )
    qkv_grad, gate_moved, out_parts = tie(qkv_grad, gate_moved, out_parts)
    out_rows = jnp.concatenate([chips_last(part) for part in out_parts], axis=0)
    gate_s, gate_e = place_slices(gate_moved)
    qkv_sum = dot(normed_1, qkv_grad, ((0,), (0,)))
    normed_grad_1 = col_sum(dot(qkv_grad, qkv, ((1,), (1,))), n_c)
    normed_grad_1, up_moved = tie(normed_grad_1, up_moved)
    up_s, up_e = place_slices(up_moved)
    own_scale = lax.dynamic_slice_in_dim(first_scale, at_c * own_rows, own_rows, 0)
    rows_part, gain_1_sum = norm_back(normed_grad_1, own_inputs * own_scale, own_scale, gain_1)
    token_grad = rows_to_features((hidden_grad + rows_part).astype(BF16), n_c).astype(F32)

    result = rows_to_features((hidden + out_rows).astype(BF16), n_c)

    sums = jnp.stack([gain_1_sum, gain_2_sum, logit_sum]).reshape(3, n_row, d_own)
    sums = jnp.broadcast_to(sums.transpose(1, 0, 2)[:, None], (n_row, n_c, 3, d_own))
    sums = lax.all_to_all(sums.reshape(n_row * n_c, 3, d_own), ALL, 0, 0, tiled=True)
    sums = jnp.sum(sums, axis=0)

    out_w_grad = lax.psum_scatter(out_grad.astype(BF16), ROW, scatter_dimension=0, tiled=True)
    qkv_own = lax.psum_scatter(qkv_sum.astype(BF16), ROW, scatter_dimension=0, tiled=True)
    qkv_own = qkv_own.astype(F32)
    return (
        result,
        token_grad,
        sums[0],
        qkv_own[:, :width],
        qkv_own[:, width : 2 * width],
        qkv_own[:, 2 * width :],
        out_w_grad.T.astype(F32),
        sums[1],
        gate_s.T.astype(F32),
        up_s.T.astype(F32),
        down_s.astype(F32),
        sums[2],
        gate_e.transpose(2, 0, 1).astype(F32),
        up_e.transpose(2, 0, 1).astype(F32),
        down_e.astype(F32),
    )


def solution(mesh):
    n_row, n_col = mesh.shape["row"], mesh.shape["col"]
    inner = Mesh(mesh.devices.reshape(n_row // 2, 2, n_col // 2, 2), ALL)
    return jax.shard_map(
        shards,
        mesh=inner,
        in_specs=(
            P(None, ROW, COL),
            P(None, ROW, None),
            P(None, ROW, None),
            P(None, ROW),
            P(ROW),
            P(ROW, COL),
            P(ROW, COL),
            P(ROW, COL),
            P(COL, ROW),
            P(ROW),
            P(ROW, COL),
            P(ROW, COL),
            P(COL, ROW),
            P(ROW),
            P(ROW, COL, None),
            P(ROW, COL, None),
            P(COL, None, ROW),
            P(None, ROW, COL),
        ),
        out_specs=(
            P(None, ROW, COL),
            P(None, ROW, COL),
            P(ROW),
            P(ROW, COL),
            P(ROW, COL),
            P(ROW, COL),
            P(COL, ROW),
            P(ROW),
            P(ROW, COL),
            P(ROW, COL),
            P(COL, ROW),
            P(ROW),
            P(ROW, COL, None),
            P(ROW, COL, None),
            P(COL, None, ROW),
        ),
        check_vma=False,
    )
```

```python
import functools
import math

import jax
import jax.numpy as jnp
from jax import lax
from jax.experimental import pallas as pl
from jax.experimental.pallas import tpu as pltpu
from jax.sharding import Mesh, PartitionSpec as P

HEAD_DIM = 128
EXPERTS = 8
PROMPTS = 2
CONTS = 2
CONT_LEN = 64
PROMPT_LEN = 64

epsilon = 1e-06
rope_base = 1000000.0
masked_score = -1000000000.0

F32 = jnp.float32
BF16 = jnp.bfloat16
COL = ("y", "x")
ROW = ("g", "k")
ALL = ("g", "k", "y", "x")


def block_layout(groups, row_count):
    token_index = jnp.arange(row_count, dtype=jnp.int32)
    prompt_rows = PROMPTS * PROMPT_LEN
    is_prompt = token_index < prompt_rows
    cont_offset = jnp.maximum(token_index - prompt_rows, 0)
    cont_number = cont_offset // CONT_LEN
    segment = jnp.where(is_prompt, token_index // PROMPT_LEN, PROMPTS + cont_number)
    position = jnp.where(is_prompt, token_index % PROMPT_LEN, PROMPT_LEN + cont_offset % CONT_LEN)
    cont_picks = (cont_number[:, None] == jnp.arange(CONTS, dtype=jnp.int32)[None, :]).astype(
        jnp.int32
    )
    source = jnp.where(
        is_prompt[None], segment[None], jnp.sum(cont_picks[None] * groups[:, None, :], axis=2)
    )
    same_segment = (segment[:, None] == segment[None, :]) & (position[None, :] <= position[:, None])
    context = (
        jnp.logical_not(is_prompt)[None, :, None]
        & is_prompt[None, None, :]
        & (source[:, :, None] == segment[None, None, :])
    )
    return (same_segment[None] | context, position)


def rotary_tables(position):
    half_dim = HEAD_DIM // 2
    frequency = rope_base ** (-(2.0 * jnp.arange(half_dim, dtype=F32)) / HEAD_DIM)
    angles = position.astype(F32)[:, None] * frequency[None, :]
    cosine = jnp.cos(angles)
    sine = jnp.sin(angles)
    return (cosine[None, :, None, :], sine[None, :, None, :])


def rotate(values, cosine, sine):
    first, second = jnp.split(values, 2, axis=-1)
    return jnp.concatenate([first * cosine - second * sine, second * cosine + first * sine], -1)


def dot(left, right, dims):
    return lax.dot_general(left, right, (dims, ((), ())), preferred_element_type=F32)


PARTS = 2
EXTRA = 16


def ffn_kernel(sizes, groups, meta, rows_ref, cot_ref, side_ref, *refs):
    n_g, f_pad, f_one, d_own = sizes
    blocks = refs[: groups * 2 * n_g]
    sums = refs[groups * 2 * n_g : -8]
    out_ref, normed_ref, act_ref, gate_ref, up_ref, w_gu, w_down, sems = refs[-8:]
    g_at, k_at, c_at = meta[0], meta[1], meta[2]
    shared = groups == 1

    @pl.when(pl.program_id(0) == 0)
    def _():
        copies = []
        for half in range(2):
            for shift in range(n_g):
                at = half * n_g + shift
                column = 2 * (g_at ^ shift) + (k_at ^ half)
                lanes = pl.ds(pl.multiple_of(column * d_own, d_own), d_own)
                if shared:
                    both, down = blocks[at].at[: 2 * f_pad], blocks[at].at[2 * f_pad :]
                else:
                    both, down = blocks[at], blocks[2 * n_g + at]
                copies.append(
                    pltpu.make_async_copy(both, w_gu.at[: 2 * f_pad, lanes], sems.at[2 * at])
                )
                copies.append(pltpu.make_async_copy(down, w_down.at[:, lanes], sems.at[2 * at + 1]))
        for copy in copies:
            copy.start()
        if shared:
            w_gu[2 * f_pad :, :] = side_ref[...]
        for copy in copies:
            copy.wait()

    rows = rows_ref[...]
    count = rows.shape[0]
    n_c = cot_ref.shape[0]
    cot = jnp.concatenate(
        [
            jnp.concatenate([cot_ref[c ^ c_at, 0, row ^ c_at] for row in range(n_c)], axis=0)
            for c in range(n_c)
        ],
        axis=1,
    )
    minor = ((1,), (1,))
    pre = dot(w_gu[...], rows, minor)
    down_back = dot(w_down[...], cot, minor)
    gate_pre, up_pre = pre[:f_pad], pre[f_pad : 2 * f_pad]
    if shared:
        prob = jax.nn.sigmoid(pre[2 * f_pad : 2 * f_pad + 1])
        scale = jnp.broadcast_to(prob, (f_pad, count))
    else:
        full = f_pad // f_one
        pieces = [jnp.broadcast_to(side_ref[0, e : e + 1, :], (f_one, count)) for e in range(full)]
        if f_pad > full * f_one:
            pieces.append(jnp.zeros((f_pad - full * f_one, count), F32))
        scale = jnp.concatenate(pieces, axis=0)
    sigma = jax.nn.sigmoid(gate_pre)
    silu = gate_pre * sigma
    act = silu * up_pre
    act_grad = down_back * scale
    act_low = (act * scale).astype(BF16)
    gate_low = (act_grad * up_pre * sigma * (1.0 + gate_pre * (1.0 - sigma))).astype(BF16)
    up_low = (act_grad * silu).astype(BF16)
    act_ref[...] = act_low
    gate_ref[:f_pad, :] = gate_low
    up_ref[...] = up_low
    both = [gate_low, up_low]
    if shared:
        prob_part = jnp.sum(act * down_back, axis=0, keepdims=True)
        logit_part = prob_part * prob * (1.0 - prob)
        logit_high = logit_part.astype(BF16).astype(F32)
        logit_rows = jnp.concatenate(
            [logit_high, logit_part - logit_high, jnp.zeros((EXTRA - 2, count), F32)], axis=0
        ).astype(BF16)
        gate_ref[f_pad:, :] = logit_rows
        both.append(logit_rows)
    major = ((0,), (0,))
    out = dot(act_low, w_down[...], major)
    normed = dot(jnp.concatenate(both, axis=0), w_gu[...], major)
    if sums:
        out = out + sums[0][...].astype(F32)
        normed = normed + sums[1][...].astype(F32)
    out_ref[...] = out.astype(BF16)
    normed_ref[...] = normed.astype(BF16)


def ffn_pass(sizes, meta, rows, cot, side, blocks, sums):
    n_g, f_pad, _, d_own = sizes
    total, dim = rows.shape
    n_c, _, _, sub, cw = cot.shape
    tile = n_c * sub
    groups = len(blocks) // (2 * n_g)
    extra = EXTRA if groups == 1 else 0
    flat = lambda i, m: (i, 0)
    wide = lambda i, m: (0, i)
    if groups == 1:
        side_spec = pl.BlockSpec((EXTRA, dim), lambda i, m: (0, 0))
    else:
        side = side.reshape(-1, tile, 8).transpose(0, 2, 1)
        side_spec = pl.BlockSpec((1, 8, tile), lambda i, m: (i, 0, 0))
    return pl.pallas_call(
        functools.partial(ffn_kernel, sizes, groups),
        grid_spec=pltpu.PrefetchScalarGridSpec(
            num_scalar_prefetch=1,
            grid=(n_g,),
            in_specs=[
                pl.BlockSpec((tile, dim), flat),
                pl.BlockSpec((n_c, 1, n_c, sub, cw), lambda i, m: (0, i, 0, 0, 0)),
                side_spec,
            ]
            + [pl.BlockSpec(memory_space=pl.ANY)] * len(blocks)
            + [pl.BlockSpec((tile, dim), flat)] * len(sums),
            out_specs=[
                pl.BlockSpec((tile, dim), flat),
                pl.BlockSpec((tile, dim), flat),
                pl.BlockSpec((f_pad, tile), wide),
                pl.BlockSpec((f_pad + extra, tile), wide),
                pl.BlockSpec((f_pad, tile), wide),
            ],
            scratch_shapes=[
                pltpu.VMEM((2 * f_pad + extra, dim), BF16),
                pltpu.VMEM((f_pad, dim), BF16),
                pltpu.SemaphoreType.DMA((4 * n_g,)),
            ],
        ),
        out_shape=[
            jax.ShapeDtypeStruct((total, dim), BF16),
            jax.ShapeDtypeStruct((total, dim), BF16),
            jax.ShapeDtypeStruct((f_pad, total), BF16),
            jax.ShapeDtypeStruct((f_pad + extra, total), BF16),
            jax.ShapeDtypeStruct((f_pad, total), BF16),
        ],
        compiler_params=pltpu.CompilerParams(
            dimension_semantics=("arbitrary",), vmem_limit_bytes=60 * 1024 * 1024
        ),
        cost_estimate=pl.CostEstimate(
            flops=12 * total * dim * f_pad,
            bytes_accessed=(8 + 4 * len(sums)) * total * dim + 6 * total * f_pad + 6 * f_pad * dim,
            transcendentals=total * f_pad,
        ),
        name="ffn_pass",
    )(meta, rows, cot, side, *blocks, *sums)


def grad_kernel(parts, kinds, f_pad, meta, *refs):
    lefts, refs = refs[: parts * len(kinds)], refs[parts * len(kinds) :]
    values = {}
    for cot in sorted(set(kinds)):
        rights, refs = refs[:parts], refs[parts:]
        if cot:
            _, n_g, n_c, _, _ = rights[0].shape
            order = [(g, c) for g in range(n_g) for c in range(n_c)]
            values[cot] = [
                jnp.concatenate([right[0, g, c ^ meta[2]] for g, c in order], axis=0)
                for right in rights
            ]
        else:
            values[cot] = [right[...] for right in rights]
    for i, cot in enumerate(kinds):
        total = None
        for left, value in zip(lefts[i * parts : (i + 1) * parts], values[cot]):
            term = dot(left[...], value, ((1,), (0,)))
            total = term if total is None else total + term
        refs[0][0, 0, i * f_pad : (i + 1) * f_pad] = total[:f_pad].astype(BF16)
        if total.shape[0] > f_pad:
            refs[1][...] = jnp.broadcast_to(
                total[f_pad : f_pad + 1] + total[f_pad + 1 : f_pad + 2], refs[1].shape
            )


def weight_grad(sizes, meta, kinds, lefts, normed, cots):
    n_g, f_pad, _, d_own = sizes
    parts = len(normed)
    part_rows, dim = normed[0].shape
    extra = max(value[0].shape[0] for value in lefts) > f_pad
    n_c, _, _, sub, cw = cots[0].shape
    per = cw // d_own
    arrays, specs = [], []
    for values in lefts:
        arrays += values
        specs += [pl.BlockSpec(values[0].shape, lambda j, m: (0, 0))] * parts
    if False in kinds:
        arrays += normed
        specs += [pl.BlockSpec((part_rows, d_own), lambda j, m: (0, j))] * parts
    if True in kinds:
        arrays += cots
        specs += [
            pl.BlockSpec(
                (1, n_g, n_c, sub, d_own), lambda j, m: ((j // per) ^ m[2], 0, 0, 0, j % per)
            )
        ] * parts
    f_out = len(kinds) * f_pad
    out_specs = [
        pl.BlockSpec((1, 1, f_out, d_own), lambda j, m: ((j % 2) ^ m[1], (j // 2) ^ m[0], 0, 0))
    ]
    out_shape = [jax.ShapeDtypeStruct((2, n_g, f_out, d_own), BF16)]
    if extra:
        out_specs.append(pl.BlockSpec((8, d_own), lambda j, m: (0, j)))
        out_shape.append(jax.ShapeDtypeStruct((8, dim), F32))
    return pl.pallas_call(
        functools.partial(grad_kernel, parts, kinds, f_pad),
        grid_spec=pltpu.PrefetchScalarGridSpec(
            num_scalar_prefetch=1, grid=(2 * n_g,), in_specs=specs, out_specs=out_specs
        ),
        out_shape=out_shape,
        compiler_params=pltpu.CompilerParams(
            dimension_semantics=("arbitrary",), vmem_limit_bytes=56 * 1024 * 1024
        ),
        cost_estimate=pl.CostEstimate(
            flops=2 * parts * part_rows * dim * f_out,
            bytes_accessed=2 * parts * part_rows * (dim + f_out) + 2 * f_out * dim,
            transcendentals=0,
        ),
        name="weight_grad",
    )(meta, *arrays)


def tie(*values):
    return lax.optimization_barrier(values)


def norm_back(normed_grad, unit_rows, scale, gain):
    weighted = normed_grad * gain
    rows_grad = scale * (
        weighted - unit_rows * jnp.mean(weighted * unit_rows, axis=-1, keepdims=True)
    )
    return (rows_grad, jnp.sum(normed_grad * unit_rows, axis=0))


def swap(value, axis):
    return lax.ppermute(value, axis, [(0, 1), (1, 0)])


def shift_by(value, axis, shift):
    if shift == 0:
        return value
    return lax.ppermute(value, axis, [(i, i ^ shift) for i in range(lax.axis_size(axis))])


def gather_joined(value, axis, at):
    bit = lax.axis_size(axis) // 2
    while bit:
        shape = value.shape[:at] + (2 * value.shape[at],) + value.shape[at + 1 :]
        value = jnp.stack([value, shift_by(value, axis, bit)], axis=at + 1).reshape(shape)
        bit //= 2
    return value


def halve(value, axis, at, bit):
    size = value.shape[at]
    shape = value.shape[:at] + (size // 2, 2) + value.shape[at + 1 :]
    pair = value.reshape(shape)
    keep, send = (lax.index_in_dim(pair, i, at + 1, keepdims=False) for i in range(2))
    other = shift_by(send, axis, bit)
    return (keep.astype(F32) + other.astype(F32)).astype(BF16)


def col_gather(value, count):
    spread = jnp.broadcast_to(value[None], (count,) + value.shape)
    return lax.all_to_all(spread, COL, 0, 0, tiled=True)


def col_sum(partial, count):
    parts = partial.astype(BF16).reshape((count, -1) + partial.shape[1:])
    return jnp.sum(lax.all_to_all(parts, COL, 0, 0, tiled=True).astype(F32), axis=0)


def rows_to_features(rows, count):
    row_count, width = rows.shape
    parts = rows.reshape(row_count, count, width // count).transpose(1, 0, 2)
    moved = lax.all_to_all(parts, COL, 0, 0, tiled=True)
    blocks = moved.reshape(2, row_count * count // 2, width // count)
    return lax.all_to_all(blocks, "k", 0, 0, tiled=True)


def shards(
    tokens,
    routes,
    route_weights,
    group_ids,
    first_gain,
    query_weight,
    key_weight,
    value_weight,
    output_weight,
    second_gain,
    shared_gate,
    shared_up,
    shared_down,
    shared_logit,
    expert_gate,
    expert_up,
    expert_down,
    cotangent,
):
    n_g = lax.axis_size("g")
    n_c = lax.axis_size("y") * lax.axis_size("x")
    n_y, n_x = lax.axis_size("y"), lax.axis_size("x")
    n_row = 2 * n_g
    at_g, at_k = lax.axis_index("g"), lax.axis_index("k")
    at_c = lax.axis_index(COL)
    block = tokens.shape[1]
    dim = query_weight.shape[0] * n_row
    d_own = query_weight.shape[0]
    width = query_weight.shape[1]
    heads = width // HEAD_DIM
    local_experts = expert_gate.shape[1]
    span = 2 * block
    total = n_g * span
    own_rows = span // n_c
    pick = lambda array, index, axis=0: lax.dynamic_index_in_dim(array, index, axis, keepdims=False)

    labels = jnp.arange(EXPERTS, dtype=jnp.int32)
    mixing = jnp.sum(
        jnp.where(
            routes[:, None] == labels[None, :, None, None], route_weights[:, None], 0.0
        ),
        axis=-1,
    )
    small = jnp.concatenate(
        [
            mixing.reshape(2 * EXPERTS, block),
            jnp.zeros((8, block), F32)
            .at[0, :d_own].set(first_gain.astype(F32))
            .at[1, :d_own].set(second_gain.astype(F32))
            .at[2, :d_own].set(shared_logit.astype(F32))
            .at[3, : 2 * CONTS].set(group_ids.astype(F32).reshape(-1)),
        ],
        axis=0,
    )
    small_all = lax.all_to_all(
        jnp.broadcast_to(small[None], (n_row,) + small.shape), ROW, 0, 0, tiled=True
    )
    f_shared = shared_gate.shape[1] // n_g
    f_routed = expert_gate.shape[2] // n_g
    f_experts = local_experts * f_routed
    f_one, f_two = -(-f_shared // 16) * 16, -(-f_experts // 16) * 16
    sizes_s = (n_g, f_one, f_shared, d_own)
    sizes_e = (n_g, f_two, f_routed, d_own)
    meta = jnp.stack([at_g, at_k, at_c]).astype(jnp.int32)

    def fill(value, size):
        return jnp.pad(value, ((0, 0), (0, size - value.shape[1]), (0, 0)))

    def slices_s(value):
        return fill(value.reshape(n_g, f_shared, d_own), f_one)

    def slices_e(value):
        value = value.reshape(local_experts, n_g, f_routed, d_own).transpose(1, 0, 2, 3)
        return fill(value.reshape(n_g, f_experts, d_own), f_two)

    weight_slices = [
        jnp.concatenate([slices_s(w) for w in (shared_gate.T, shared_up.T, shared_down)], axis=1),
        jnp.concatenate([slices_e(w.transpose(1, 2, 0)) for w in (expert_gate, expert_up)], axis=1),
        slices_e(expert_down),
    ]
    picked = [[pick(value, at_g ^ shift) for shift in range(n_g)] for value in weight_slices]
    picked[0], small_all = tie(picked[0], small_all)
    own_blocks = [
        [shift_by(value, "g", shift) for shift, value in enumerate(values)] for values in picked
    ]

    gain_1 = small_all[:, 16, :d_own].reshape(dim)
    gain_2 = small_all[:, 17, :d_own].reshape(dim)
    logit_w = small_all[:, 18, :d_own].reshape(dim)
    groups_all = small_all[:, 19, : 2 * CONTS].reshape(n_g, 2, 2, CONTS)
    groups = pick(pick(groups_all, at_g), at_k, 1).astype(jnp.int32)
    mixing_all = small_all[:, : 2 * EXPERTS].reshape(n_row, 2, EXPERTS, block)
    mixing_own = lax.dynamic_slice_in_dim(
        pick(mixing_all, at_k, 1), at_c * local_experts, local_experts, 1
    )
    mixing_own = mixing_own.transpose(0, 2, 1).reshape(total, local_experts)

    token_part = lax.all_to_all(tokens, "k", 0, 0, tiled=True).reshape(span, -1)
    cot_part = lax.all_to_all(cotangent, "k", 0, 0, tiled=True).reshape(span, -1)

    sub = own_rows // PARTS
    cot_rows = cot_part.reshape(1, n_c, PARTS, sub, dim // n_c)
    cot_rows = gather_joined(cot_rows, "g", 0)
    cot_all = []
    for part in range(PARTS):
        value = cot_rows[:, :, part][None, None]
        for axis in ("x", "y") if part % 2 else ("y", "x"):
            value = gather_joined(value, axis, ("y", "x").index(axis))
        cot_all.append(value.reshape(n_c, n_g, n_c, sub, dim // n_c))

    qkv = lax.all_gather(
        jnp.concatenate([query_weight, key_weight, value_weight], axis=1), ROW, axis=0, tiled=True
    )
    out_w = lax.all_gather(output_weight, ROW, axis=1, tiled=True)
    inputs = col_gather(token_part, n_c).reshape(n_c, span, -1).transpose(1, 0, 2)
    inputs = inputs.reshape(span, dim).astype(F32)

    own_blocks[0], inputs = tie(own_blocks[0], inputs)
    first_scale = lax.rsqrt(jnp.mean(inputs * inputs, axis=-1, keepdims=True) + epsilon)
    normed_1 = (inputs * first_scale * gain_1).astype(BF16)
    projected = dot(normed_1, qkv, ((1,), (0,)))
    allowed, position = block_layout(groups, block)
    cosine, sine = rotary_tables(position)
    head_shape = (2, block, heads, HEAD_DIM)
    query_rot = rotate(projected[:, :width].reshape(head_shape), cosine, sine).astype(BF16)
    key_rot = rotate(projected[:, width : 2 * width].reshape(head_shape), cosine, sine).astype(BF16)
    value_low = projected[:, 2 * width :].reshape(head_shape).astype(BF16)

    def einsum(form, left, right):
        return jnp.einsum(form, left, right, preferred_element_type=F32)

    scores = jnp.where(
        allowed[:, None],
        einsum("bqhd,bkhd->bhqk", query_rot, key_rot) * (1.0 / math.sqrt(HEAD_DIM)),
        masked_score,
    )
    peak = jnp.max(scores, axis=-1, keepdims=True)
    exp_scores = jnp.exp(scores - peak)
    probabilities = exp_scores / jnp.sum(exp_scores, axis=-1, keepdims=True)
    prob_low = probabilities.astype(BF16)
    mixed = einsum("bhqk,bkhd->bqhd", prob_low, value_low).astype(BF16).reshape(span, width)
    attention = col_sum(dot(mixed, out_w, ((1,), (0,))), n_c)

    own_inputs = lax.dynamic_slice_in_dim(inputs, at_c * own_rows, own_rows, 0)
    cot_all, attention = tie(cot_all, attention)
    hidden = own_inputs + attention
    second_scale = lax.rsqrt(jnp.mean(hidden * hidden, axis=-1, keepdims=True) + epsilon)
    unit_2 = hidden * second_scale
    normed_own = (unit_2 * gain_2).astype(BF16)

    def gather_cols(value):
        sides = []
        for side, order in enumerate((("y", "x"), ("x", "y"))):
            half = value[..., side * (dim // 2) : (side + 1) * (dim // 2)]
            for axis in order:
                half = gather_joined(half, axis, 1 + ("y", "x").index(axis))
            sides.append(half)
        return jnp.concatenate(sides, axis=-1).reshape(-1, dim)

    routed_gu, routed_d = own_blocks[1:]
    routed_gu[1], normed_own = tie(routed_gu[1], normed_own)
    halves = [normed_own[part * sub : (part + 1) * sub][None] for part in range(PARTS)]
    halves[0] = gather_joined(halves[0], "g", 0)
    halves[0], halves[1], routed_gu[2:3] = tie(halves[0], halves[1], routed_gu[2:3])
    halves[1] = gather_joined(halves[1], "g", 0)
    normed_parts = [gather_cols(halves[0][:, None, None])]
    normed_parts[0], halves[1], routed_gu[3:], routed_d[1] = tie(
        normed_parts[0], halves[1], routed_gu[3:], routed_d[1]
    )
    normed_parts.append(gather_cols(halves[1][:, None, None]))
    normed_parts[1], routed_d[2:3] = tie(normed_parts[1], routed_d[2:3])
    own_cot = [
        lax.dynamic_index_in_dim(cot[:, 0], at_c, 1, keepdims=False) for cot in cot_all
    ]
    own_cot = jnp.concatenate(own_cot, axis=1)
    own_cot = jnp.stack([pick(own_cot, at_c ^ c) for c in range(n_c)], axis=1)
    own_cot = own_cot.reshape(own_rows, dim)

    def own_core(grad):
        other = swap(grad[1], "k")
        return (grad[0].astype(F32) + other.astype(F32)).astype(BF16)

    def send_slices(both):
        return [shift_by(both[shift], "g", shift) for shift in range(n_g)]

    def place_slices(moved, kinds):
        moved = jnp.stack(moved)
        moved = jnp.stack([pick(moved, at_g ^ source) for source in range(n_g)])
        return [
            moved[:, i * (moved.shape[1] // kinds) :][:, : moved.shape[1] // kinds]
            for i in range(kinds)
        ]

    def place_s(value):
        return value[:, :f_shared].reshape(n_g * f_shared, d_own)

    def place_e(value):
        value = value[:, :f_experts].reshape(n_g, local_experts, f_routed, d_own)
        return value.transpose(1, 0, 2, 3).reshape(local_experts, n_g * f_routed, d_own)

    logit_low = jnp.zeros((EXTRA, dim), BF16).at[:2].set(logit_w.astype(BF16)[None])
    mixing_parts = mixing_own.reshape(n_g, n_c, PARTS, sub, local_experts)
    mixing_parts = jnp.stack([pick(mixing_parts, at_g ^ shift) for shift in range(n_g)])
    mixing_parts = jnp.stack([pick(mixing_parts, at_c ^ c, 1) for c in range(n_c)], axis=1)
    mixing_parts = jnp.pad(mixing_parts, ((0, 0),) * 4 + ((0, 8 - local_experts),))
    def blocks_of(values):
        return values + [swap(value, "k") for value in values]

    blocks_s = blocks_of(own_blocks[0])
    passes_s = [
        ffn_pass(sizes_s, meta, normed_parts[part], cot_all[part], logit_low, blocks_s, [])
        for part in range(PARTS)
    ]
    kinds = (False, False, True)
    grad_s, logit_sum = weight_grad(
        sizes_s, meta, kinds, [[p[i] for p in passes_s] for i in (3, 4, 2)], normed_parts, cot_all
    )
    logit_sum = logit_sum[0]
    sums = [[passes_s[part][0], passes_s[part][1]] for part in range(PARTS)]
    sums[0], grad_s = tie(sums[0], grad_s)
    blocks_e = blocks_of(own_blocks[1]) + blocks_of(own_blocks[2])
    passes = []
    for part in range(PARTS):
        if part == 1:
            both_s = own_core(grad_s)
            sums[1], both_s = tie(sums[1], both_s)
        passes.append(
            ffn_pass(
                sizes_e,
                meta,
                normed_parts[part],
                cot_all[part],
                mixing_parts[:, :, part].reshape(-1, 8),
                blocks_e,
                sums[part],
            )
        )
    moved_s = send_slices(both_s)

    def split_sides(partial):
        part = partial.reshape(n_g, n_y, n_x, sub, dim)
        return [part[..., : dim // 2], part[..., dim // 2 :]]

    def scatter_axis(value, axis, at):
        bit = 1
        while bit < lax.axis_size(axis):
            value = halve(value, axis, at, bit)
            bit *= 2
        return lax.index_in_dim(value, 0, at, keepdims=False)

    def cols_first(sides):
        return [scatter_axis(sides[0], "x", 2), scatter_axis(sides[1], "y", 1)]

    def cols_second(sides):
        sides = [scatter_axis(sides[0], "y", 1), scatter_axis(sides[1], "x", 1)]
        return jnp.concatenate(sides, axis=-1)

    def chips_steps(value):
        bit = 1
        while 2 * bit < n_g:
            value = halve(value, "g", 0, bit)
            bit *= 2
        return value

    def chips_last(value):
        other = shift_by(value[1], "g", n_g // 2)
        return value[0].astype(F32) + other.astype(F32)

    acts, gates, ups = ([parts[i] for parts in passes] for i in (2, 3, 4))
    first = cols_first(split_sides(passes[0][1]))
    first, acts = tie(first, acts)
    (grad_d,) = weight_grad(sizes_e, meta, (True,), [acts], normed_parts, cot_all)
    first = cols_second(first)
    second = cols_first(split_sides(passes[1][1]))
    first, second, gates, grad_d = tie(first, second, gates, grad_d)
    (grad_gu,) = weight_grad(sizes_e, meta, (False, False), [gates, ups], normed_parts, cot_all)
    first = chips_steps(first)
    second = cols_second(second)
    both_d = own_core(grad_d)
    first, second, both_d, moved_s, grad_gu = tie(first, second, both_d, moved_s, grad_gu)
    moved_d = send_slices(both_d)
    first = chips_last(first)
    second = chips_steps(second)
    both_gu = own_core(grad_gu)
    first, second, both_gu = tie(first, second, both_gu)
    second = chips_last(second)
    out_sides = [cols_first(split_sides(parts[0])) for parts in passes]
    normed_grad_2 = jnp.concatenate([first, second], axis=0)
    hidden_part, gain_2_sum = norm_back(normed_grad_2, unit_2, second_scale, gain_2)
    hidden_grad = own_cot.astype(F32) + hidden_part
    moved_gu = send_slices(both_gu)
    attn_grad = col_gather(hidden_grad.astype(BF16), n_c).reshape(span, dim)
    out_sides, attn_grad, moved_d = tie(out_sides, attn_grad, moved_d)
    out_parts = [cols_second(sides) for sides in out_sides]
    gate_s, up_s, down_s = (place_s(value) for value in place_slices(moved_s, 3))
    down_e = place_e(place_slices(moved_d, 1)[0])

    out_grad = dot(attn_grad, mixed, ((0,), (0,)))
    mixed_grad = dot(attn_grad, out_w, ((1,), (1,))).astype(BF16).reshape(head_shape)
    out_parts, mixed_grad = tie(out_parts, mixed_grad)
    out_parts = [chips_steps(part) for part in out_parts]
    prob_grad = einsum("bqhd,bkhd->bhqk", mixed_grad, value_low)
    value_grad = einsum("bhqk,bqhd->bkhd", prob_low, mixed_grad).astype(BF16)
    center = jnp.sum(prob_grad * probabilities, axis=-1, keepdims=True)
    score_grad = (probabilities * (prob_grad - center) * (1.0 / math.sqrt(HEAD_DIM))).astype(BF16)
    query_grad = rotate(einsum("bhqk,bkhd->bqhd", score_grad, key_rot), cosine, -sine).astype(BF16)
    key_grad = rotate(einsum("bhqk,bqhd->bkhd", score_grad, query_rot), cosine, -sine).astype(BF16)
    qkv_grad = jnp.concatenate(
        [part.reshape(span, width) for part in (query_grad, key_grad, value_grad)], axis=1
    )
    qkv_grad, out_parts = tie(qkv_grad, out_parts)
    out_rows = jnp.concatenate([chips_last(part) for part in out_parts], axis=0)
    qkv_sum = dot(normed_1, qkv_grad, ((0,), (0,)))
    normed_grad_1 = col_sum(dot(qkv_grad, qkv, ((1,), (1,))), n_c)
    normed_grad_1, moved_gu, out_rows = tie(normed_grad_1, moved_gu, out_rows)
    gate_e, up_e = (place_e(value) for value in place_slices(moved_gu, 2))
    own_scale = lax.dynamic_slice_in_dim(first_scale, at_c * own_rows, own_rows, 0)
    rows_part, gain_1_sum = norm_back(normed_grad_1, own_inputs * own_scale, own_scale, gain_1)
    token_grad = rows_to_features((hidden_grad + rows_part).astype(BF16), n_c).astype(F32)

    result = rows_to_features((hidden + out_rows).astype(BF16), n_c)

    sums = jnp.stack([gain_1_sum, gain_2_sum, logit_sum]).reshape(3, n_row, d_own)
    sums = jnp.broadcast_to(sums.transpose(1, 0, 2)[:, None], (n_row, n_c, 3, d_own))
    sums = lax.all_to_all(sums.reshape(n_row * n_c, 3, d_own), ALL, 0, 0, tiled=True)
    sums = jnp.sum(sums, axis=0)

    out_w_grad = lax.psum_scatter(out_grad.astype(BF16), ROW, scatter_dimension=0, tiled=True)
    qkv_own = lax.psum_scatter(qkv_sum.astype(BF16), ROW, scatter_dimension=0, tiled=True)
    qkv_own = qkv_own.astype(F32)
    return (
        result,
        token_grad,
        sums[0],
        qkv_own[:, :width],
        qkv_own[:, width : 2 * width],
        qkv_own[:, 2 * width :],
        out_w_grad.T.astype(F32),
        sums[1],
        gate_s.T.astype(F32),
        up_s.T.astype(F32),
        down_s.astype(F32),
        sums[2],
        gate_e.transpose(2, 0, 1).astype(F32),
        up_e.transpose(2, 0, 1).astype(F32),
        down_e.astype(F32),
    )


def solution(mesh):
    n_row, n_col = mesh.shape["row"], mesh.shape["col"]
    inner = Mesh(mesh.devices.reshape(n_row // 2, 2, n_col // 2, 2), ALL)
    return jax.shard_map(
        shards,
        mesh=inner,
        in_specs=(
            P(None, ROW, COL),
            P(None, ROW, None),
            P(None, ROW, None),
            P(None, ROW),
            P(ROW),
            P(ROW, COL),
            P(ROW, COL),
            P(ROW, COL),
            P(COL, ROW),
            P(ROW),
            P(ROW, COL),
            P(ROW, COL),
            P(COL, ROW),
            P(ROW),
            P(ROW, COL, None),
            P(ROW, COL, None),
            P(COL, None, ROW),
            P(None, ROW, COL),
        ),
        out_specs=(
            P(None, ROW, COL),
            P(None, ROW, COL),
            P(ROW),
            P(ROW, COL),
            P(ROW, COL),
            P(ROW, COL),
            P(COL, ROW),
            P(ROW),
            P(ROW, COL),
            P(ROW, COL),
            P(COL, ROW),
            P(ROW),
            P(ROW, COL, None),
            P(ROW, COL, None),
            P(COL, None, ROW),
        ),
        check_vma=False,
    )
```

```python
import functools
import math

import jax
import jax.numpy as jnp
from jax import lax
from jax.experimental import pallas as pl
from jax.experimental.pallas import tpu as pltpu
from jax.sharding import Mesh, PartitionSpec as P

HEAD_DIM = 128
EXPERTS = 8
PROMPTS = 2
CONTS = 2
CONT_LEN = 64
PROMPT_LEN = 64

epsilon = 1e-06
rope_base = 1000000.0
masked_score = -1000000000.0

F32 = jnp.float32
BF16 = jnp.bfloat16
COL = ("y", "x")
ROW = ("g", "k")
ALL = ("g", "k", "y", "x")


def block_layout(groups, row_count):
    token_index = jnp.arange(row_count, dtype=jnp.int32)
    prompt_rows = PROMPTS * PROMPT_LEN
    is_prompt = token_index < prompt_rows
    cont_offset = jnp.maximum(token_index - prompt_rows, 0)
    cont_number = cont_offset // CONT_LEN
    segment = jnp.where(is_prompt, token_index // PROMPT_LEN, PROMPTS + cont_number)
    position = jnp.where(is_prompt, token_index % PROMPT_LEN, PROMPT_LEN + cont_offset % CONT_LEN)
    cont_picks = (cont_number[:, None] == jnp.arange(CONTS, dtype=jnp.int32)[None, :]).astype(
        jnp.int32
    )
    source = jnp.where(
        is_prompt[None], segment[None], jnp.sum(cont_picks[None] * groups[:, None, :], axis=2)
    )
    same_segment = (segment[:, None] == segment[None, :]) & (position[None, :] <= position[:, None])
    context = (
        jnp.logical_not(is_prompt)[None, :, None]
        & is_prompt[None, None, :]
        & (source[:, :, None] == segment[None, None, :])
    )
    return (same_segment[None] | context, position)


def rotary_tables(position):
    half_dim = HEAD_DIM // 2
    frequency = rope_base ** (-(2.0 * jnp.arange(half_dim, dtype=F32)) / HEAD_DIM)
    angles = position.astype(F32)[:, None] * frequency[None, :]
    cosine = jnp.cos(angles)
    sine = jnp.sin(angles)
    return (cosine[None, :, None, :], sine[None, :, None, :])


def rotate(values, cosine, sine):
    first, second = jnp.split(values, 2, axis=-1)
    return jnp.concatenate([first * cosine - second * sine, second * cosine + first * sine], -1)


def dot(left, right, dims):
    return lax.dot_general(left, right, (dims, ((), ())), preferred_element_type=F32)


PARTS = 2
EXTRA = 16


def ffn_kernel(sizes, groups, meta, rows_ref, cot_ref, side_ref, *refs):
    n_g, f_pad, f_one, d_own = sizes
    blocks = refs[: groups * 2 * n_g]
    sums = refs[groups * 2 * n_g : -8]
    out_ref, normed_ref, act_ref, gate_ref, up_ref, w_gu, w_down, sems = refs[-8:]
    g_at, k_at, c_at = meta[0], meta[1], meta[2]
    shared = groups == 1

    @pl.when(pl.program_id(0) == 0)
    def _():
        copies = []
        for half in range(2):
            for shift in range(n_g):
                at = half * n_g + shift
                column = 2 * (g_at ^ shift) + (k_at ^ half)
                lanes = pl.ds(pl.multiple_of(column * d_own, d_own), d_own)
                if shared:
                    both, down = blocks[at].at[: 2 * f_pad], blocks[at].at[2 * f_pad :]
                else:
                    both, down = blocks[at], blocks[2 * n_g + at]
                copies.append(
                    pltpu.make_async_copy(both, w_gu.at[: 2 * f_pad, lanes], sems.at[2 * at])
                )
                copies.append(pltpu.make_async_copy(down, w_down.at[:, lanes], sems.at[2 * at + 1]))
        for copy in copies:
            copy.start()
        if shared:
            w_gu[2 * f_pad :, :] = side_ref[...]
        for copy in copies:
            copy.wait()

    rows = rows_ref[...]
    count = rows.shape[0]
    n_c = cot_ref.shape[0]
    cot = jnp.concatenate(
        [
            jnp.concatenate([cot_ref[c ^ c_at, 0, row ^ c_at] for row in range(n_c)], axis=0)
            for c in range(n_c)
        ],
        axis=1,
    )
    minor = ((1,), (1,))
    pre = dot(w_gu[...], rows, minor)
    down_back = dot(w_down[...], cot, minor)
    gate_pre, up_pre = pre[:f_pad], pre[f_pad : 2 * f_pad]
    if shared:
        prob = jax.nn.sigmoid(pre[2 * f_pad : 2 * f_pad + 1])
        scale = jnp.broadcast_to(prob, (f_pad, count))
    else:
        full = f_pad // f_one
        pieces = [jnp.broadcast_to(side_ref[0, e : e + 1, :], (f_one, count)) for e in range(full)]
        if f_pad > full * f_one:
            pieces.append(jnp.zeros((f_pad - full * f_one, count), F32))
        scale = jnp.concatenate(pieces, axis=0)
    sigma = jax.nn.sigmoid(gate_pre)
    silu = gate_pre * sigma
    act = silu * up_pre
    act_grad = down_back * scale
    act_low = (act * scale).astype(BF16)
    gate_low = (act_grad * up_pre * sigma * (1.0 + gate_pre * (1.0 - sigma))).astype(BF16)
    up_low = (act_grad * silu).astype(BF16)
    act_ref[...] = act_low
    gate_ref[:f_pad, :] = gate_low
    up_ref[...] = up_low
    both = [gate_low, up_low]
    if shared:
        prob_part = jnp.sum(act * down_back, axis=0, keepdims=True)
        logit_part = prob_part * prob * (1.0 - prob)
        logit_high = logit_part.astype(BF16).astype(F32)
        logit_rows = jnp.concatenate(
            [logit_high, logit_part - logit_high, jnp.zeros((EXTRA - 2, count), F32)], axis=0
        ).astype(BF16)
        gate_ref[f_pad:, :] = logit_rows
        both.append(logit_rows)
    major = ((0,), (0,))
    out = dot(act_low, w_down[...], major)
    normed = dot(jnp.concatenate(both, axis=0), w_gu[...], major)
    if sums:
        out = out + sums[0][...].astype(F32)
        normed = normed + sums[1][...].astype(F32)
    out_ref[...] = out.astype(BF16)
    normed_ref[...] = normed.astype(BF16)


def ffn_pass(sizes, meta, rows, cot, side, blocks, sums):
    n_g, f_pad, _, d_own = sizes
    total, dim = rows.shape
    n_c, _, _, sub, cw = cot.shape
    tile = n_c * sub
    groups = len(blocks) // (2 * n_g)
    extra = EXTRA if groups == 1 else 0
    flat = lambda i, m: (i, 0)
    wide = lambda i, m: (0, i)
    if groups == 1:
        side_spec = pl.BlockSpec((EXTRA, dim), lambda i, m: (0, 0))
    else:
        side = side.reshape(-1, tile, 8).transpose(0, 2, 1)
        side_spec = pl.BlockSpec((1, 8, tile), lambda i, m: (i, 0, 0))
    return pl.pallas_call(
        functools.partial(ffn_kernel, sizes, groups),
        grid_spec=pltpu.PrefetchScalarGridSpec(
            num_scalar_prefetch=1,
            grid=(n_g,),
            in_specs=[
                pl.BlockSpec((tile, dim), flat),
                pl.BlockSpec((n_c, 1, n_c, sub, cw), lambda i, m: (0, i, 0, 0, 0)),
                side_spec,
            ]
            + [pl.BlockSpec(memory_space=pl.ANY)] * len(blocks)
            + [pl.BlockSpec((tile, dim), flat)] * len(sums),
            out_specs=[
                pl.BlockSpec((tile, dim), flat),
                pl.BlockSpec((tile, dim), flat),
                pl.BlockSpec((f_pad, tile), wide),
                pl.BlockSpec((f_pad + extra, tile), wide),
                pl.BlockSpec((f_pad, tile), wide),
            ],
            scratch_shapes=[
                pltpu.VMEM((2 * f_pad + extra, dim), BF16),
                pltpu.VMEM((f_pad, dim), BF16),
                pltpu.SemaphoreType.DMA((4 * n_g,)),
            ],
        ),
        out_shape=[
            jax.ShapeDtypeStruct((total, dim), BF16),
            jax.ShapeDtypeStruct((total, dim), BF16),
            jax.ShapeDtypeStruct((f_pad, total), BF16),
            jax.ShapeDtypeStruct((f_pad + extra, total), BF16),
            jax.ShapeDtypeStruct((f_pad, total), BF16),
        ],
        compiler_params=pltpu.CompilerParams(
            dimension_semantics=("arbitrary",), vmem_limit_bytes=60 * 1024 * 1024
        ),
        cost_estimate=pl.CostEstimate(
            flops=12 * total * dim * f_pad,
            bytes_accessed=(8 + 4 * len(sums)) * total * dim + 6 * total * f_pad + 6 * f_pad * dim,
            transcendentals=total * f_pad,
        ),
        name="ffn_pass",
    )(meta, rows, cot, side, *blocks, *sums)


def grad_kernel(parts, kinds, f_pad, meta, *refs):
    lefts, refs = refs[: parts * len(kinds)], refs[parts * len(kinds) :]
    values = {}
    for cot in sorted(set(kinds)):
        rights, refs = refs[:parts], refs[parts:]
        if cot:
            _, n_g, n_c, _, _ = rights[0].shape
            order = [(g, c) for g in range(n_g) for c in range(n_c)]
            values[cot] = [
                jnp.concatenate([right[0, g, c ^ meta[2]] for g, c in order], axis=0)
                for right in rights
            ]
        else:
            values[cot] = [right[...] for right in rights]
    for i, cot in enumerate(kinds):
        total = None
        for left, value in zip(lefts[i * parts : (i + 1) * parts], values[cot]):
            term = dot(left[...], value, ((1,), (0,)))
            total = term if total is None else total + term
        refs[0][0, 0, i * f_pad : (i + 1) * f_pad] = total[:f_pad].astype(BF16)
        if total.shape[0] > f_pad:
            refs[1][...] = jnp.broadcast_to(
                total[f_pad : f_pad + 1] + total[f_pad + 1 : f_pad + 2], refs[1].shape
            )


def weight_grad(sizes, meta, kinds, lefts, normed, cots):
    n_g, f_pad, _, d_own = sizes
    parts = len(normed)
    part_rows, dim = normed[0].shape
    extra = max(value[0].shape[0] for value in lefts) > f_pad
    n_c, _, _, sub, cw = cots[0].shape
    per = cw // d_own
    arrays, specs = [], []
    for values in lefts:
        arrays += values
        specs += [pl.BlockSpec(values[0].shape, lambda j, m: (0, 0))] * parts
    if False in kinds:
        arrays += normed
        specs += [pl.BlockSpec((part_rows, d_own), lambda j, m: (0, j))] * parts
    if True in kinds:
        arrays += cots
        specs += [
            pl.BlockSpec(
                (1, n_g, n_c, sub, d_own), lambda j, m: ((j // per) ^ m[2], 0, 0, 0, j % per)
            )
        ] * parts
    f_out = len(kinds) * f_pad
    out_specs = [
        pl.BlockSpec((1, 1, f_out, d_own), lambda j, m: ((j % 2) ^ m[1], (j // 2) ^ m[0], 0, 0))
    ]
    out_shape = [jax.ShapeDtypeStruct((2, n_g, f_out, d_own), BF16)]
    if extra:
        out_specs.append(pl.BlockSpec((8, d_own), lambda j, m: (0, j)))
        out_shape.append(jax.ShapeDtypeStruct((8, dim), F32))
    return pl.pallas_call(
        functools.partial(grad_kernel, parts, kinds, f_pad),
        grid_spec=pltpu.PrefetchScalarGridSpec(
            num_scalar_prefetch=1, grid=(2 * n_g,), in_specs=specs, out_specs=out_specs
        ),
        out_shape=out_shape,
        compiler_params=pltpu.CompilerParams(
            dimension_semantics=("arbitrary",), vmem_limit_bytes=56 * 1024 * 1024
        ),
        cost_estimate=pl.CostEstimate(
            flops=2 * parts * part_rows * dim * f_out,
            bytes_accessed=2 * parts * part_rows * (dim + f_out) + 2 * f_out * dim,
            transcendentals=0,
        ),
        name="weight_grad",
    )(meta, *arrays)


def tie(*values):
    return lax.optimization_barrier(values)


def norm_back(normed_grad, unit_rows, scale, gain):
    weighted = normed_grad * gain
    rows_grad = scale * (
        weighted - unit_rows * jnp.mean(weighted * unit_rows, axis=-1, keepdims=True)
    )
    return (rows_grad, jnp.sum(normed_grad * unit_rows, axis=0))


def swap(value, axis):
    return lax.ppermute(value, axis, [(0, 1), (1, 0)])


def shift_by(value, axis, shift):
    if shift == 0:
        return value
    return lax.ppermute(value, axis, [(i, i ^ shift) for i in range(lax.axis_size(axis))])


def gather_joined(value, axis, at):
    bit = lax.axis_size(axis) // 2
    while bit:
        shape = value.shape[:at] + (2 * value.shape[at],) + value.shape[at + 1 :]
        value = jnp.stack([value, shift_by(value, axis, bit)], axis=at + 1).reshape(shape)
        bit //= 2
    return value


def halve(value, axis, at, bit):
    size = value.shape[at]
    shape = value.shape[:at] + (size // 2, 2) + value.shape[at + 1 :]
    pair = value.reshape(shape)
    keep, send = (lax.index_in_dim(pair, i, at + 1, keepdims=False) for i in range(2))
    other = shift_by(send, axis, bit)
    return (keep.astype(F32) + other.astype(F32)).astype(BF16)


def col_gather(value, count):
    spread = jnp.broadcast_to(value[None], (count,) + value.shape)
    return lax.all_to_all(spread, COL, 0, 0, tiled=True)


def col_sum(partial, count):
    parts = partial.astype(BF16).reshape((count, -1) + partial.shape[1:])
    return jnp.sum(lax.all_to_all(parts, COL, 0, 0, tiled=True).astype(F32), axis=0)


def rows_to_features(rows, count):
    row_count, width = rows.shape
    parts = rows.reshape(row_count, count, width // count).transpose(1, 0, 2)
    moved = lax.all_to_all(parts, COL, 0, 0, tiled=True)
    blocks = moved.reshape(2, row_count * count // 2, width // count)
    return lax.all_to_all(blocks, "k", 0, 0, tiled=True)


def shards(
    tokens,
    routes,
    route_weights,
    group_ids,
    first_gain,
    query_weight,
    key_weight,
    value_weight,
    output_weight,
    second_gain,
    shared_gate,
    shared_up,
    shared_down,
    shared_logit,
    expert_gate,
    expert_up,
    expert_down,
    cotangent,
):
    n_g = lax.axis_size("g")
    n_c = lax.axis_size("y") * lax.axis_size("x")
    n_y, n_x = lax.axis_size("y"), lax.axis_size("x")
    n_row = 2 * n_g
    at_g, at_k = lax.axis_index("g"), lax.axis_index("k")
    at_c = lax.axis_index(COL)
    block = tokens.shape[1]
    dim = query_weight.shape[0] * n_row
    d_own = query_weight.shape[0]
    width = query_weight.shape[1]
    heads = width // HEAD_DIM
    local_experts = expert_gate.shape[1]
    span = 2 * block
    total = n_g * span
    own_rows = span // n_c
    pick = lambda array, index, axis=0: lax.dynamic_index_in_dim(array, index, axis, keepdims=False)

    labels = jnp.arange(EXPERTS, dtype=jnp.int32)
    mixing = jnp.sum(
        jnp.where(
            routes[:, None] == labels[None, :, None, None], route_weights[:, None], 0.0
        ),
        axis=-1,
    )
    small = jnp.concatenate(
        [
            mixing.reshape(2 * EXPERTS, block),
            jnp.zeros((8, block), F32)
            .at[0, :d_own].set(first_gain.astype(F32))
            .at[1, :d_own].set(second_gain.astype(F32))
            .at[2, :d_own].set(shared_logit.astype(F32))
            .at[3, : 2 * CONTS].set(group_ids.astype(F32).reshape(-1)),
        ],
        axis=0,
    )
    f_shared = shared_gate.shape[1] // n_g
    f_routed = expert_gate.shape[2] // n_g
    f_experts = local_experts * f_routed
    f_one, f_two = -(-f_shared // 16) * 16, -(-f_experts // 16) * 16
    sizes_s = (n_g, f_one, f_shared, d_own)
    sizes_e = (n_g, f_two, f_routed, d_own)
    meta = jnp.stack([at_g, at_k, at_c]).astype(jnp.int32)

    def fill(value, size):
        return jnp.pad(value, ((0, 0), (0, size - value.shape[1]), (0, 0)))

    def slices_s(value):
        return fill(value.reshape(n_g, f_shared, d_own), f_one)

    def slices_e(value):
        value = value.reshape(local_experts, n_g, f_routed, d_own).transpose(1, 0, 2, 3)
        return fill(value.reshape(n_g, f_experts, d_own), f_two)

    weight_slices = [
        jnp.concatenate([slices_s(w) for w in (shared_gate.T, shared_up.T, shared_down)], axis=1),
        jnp.concatenate([slices_e(w.transpose(1, 2, 0)) for w in (expert_gate, expert_up)], axis=1),
        slices_e(expert_down),
    ]
    picked = [[pick(value, at_g ^ shift) for shift in range(n_g)] for value in weight_slices]
    picked[0], tokens, cotangent = tie(picked[0], tokens, cotangent)
    own_blocks = [
        [shift_by(value, "g", shift) for shift, value in enumerate(values)] for values in picked
    ]

    token_part = lax.all_to_all(tokens, "k", 0, 0, tiled=True).reshape(span, -1)
    cot_part = lax.all_to_all(cotangent, "k", 0, 0, tiled=True).reshape(span, -1)

    sub = own_rows // PARTS
    cot_rows = cot_part.reshape(1, n_c, PARTS, sub, dim // n_c)
    cot_rows = gather_joined(cot_rows, "g", 0)
    qkv = lax.all_gather(
        jnp.concatenate([query_weight, key_weight, value_weight], axis=1), ROW, axis=0, tiled=True
    )
    out_w = lax.all_gather(output_weight, ROW, axis=1, tiled=True)
    inputs = col_gather(token_part, n_c).reshape(n_c, span, -1).transpose(1, 0, 2)
    inputs = inputs.reshape(span, dim).astype(F32)

    small, inputs = tie(small, inputs)
    small_all = lax.all_to_all(
        jnp.broadcast_to(small[None], (n_row,) + small.shape), ROW, 0, 0, tiled=True
    )
    gain_1 = small_all[:, 16, :d_own].reshape(dim)
    gain_2 = small_all[:, 17, :d_own].reshape(dim)
    logit_w = small_all[:, 18, :d_own].reshape(dim)
    groups_all = small_all[:, 19, : 2 * CONTS].reshape(n_g, 2, 2, CONTS)
    groups = pick(pick(groups_all, at_g), at_k, 1).astype(jnp.int32)
    mixing_all = small_all[:, : 2 * EXPERTS].reshape(n_row, 2, EXPERTS, block)
    mixing_own = lax.dynamic_slice_in_dim(
        pick(mixing_all, at_k, 1), at_c * local_experts, local_experts, 1
    )
    mixing_own = mixing_own.transpose(0, 2, 1).reshape(total, local_experts)

    own_blocks[0][1:], inputs, cot_rows = tie(own_blocks[0][1:], inputs, cot_rows)
    cot_all = []
    for part in range(PARTS):
        value = cot_rows[:, :, part][None, None]
        for axis in ("x", "y") if part % 2 else ("y", "x"):
            value = gather_joined(value, axis, ("y", "x").index(axis))
        cot_all.append(value.reshape(n_c, n_g, n_c, sub, dim // n_c))

    first_scale = lax.rsqrt(jnp.mean(inputs * inputs, axis=-1, keepdims=True) + epsilon)
    normed_1 = (inputs * first_scale * gain_1).astype(BF16)
    projected = dot(normed_1, qkv, ((1,), (0,)))
    allowed, position = block_layout(groups, block)
    cosine, sine = rotary_tables(position)
    head_shape = (2, block, heads, HEAD_DIM)
    query_rot = rotate(projected[:, :width].reshape(head_shape), cosine, sine).astype(BF16)
    key_rot = rotate(projected[:, width : 2 * width].reshape(head_shape), cosine, sine).astype(BF16)
    value_low = projected[:, 2 * width :].reshape(head_shape).astype(BF16)

    def einsum(form, left, right):
        return jnp.einsum(form, left, right, preferred_element_type=F32)

    scores = jnp.where(
        allowed[:, None],
        einsum("bqhd,bkhd->bhqk", query_rot, key_rot) * (1.0 / math.sqrt(HEAD_DIM)),
        masked_score,
    )
    peak = jnp.max(scores, axis=-1, keepdims=True)
    exp_scores = jnp.exp(scores - peak)
    probabilities = exp_scores / jnp.sum(exp_scores, axis=-1, keepdims=True)
    prob_low = probabilities.astype(BF16)
    mixed = einsum("bhqk,bkhd->bqhd", prob_low, value_low).astype(BF16).reshape(span, width)
    attention = col_sum(dot(mixed, out_w, ((1,), (0,))), n_c)

    own_inputs = lax.dynamic_slice_in_dim(inputs, at_c * own_rows, own_rows, 0)
    cot_all, attention = tie(cot_all, attention)
    hidden = own_inputs + attention
    second_scale = lax.rsqrt(jnp.mean(hidden * hidden, axis=-1, keepdims=True) + epsilon)
    unit_2 = hidden * second_scale
    normed_own = (unit_2 * gain_2).astype(BF16)

    def gather_cols(value):
        sides = []
        for side, order in enumerate((("y", "x"), ("x", "y"))):
            half = value[..., side * (dim // 2) : (side + 1) * (dim // 2)]
            for axis in order:
                half = gather_joined(half, axis, 1 + ("y", "x").index(axis))
            sides.append(half)
        return jnp.concatenate(sides, axis=-1).reshape(-1, dim)

    routed_gu, routed_d = own_blocks[1:]
    routed_gu[1], normed_own = tie(routed_gu[1], normed_own)
    halves = [normed_own[part * sub : (part + 1) * sub][None] for part in range(PARTS)]
    halves[0] = gather_joined(halves[0], "g", 0)
    halves[0], halves[1], routed_gu[2:3] = tie(halves[0], halves[1], routed_gu[2:3])
    halves[1] = gather_joined(halves[1], "g", 0)
    normed_parts = [gather_cols(halves[0][:, None, None])]
    normed_parts[0], halves[1], routed_gu[3:], routed_d[1] = tie(
        normed_parts[0], halves[1], routed_gu[3:], routed_d[1]
    )
    normed_parts.append(gather_cols(halves[1][:, None, None]))
    normed_parts[1], routed_d[2:3] = tie(normed_parts[1], routed_d[2:3])
    own_cot = [
        lax.dynamic_index_in_dim(cot[:, 0], at_c, 1, keepdims=False) for cot in cot_all
    ]
    own_cot = jnp.concatenate(own_cot, axis=1)
    own_cot = jnp.stack([pick(own_cot, at_c ^ c) for c in range(n_c)], axis=1)
    own_cot = own_cot.reshape(own_rows, dim)

    def own_core(grad):
        other = swap(grad[1], "k")
        return (grad[0].astype(F32) + other.astype(F32)).astype(BF16)

    def send_slices(both):
        return [shift_by(both[shift], "g", shift) for shift in range(n_g)]

    def place_slices(moved, kinds):
        moved = jnp.stack(moved)
        moved = jnp.stack([pick(moved, at_g ^ source) for source in range(n_g)])
        return [
            moved[:, i * (moved.shape[1] // kinds) :][:, : moved.shape[1] // kinds]
            for i in range(kinds)
        ]

    def place_s(value):
        return value[:, :f_shared].reshape(n_g * f_shared, d_own)

    def place_e(value):
        value = value[:, :f_experts].reshape(n_g, local_experts, f_routed, d_own)
        return value.transpose(1, 0, 2, 3).reshape(local_experts, n_g * f_routed, d_own)

    logit_low = jnp.zeros((EXTRA, dim), BF16).at[:2].set(logit_w.astype(BF16)[None])
    mixing_parts = mixing_own.reshape(n_g, n_c, PARTS, sub, local_experts)
    mixing_parts = jnp.stack([pick(mixing_parts, at_g ^ shift) for shift in range(n_g)])
    mixing_parts = jnp.stack([pick(mixing_parts, at_c ^ c, 1) for c in range(n_c)], axis=1)
    mixing_parts = jnp.pad(mixing_parts, ((0, 0),) * 4 + ((0, 8 - local_experts),))
    def blocks_of(values):
        return values + [swap(value, "k") for value in values]

    blocks_s = blocks_of(own_blocks[0])
    passes_s = [
        ffn_pass(sizes_s, meta, normed_parts[part], cot_all[part], logit_low, blocks_s, [])
        for part in range(PARTS)
    ]
    kinds = (False, False, True)
    grad_s, logit_sum = weight_grad(
        sizes_s, meta, kinds, [[p[i] for p in passes_s] for i in (3, 4, 2)], normed_parts, cot_all
    )
    logit_sum = logit_sum[0]
    sums = [[passes_s[part][0], passes_s[part][1]] for part in range(PARTS)]
    sums[0], grad_s = tie(sums[0], grad_s)
    blocks_e = blocks_of(own_blocks[1]) + blocks_of(own_blocks[2])
    passes = []
    for part in range(PARTS):
        if part == 1:
            both_s = own_core(grad_s)
            sums[1], both_s = tie(sums[1], both_s)
        passes.append(
            ffn_pass(
                sizes_e,
                meta,
                normed_parts[part],
                cot_all[part],
                mixing_parts[:, :, part].reshape(-1, 8),
                blocks_e,
                sums[part],
            )
        )
    moved_s = send_slices(both_s)

    def split_sides(partial):
        part = partial.reshape(n_g, n_y, n_x, sub, dim)
        return [part[..., : dim // 2], part[..., dim // 2 :]]

    def scatter_axis(value, axis, at):
        bit = 1
        while bit < lax.axis_size(axis):
            value = halve(value, axis, at, bit)
            bit *= 2
        return lax.index_in_dim(value, 0, at, keepdims=False)

    def cols_first(sides):
        return [scatter_axis(sides[0], "x", 2), scatter_axis(sides[1], "y", 1)]

    def cols_second(sides):
        sides = [scatter_axis(sides[0], "y", 1), scatter_axis(sides[1], "x", 1)]
        return jnp.concatenate(sides, axis=-1)

    def chips_steps(value):
        bit = 1
        while 2 * bit < n_g:
            value = halve(value, "g", 0, bit)
            bit *= 2
        return value

    def chips_last(value):
        other = shift_by(value[1], "g", n_g // 2)
        return value[0].astype(F32) + other.astype(F32)

    acts, gates, ups = ([parts[i] for parts in passes] for i in (2, 3, 4))
    first = cols_first(split_sides(passes[0][1]))
    first, acts, moved_s[1:3] = tie(first, acts, moved_s[1:3])
    (grad_d,) = weight_grad(sizes_e, meta, (True,), [acts], normed_parts, cot_all)
    first = cols_second(first)
    second = cols_first(split_sides(passes[1][1]))
    first, second, gates, grad_d = tie(first, second, gates, grad_d)
    (grad_gu,) = weight_grad(sizes_e, meta, (False, False), [gates, ups], normed_parts, cot_all)
    first = chips_steps(first)
    second = cols_second(second)
    both_d = own_core(grad_d)
    first, second, both_d, moved_s[3:], grad_gu = tie(first, second, both_d, moved_s[3:], grad_gu)
    moved_d = send_slices(both_d)
    first = chips_last(first)
    second = chips_steps(second)
    both_gu = own_core(grad_gu)
    first, second, both_gu = tie(first, second, both_gu)
    second = chips_last(second)
    out_sides = [cols_first(split_sides(parts[0])) for parts in passes]
    moved_gu = send_slices(both_gu)
    normed_grad_2 = jnp.concatenate([first, second], axis=0)
    normed_grad_2, moved_d[1:] = tie(normed_grad_2, moved_d[1:])
    hidden_part, gain_2_sum = norm_back(normed_grad_2, unit_2, second_scale, gain_2)
    hidden_grad = own_cot.astype(F32) + hidden_part
    attn_grad = col_gather(hidden_grad.astype(BF16), n_c).reshape(span, dim)
    out_sides, attn_grad, moved_gu[1] = tie(out_sides, attn_grad, moved_gu[1])
    out_parts = [cols_second(sides) for sides in out_sides]
    gate_s, up_s, down_s = (place_s(value) for value in place_slices(moved_s, 3))
    down_e = place_e(place_slices(moved_d, 1)[0])

    out_grad = dot(attn_grad, mixed, ((0,), (0,)))
    mixed_grad = dot(attn_grad, out_w, ((1,), (1,))).astype(BF16).reshape(head_shape)
    out_parts, mixed_grad, moved_gu[2:3] = tie(out_parts, mixed_grad, moved_gu[2:3])
    out_parts = [chips_steps(part) for part in out_parts]
    prob_grad = einsum("bqhd,bkhd->bhqk", mixed_grad, value_low)
    value_grad = einsum("bhqk,bqhd->bkhd", prob_low, mixed_grad).astype(BF16)
    center = jnp.sum(prob_grad * probabilities, axis=-1, keepdims=True)
    score_grad = (probabilities * (prob_grad - center) * (1.0 / math.sqrt(HEAD_DIM))).astype(BF16)
    out_parts, score_grad = tie(out_parts, score_grad)
    out_rows = [chips_last(part) for part in out_parts]
    query_grad = rotate(einsum("bhqk,bkhd->bqhd", score_grad, key_rot), cosine, -sine).astype(BF16)
    key_grad = rotate(einsum("bhqk,bqhd->bkhd", score_grad, query_rot), cosine, -sine).astype(BF16)
    qkv_grad = jnp.concatenate(
        [part.reshape(span, width) for part in (query_grad, key_grad, value_grad)], axis=1
    )
    qkv_grad, out_rows, moved_gu[3:] = tie(qkv_grad, out_rows, moved_gu[3:])
    out_rows = jnp.concatenate(out_rows, axis=0)
    qkv_sum = dot(normed_1, qkv_grad, ((0,), (0,)))
    normed_grad_1 = col_sum(dot(qkv_grad, qkv, ((1,), (1,))), n_c)
    gate_e, up_e = (place_e(value) for value in place_slices(moved_gu, 2))
    own_scale = lax.dynamic_slice_in_dim(first_scale, at_c * own_rows, own_rows, 0)
    rows_part, gain_1_sum = norm_back(normed_grad_1, own_inputs * own_scale, own_scale, gain_1)
    token_grad = rows_to_features((hidden_grad + rows_part).astype(BF16), n_c).astype(F32)

    result = rows_to_features((hidden + out_rows).astype(BF16), n_c)

    sums = jnp.stack([gain_1_sum, gain_2_sum, logit_sum]).reshape(3, n_row, d_own)
    sums = jnp.broadcast_to(sums.transpose(1, 0, 2)[:, None], (n_row, n_c, 3, d_own))
    sums = lax.all_to_all(sums.reshape(n_row * n_c, 3, d_own), ALL, 0, 0, tiled=True)
    sums = jnp.sum(sums, axis=0)

    out_w_grad = lax.psum_scatter(out_grad.astype(BF16), ROW, scatter_dimension=0, tiled=True)
    qkv_own = lax.psum_scatter(qkv_sum.astype(BF16), ROW, scatter_dimension=0, tiled=True)
    qkv_own = qkv_own.astype(F32)
    return (
        result,
        token_grad,
        sums[0],
        qkv_own[:, :width],
        qkv_own[:, width : 2 * width],
        qkv_own[:, 2 * width :],
        out_w_grad.T.astype(F32),
        sums[1],
        gate_s.T.astype(F32),
        up_s.T.astype(F32),
        down_s.astype(F32),
        sums[2],
        gate_e.transpose(2, 0, 1).astype(F32),
        up_e.transpose(2, 0, 1).astype(F32),
        down_e.astype(F32),
    )


def solution(mesh):
    n_row, n_col = mesh.shape["row"], mesh.shape["col"]
    inner = Mesh(mesh.devices.reshape(n_row // 2, 2, n_col // 2, 2), ALL)
    return jax.shard_map(
        shards,
        mesh=inner,
        in_specs=(
            P(None, ROW, COL),
            P(None, ROW, None),
            P(None, ROW, None),
            P(None, ROW),
            P(ROW),
            P(ROW, COL),
            P(ROW, COL),
            P(ROW, COL),
            P(COL, ROW),
            P(ROW),
            P(ROW, COL),
            P(ROW, COL),
            P(COL, ROW),
            P(ROW),
            P(ROW, COL, None),
            P(ROW, COL, None),
            P(COL, None, ROW),
            P(None, ROW, COL),
        ),
        out_specs=(
            P(None, ROW, COL),
            P(None, ROW, COL),
            P(ROW),
            P(ROW, COL),
            P(ROW, COL),
            P(ROW, COL),
            P(COL, ROW),
            P(ROW),
            P(ROW, COL),
            P(ROW, COL),
            P(COL, ROW),
            P(ROW),
            P(ROW, COL, None),
            P(ROW, COL, None),
            P(COL, None, ROW),
        ),
        check_vma=False,
    )
```

```python
import functools
import math

import jax
import jax.numpy as jnp
from jax import lax
from jax.experimental import pallas as pl
from jax.experimental.pallas import tpu as pltpu
from jax.sharding import Mesh, PartitionSpec as P

HEAD_DIM = 128
EXPERTS = 8
PROMPTS = 2
CONTS = 2
CONT_LEN = 64
PROMPT_LEN = 64

epsilon = 1e-06
rope_base = 1000000.0
masked_score = -1000000000.0

F32 = jnp.float32
BF16 = jnp.bfloat16
COL = ("y", "x")
ROW = ("g", "k")
ALL = ("g", "k", "y", "x")


def block_layout(groups, row_count):
    token_index = jnp.arange(row_count, dtype=jnp.int32)
    prompt_rows = PROMPTS * PROMPT_LEN
    is_prompt = token_index < prompt_rows
    cont_offset = jnp.maximum(token_index - prompt_rows, 0)
    cont_number = cont_offset // CONT_LEN
    segment = jnp.where(is_prompt, token_index // PROMPT_LEN, PROMPTS + cont_number)
    position = jnp.where(is_prompt, token_index % PROMPT_LEN, PROMPT_LEN + cont_offset % CONT_LEN)
    cont_picks = (cont_number[:, None] == jnp.arange(CONTS, dtype=jnp.int32)[None, :]).astype(
        jnp.int32
    )
    source = jnp.where(
        is_prompt[None], segment[None], jnp.sum(cont_picks[None] * groups[:, None, :], axis=2)
    )
    same_segment = (segment[:, None] == segment[None, :]) & (position[None, :] <= position[:, None])
    context = (
        jnp.logical_not(is_prompt)[None, :, None]
        & is_prompt[None, None, :]
        & (source[:, :, None] == segment[None, None, :])
    )
    return (same_segment[None] | context, position)


def rotary_tables(position):
    half_dim = HEAD_DIM // 2
    frequency = rope_base ** (-(2.0 * jnp.arange(half_dim, dtype=F32)) / HEAD_DIM)
    angles = position.astype(F32)[:, None] * frequency[None, :]
    cosine = jnp.cos(angles)
    sine = jnp.sin(angles)
    return (cosine[None, :, None, :], sine[None, :, None, :])


def rotate(values, cosine, sine):
    first, second = jnp.split(values, 2, axis=-1)
    return jnp.concatenate([first * cosine - second * sine, second * cosine + first * sine], -1)


def dot(left, right, dims):
    return lax.dot_general(left, right, (dims, ((), ())), preferred_element_type=F32)


PARTS = 2
EXTRA = 16


def ffn_kernel(sizes, groups, meta, rows_ref, cot_ref, side_ref, *refs):
    n_g, f_pad, f_one, d_own = sizes
    blocks = refs[: groups * 2 * n_g]
    sums = refs[groups * 2 * n_g : -8]
    out_ref, normed_ref, act_ref, gate_ref, up_ref, w_gu, w_down, sems = refs[-8:]
    g_at, k_at, c_at = meta[0], meta[1], meta[2]
    shared = groups == 1

    @pl.when(pl.program_id(0) == 0)
    def _():
        copies = []
        for half in range(2):
            for shift in range(n_g):
                at = half * n_g + shift
                column = 2 * (g_at ^ shift) + (k_at ^ half)
                lanes = pl.ds(pl.multiple_of(column * d_own, d_own), d_own)
                if shared:
                    both, down = blocks[at].at[: 2 * f_pad], blocks[at].at[2 * f_pad :]
                else:
                    both, down = blocks[at], blocks[2 * n_g + at]
                copies.append(
                    pltpu.make_async_copy(both, w_gu.at[: 2 * f_pad, lanes], sems.at[2 * at])
                )
                copies.append(pltpu.make_async_copy(down, w_down.at[:, lanes], sems.at[2 * at + 1]))
        for copy in copies:
            copy.start()
        if shared:
            w_gu[2 * f_pad :, :] = side_ref[...]
        for copy in copies:
            copy.wait()

    rows = rows_ref[...]
    count = rows.shape[0]
    n_c = cot_ref.shape[0]
    cot = jnp.concatenate(
        [
            jnp.concatenate([cot_ref[c ^ c_at, 0, row ^ c_at] for row in range(n_c)], axis=0)
            for c in range(n_c)
        ],
        axis=1,
    )
    minor = ((1,), (1,))
    pre = dot(w_gu[...], rows, minor)
    down_back = dot(w_down[...], cot, minor)
    gate_pre, up_pre = pre[:f_pad], pre[f_pad : 2 * f_pad]
    if shared:
        prob = jax.nn.sigmoid(pre[2 * f_pad : 2 * f_pad + 1])
        scale = jnp.broadcast_to(prob, (f_pad, count))
    else:
        full = f_pad // f_one
        pieces = [jnp.broadcast_to(side_ref[0, e : e + 1, :], (f_one, count)) for e in range(full)]
        if f_pad > full * f_one:
            pieces.append(jnp.zeros((f_pad - full * f_one, count), F32))
        scale = jnp.concatenate(pieces, axis=0)
    sigma = jax.nn.sigmoid(gate_pre)
    silu = gate_pre * sigma
    act = silu * up_pre
    act_grad = down_back * scale
    act_low = (act * scale).astype(BF16)
    gate_low = (act_grad * up_pre * sigma * (1.0 + gate_pre * (1.0 - sigma))).astype(BF16)
    up_low = (act_grad * silu).astype(BF16)
    act_ref[...] = act_low
    gate_ref[:f_pad, :] = gate_low
    up_ref[...] = up_low
    both = [gate_low, up_low]
    if shared:
        prob_part = jnp.sum(act * down_back, axis=0, keepdims=True)
        logit_part = prob_part * prob * (1.0 - prob)
        logit_high = logit_part.astype(BF16).astype(F32)
        logit_rows = jnp.concatenate(
            [logit_high, logit_part - logit_high, jnp.zeros((EXTRA - 2, count), F32)], axis=0
        ).astype(BF16)
        gate_ref[f_pad:, :] = logit_rows
        both.append(logit_rows)
    major = ((0,), (0,))
    out = dot(act_low, w_down[...], major)
    normed = dot(jnp.concatenate(both, axis=0), w_gu[...], major)
    if sums:
        out = out + sums[0][...].astype(F32)
        normed = normed + sums[1][...].astype(F32)
    out_ref[...] = out.astype(BF16)
    normed_ref[...] = normed.astype(BF16)


def ffn_pass(sizes, meta, rows, cot, side, blocks, sums):
    n_g, f_pad, _, d_own = sizes
    total, dim = rows.shape
    n_c, _, _, sub, cw = cot.shape
    tile = n_c * sub
    groups = len(blocks) // (2 * n_g)
    extra = EXTRA if groups == 1 else 0
    flat = lambda i, m: (i, 0)
    wide = lambda i, m: (0, i)
    if groups == 1:
        side_spec = pl.BlockSpec((EXTRA, dim), lambda i, m: (0, 0))
    else:
        side = side.reshape(-1, tile, 8).transpose(0, 2, 1)
        side_spec = pl.BlockSpec((1, 8, tile), lambda i, m: (i, 0, 0))
    return pl.pallas_call(
        functools.partial(ffn_kernel, sizes, groups),
        grid_spec=pltpu.PrefetchScalarGridSpec(
            num_scalar_prefetch=1,
            grid=(n_g,),
            in_specs=[
                pl.BlockSpec((tile, dim), flat),
                pl.BlockSpec((n_c, 1, n_c, sub, cw), lambda i, m: (0, i, 0, 0, 0)),
                side_spec,
            ]
            + [pl.BlockSpec(memory_space=pl.ANY)] * len(blocks)
            + [pl.BlockSpec((tile, dim), flat)] * len(sums),
            out_specs=[
                pl.BlockSpec((tile, dim), flat),
                pl.BlockSpec((tile, dim), flat),
                pl.BlockSpec((f_pad, tile), wide),
                pl.BlockSpec((f_pad + extra, tile), wide),
                pl.BlockSpec((f_pad, tile), wide),
            ],
            scratch_shapes=[
                pltpu.VMEM((2 * f_pad + extra, dim), BF16),
                pltpu.VMEM((f_pad, dim), BF16),
                pltpu.SemaphoreType.DMA((4 * n_g,)),
            ],
        ),
        out_shape=[
            jax.ShapeDtypeStruct((total, dim), BF16),
            jax.ShapeDtypeStruct((total, dim), BF16),
            jax.ShapeDtypeStruct((f_pad, total), BF16),
            jax.ShapeDtypeStruct((f_pad + extra, total), BF16),
            jax.ShapeDtypeStruct((f_pad, total), BF16),
        ],
        compiler_params=pltpu.CompilerParams(
            dimension_semantics=("arbitrary",), vmem_limit_bytes=60 * 1024 * 1024
        ),
        cost_estimate=pl.CostEstimate(
            flops=12 * total * dim * f_pad,
            bytes_accessed=(8 + 4 * len(sums)) * total * dim + 6 * total * f_pad + 6 * f_pad * dim,
            transcendentals=total * f_pad,
        ),
        name="ffn_pass",
    )(meta, rows, cot, side, *blocks, *sums)


def grad_kernel(parts, kinds, f_pad, meta, *refs):
    lefts, refs = refs[: parts * len(kinds)], refs[parts * len(kinds) :]
    values = {}
    for cot in sorted(set(kinds)):
        rights, refs = refs[:parts], refs[parts:]
        if cot:
            _, n_g, n_c, _, _ = rights[0].shape
            order = [(g, c) for g in range(n_g) for c in range(n_c)]
            values[cot] = [
                jnp.concatenate([right[0, g, c ^ meta[2]] for g, c in order], axis=0)
                for right in rights
            ]
        else:
            values[cot] = [right[...] for right in rights]
    for i, cot in enumerate(kinds):
        total = None
        for left, value in zip(lefts[i * parts : (i + 1) * parts], values[cot]):
            term = dot(left[...], value, ((1,), (0,)))
            total = term if total is None else total + term
        refs[0][0, 0, i * f_pad : (i + 1) * f_pad] = total[:f_pad].astype(BF16)
        if total.shape[0] > f_pad:
            refs[1][...] = jnp.broadcast_to(
                total[f_pad : f_pad + 1] + total[f_pad + 1 : f_pad + 2], refs[1].shape
            )


def weight_grad(sizes, meta, kinds, lefts, normed, cots):
    n_g, f_pad, _, d_own = sizes
    parts = len(normed)
    part_rows, dim = normed[0].shape
    extra = max(value[0].shape[0] for value in lefts) > f_pad
    n_c, _, _, sub, cw = cots[0].shape
    per = cw // d_own
    arrays, specs = [], []
    for values in lefts:
        arrays += values
        specs += [pl.BlockSpec(values[0].shape, lambda j, m: (0, 0))] * parts
    if False in kinds:
        arrays += normed
        specs += [pl.BlockSpec((part_rows, d_own), lambda j, m: (0, j))] * parts
    if True in kinds:
        arrays += cots
        specs += [
            pl.BlockSpec(
                (1, n_g, n_c, sub, d_own), lambda j, m: ((j // per) ^ m[2], 0, 0, 0, j % per)
            )
        ] * parts
    f_out = len(kinds) * f_pad
    out_specs = [
        pl.BlockSpec((1, 1, f_out, d_own), lambda j, m: ((j % 2) ^ m[1], (j // 2) ^ m[0], 0, 0))
    ]
    out_shape = [jax.ShapeDtypeStruct((2, n_g, f_out, d_own), BF16)]
    if extra:
        out_specs.append(pl.BlockSpec((8, d_own), lambda j, m: (0, j)))
        out_shape.append(jax.ShapeDtypeStruct((8, dim), F32))
    return pl.pallas_call(
        functools.partial(grad_kernel, parts, kinds, f_pad),
        grid_spec=pltpu.PrefetchScalarGridSpec(
            num_scalar_prefetch=1, grid=(2 * n_g,), in_specs=specs, out_specs=out_specs
        ),
        out_shape=out_shape,
        compiler_params=pltpu.CompilerParams(
            dimension_semantics=("arbitrary",), vmem_limit_bytes=56 * 1024 * 1024
        ),
        cost_estimate=pl.CostEstimate(
            flops=2 * parts * part_rows * dim * f_out,
            bytes_accessed=2 * parts * part_rows * (dim + f_out) + 2 * f_out * dim,
            transcendentals=0,
        ),
        name="weight_grad",
    )(meta, *arrays)


def tie(*values):
    return lax.optimization_barrier(values)


def norm_back(normed_grad, unit_rows, scale, gain):
    weighted = normed_grad * gain
    rows_grad = scale * (
        weighted - unit_rows * jnp.mean(weighted * unit_rows, axis=-1, keepdims=True)
    )
    return (rows_grad, jnp.sum(normed_grad * unit_rows, axis=0))


def swap(value, axis):
    return lax.ppermute(value, axis, [(0, 1), (1, 0)])


def shift_by(value, axis, shift):
    if shift == 0:
        return value
    return lax.ppermute(value, axis, [(i, i ^ shift) for i in range(lax.axis_size(axis))])


def gather_joined(value, axis, at):
    bit = lax.axis_size(axis) // 2
    while bit:
        shape = value.shape[:at] + (2 * value.shape[at],) + value.shape[at + 1 :]
        value = jnp.stack([value, shift_by(value, axis, bit)], axis=at + 1).reshape(shape)
        bit //= 2
    return value


def halve(value, axis, at, bit, after=None):
    size = value.shape[at]
    shape = value.shape[:at] + (size // 2, 2) + value.shape[at + 1 :]
    pair = value.reshape(shape)
    keep, send = (lax.index_in_dim(pair, i, at + 1, keepdims=False) for i in range(2))
    other = shift_by(send, axis, bit)
    if after is not None:
        keep, _ = tie(keep, after)
    return (keep.astype(F32) + other.astype(F32)).astype(BF16)


def col_gather(value, count):
    spread = jnp.broadcast_to(value[None], (count,) + value.shape)
    return lax.all_to_all(spread, COL, 0, 0, tiled=True)


def col_sum(partial, count):
    parts = partial.astype(BF16).reshape((count, -1) + partial.shape[1:])
    return jnp.sum(lax.all_to_all(parts, COL, 0, 0, tiled=True).astype(F32), axis=0)


def rows_to_features(rows, count):
    row_count, width = rows.shape
    parts = rows.reshape(row_count, count, width // count).transpose(1, 0, 2)
    moved = lax.all_to_all(parts, COL, 0, 0, tiled=True)
    blocks = moved.reshape(2, row_count * count // 2, width // count)
    return lax.all_to_all(blocks, "k", 0, 0, tiled=True)


def shards(
    tokens,
    routes,
    route_weights,
    group_ids,
    first_gain,
    query_weight,
    key_weight,
    value_weight,
    output_weight,
    second_gain,
    shared_gate,
    shared_up,
    shared_down,
    shared_logit,
    expert_gate,
    expert_up,
    expert_down,
    cotangent,
):
    n_g = lax.axis_size("g")
    n_c = lax.axis_size("y") * lax.axis_size("x")
    n_y, n_x = lax.axis_size("y"), lax.axis_size("x")
    n_row = 2 * n_g
    at_g, at_k = lax.axis_index("g"), lax.axis_index("k")
    at_c = lax.axis_index(COL)
    block = tokens.shape[1]
    dim = query_weight.shape[0] * n_row
    d_own = query_weight.shape[0]
    width = query_weight.shape[1]
    heads = width // HEAD_DIM
    local_experts = expert_gate.shape[1]
    span = 2 * block
    total = n_g * span
    own_rows = span // n_c
    pick = lambda array, index, axis=0: lax.dynamic_index_in_dim(array, index, axis, keepdims=False)

    labels = jnp.arange(EXPERTS, dtype=jnp.int32)
    mixing = jnp.sum(
        jnp.where(
            routes[:, None] == labels[None, :, None, None], route_weights[:, None], 0.0
        ),
        axis=-1,
    )
    small = jnp.concatenate(
        [
            mixing.reshape(2 * EXPERTS, block),
            jnp.zeros((8, block), F32)
            .at[0, :d_own].set(first_gain.astype(F32))
            .at[1, :d_own].set(second_gain.astype(F32))
            .at[2, :d_own].set(shared_logit.astype(F32))
            .at[3, : 2 * CONTS].set(group_ids.astype(F32).reshape(-1)),
        ],
        axis=0,
    )
    small_all = lax.all_to_all(
        jnp.broadcast_to(small[None], (n_row,) + small.shape), ROW, 0, 0, tiled=True
    )
    f_shared = shared_gate.shape[1] // n_g
    f_routed = expert_gate.shape[2] // n_g
    f_experts = local_experts * f_routed
    f_one, f_two = -(-f_shared // 16) * 16, -(-f_experts // 16) * 16
    sizes_s = (n_g, f_one, f_shared, d_own)
    sizes_e = (n_g, f_two, f_routed, d_own)
    meta = jnp.stack([at_g, at_k, at_c]).astype(jnp.int32)

    def fill(value, size):
        return jnp.pad(value, ((0, 0), (0, size - value.shape[1]), (0, 0)))

    def slices_s(value):
        return fill(value.reshape(n_g, f_shared, d_own), f_one)

    def slices_e(value):
        value = value.reshape(local_experts, n_g, f_routed, d_own).transpose(1, 0, 2, 3)
        return fill(value.reshape(n_g, f_experts, d_own), f_two)

    weight_slices = [
        jnp.concatenate([slices_s(w) for w in (shared_gate.T, shared_up.T, shared_down)], axis=1),
        jnp.concatenate([slices_e(w.transpose(1, 2, 0)) for w in (expert_gate, expert_up)], axis=1),
        slices_e(expert_down),
    ]
    picked = [[pick(value, at_g ^ shift) for shift in range(n_g)] for value in weight_slices]
    qkv = lax.all_gather(
        jnp.concatenate([query_weight, key_weight, value_weight], axis=1), ROW, axis=0, tiled=True
    )
    out_w = lax.all_gather(output_weight, ROW, axis=1, tiled=True)
    picked[0], qkv, small_all = tie(picked[0], qkv, small_all)
    own_blocks = [
        [shift_by(value, "g", shift) for shift, value in enumerate(values)] for values in picked
    ]

    token_part = lax.all_to_all(tokens, "k", 0, 0, tiled=True).reshape(span, -1)
    cot_part = lax.all_to_all(cotangent, "k", 0, 0, tiled=True).reshape(span, -1)

    sub = own_rows // PARTS
    cot_rows = cot_part.reshape(1, n_c, PARTS, sub, dim // n_c)
    cot_rows, qkv = tie(cot_rows, qkv)
    cot_rows = gather_joined(cot_rows, "g", 0)
    inputs = col_gather(token_part, n_c).reshape(n_c, span, -1).transpose(1, 0, 2)
    inputs = inputs.reshape(span, dim).astype(F32)

    gain_1 = small_all[:, 16, :d_own].reshape(dim)
    gain_2 = small_all[:, 17, :d_own].reshape(dim)
    logit_w = small_all[:, 18, :d_own].reshape(dim)
    groups_all = small_all[:, 19, : 2 * CONTS].reshape(n_g, 2, 2, CONTS)
    groups = pick(pick(groups_all, at_g), at_k, 1).astype(jnp.int32)
    mixing_all = small_all[:, : 2 * EXPERTS].reshape(n_row, 2, EXPERTS, block)
    mixing_own = lax.dynamic_slice_in_dim(
        pick(mixing_all, at_k, 1), at_c * local_experts, local_experts, 1
    )
    mixing_own = mixing_own.transpose(0, 2, 1).reshape(total, local_experts)

    first_scale = lax.rsqrt(jnp.mean(inputs * inputs, axis=-1, keepdims=True) + epsilon)
    normed_1 = (inputs * first_scale * gain_1).astype(BF16)
    projected = dot(normed_1, qkv, ((1,), (0,)))
    allowed, position = block_layout(groups, block)
    cosine, sine = rotary_tables(position)
    head_shape = (2, block, heads, HEAD_DIM)
    query_rot = rotate(projected[:, :width].reshape(head_shape), cosine, sine).astype(BF16)
    key_rot = rotate(projected[:, width : 2 * width].reshape(head_shape), cosine, sine).astype(BF16)
    value_low = projected[:, 2 * width :].reshape(head_shape).astype(BF16)

    def einsum(form, left, right):
        return jnp.einsum(form, left, right, preferred_element_type=F32)

    scores = jnp.where(
        allowed[:, None],
        einsum("bqhd,bkhd->bhqk", query_rot, key_rot) * (1.0 / math.sqrt(HEAD_DIM)),
        masked_score,
    )
    peak = jnp.max(scores, axis=-1, keepdims=True)
    exp_scores = jnp.exp(scores - peak)
    probabilities = exp_scores / jnp.sum(exp_scores, axis=-1, keepdims=True)
    prob_low = probabilities.astype(BF16)
    mixed = einsum("bhqk,bkhd->bqhd", prob_low, value_low).astype(BF16).reshape(span, width)
    cot_rows, mixed, own_blocks[0][1] = tie(cot_rows, mixed, own_blocks[0][1])
    cot_all = []
    for part in range(PARTS):
        value = cot_rows[:, :, part][None, None]
        for axis in ("x", "y") if part % 2 else ("y", "x"):
            value = gather_joined(value, axis, ("y", "x").index(axis))
        cot_all.append(value.reshape(n_c, n_g, n_c, sub, dim // n_c))
    attention = col_sum(dot(mixed, out_w, ((1,), (0,))), n_c)

    own_inputs = lax.dynamic_slice_in_dim(inputs, at_c * own_rows, own_rows, 0)
    own_blocks[0][2:], attention = tie(own_blocks[0][2:], attention)
    hidden = own_inputs + attention
    second_scale = lax.rsqrt(jnp.mean(hidden * hidden, axis=-1, keepdims=True) + epsilon)
    unit_2 = hidden * second_scale
    normed_own = (unit_2 * gain_2).astype(BF16)

    def gather_cols(value):
        sides = []
        for side, order in enumerate((("y", "x"), ("x", "y"))):
            half = value[..., side * (dim // 2) : (side + 1) * (dim // 2)]
            for axis in order:
                half = gather_joined(half, axis, 1 + ("y", "x").index(axis))
            sides.append(half)
        return jnp.concatenate(sides, axis=-1).reshape(-1, dim)

    routed_gu, routed_d = own_blocks[1:]
    halves = [normed_own[part * sub : (part + 1) * sub][None] for part in range(PARTS)]
    halves[0] = gather_joined(halves[0], "g", 0)
    halves[0], halves[1], routed_gu[1] = tie(halves[0], halves[1], routed_gu[1])
    halves[1] = gather_joined(halves[1], "g", 0)
    normed_parts = [gather_cols(halves[0][:, None, None])]
    normed_parts[0], halves[1], routed_gu[2:3], cot_all = tie(
        normed_parts[0], halves[1], routed_gu[2:3], cot_all
    )
    normed_parts.append(gather_cols(halves[1][:, None, None]))
    normed_parts[1], routed_gu[3:], routed_d[1] = tie(
        normed_parts[1], routed_gu[3:], routed_d[1]
    )
    own_cot = [
        lax.dynamic_index_in_dim(cot[:, 0], at_c, 1, keepdims=False) for cot in cot_all
    ]
    own_cot = jnp.concatenate(own_cot, axis=1)
    own_cot = jnp.stack([pick(own_cot, at_c ^ c) for c in range(n_c)], axis=1)
    own_cot = own_cot.reshape(own_rows, dim)

    def own_core(grad, after=None):
        other = swap(grad[1], "k")
        grad = grad[0]
        if after is not None:
            grad, _ = tie(grad, after)
        return (grad.astype(F32) + other.astype(F32)).astype(BF16)

    def send_slices(both):
        return [shift_by(both[shift], "g", shift) for shift in range(n_g)]

    def place_slices(moved, kinds):
        moved = jnp.stack(moved)
        moved = jnp.stack([pick(moved, at_g ^ source) for source in range(n_g)])
        return [
            moved[:, i * (moved.shape[1] // kinds) :][:, : moved.shape[1] // kinds]
            for i in range(kinds)
        ]

    def place_s(value):
        return value[:, :f_shared].reshape(n_g * f_shared, d_own)

    def place_e(value):
        value = value[:, :f_experts].reshape(n_g, local_experts, f_routed, d_own)
        return value.transpose(1, 0, 2, 3).reshape(local_experts, n_g * f_routed, d_own)

    logit_low = jnp.zeros((EXTRA, dim), BF16).at[:2].set(logit_w.astype(BF16)[None])
    mixing_parts = mixing_own.reshape(n_g, n_c, PARTS, sub, local_experts)
    mixing_parts = jnp.stack([pick(mixing_parts, at_g ^ shift) for shift in range(n_g)])
    mixing_parts = jnp.stack([pick(mixing_parts, at_c ^ c, 1) for c in range(n_c)], axis=1)
    mixing_parts = jnp.pad(mixing_parts, ((0, 0),) * 4 + ((0, 8 - local_experts),))
    def blocks_of(values):
        return values + [swap(value, "k") for value in values]

    blocks_s = blocks_of(own_blocks[0])
    passes_s = [
        ffn_pass(sizes_s, meta, normed_parts[part], cot_all[part], logit_low, blocks_s, [])
        for part in range(PARTS)
    ]
    kinds = (False, False, True)
    grad_s, logit_sum = weight_grad(
        sizes_s, meta, kinds, [[p[i] for p in passes_s] for i in (3, 4, 2)], normed_parts, cot_all
    )
    logit_sum = logit_sum[0]
    sums = [[passes_s[part][0], passes_s[part][1]] for part in range(PARTS)]
    sums[0], grad_s = tie(sums[0], grad_s)
    blocks_e = blocks_of(own_blocks[1]) + blocks_of(own_blocks[2])
    passes = []
    for part in range(PARTS):
        if part == 1:
            both_s = own_core(grad_s, passes[0][2][:16, :128])
            sums[1], both_s = tie(sums[1], both_s)
        passes.append(
            ffn_pass(
                sizes_e,
                meta,
                normed_parts[part],
                cot_all[part],
                mixing_parts[:, :, part].reshape(-1, 8),
                blocks_e,
                sums[part],
            )
        )
    moved_s = send_slices(both_s)

    def split_sides(partial):
        part = partial.reshape(n_g, n_y, n_x, sub, dim)
        return [part[..., : dim // 2], part[..., dim // 2 :]]

    def scatter_axis(value, axis, at, after=None):
        bit = 1
        while bit < lax.axis_size(axis):
            value = halve(value, axis, at, bit, after)
            bit *= 2
        return lax.index_in_dim(value, 0, at, keepdims=False)

    def cols_first(sides, after=None):
        return [scatter_axis(sides[0], "x", 2, after), scatter_axis(sides[1], "y", 1, after)]

    def cols_second(sides):
        sides = [scatter_axis(sides[0], "y", 1), scatter_axis(sides[1], "x", 1)]
        return jnp.concatenate(sides, axis=-1)

    def chips_steps(value):
        bit = 1
        while 2 * bit < n_g:
            value = halve(value, "g", 0, bit)
            bit *= 2
        return value

    def chips_last(value):
        other = shift_by(value[1], "g", n_g // 2)
        return value[0].astype(F32) + other.astype(F32)

    acts, gates, ups = ([parts[i] for parts in passes] for i in (2, 3, 4))
    first = cols_first(split_sides(passes[0][1]), passes[1][2][:16, :128])
    first, acts, moved_s[1:3] = tie(first, acts, moved_s[1:3])
    (grad_d,) = weight_grad(sizes_e, meta, (True,), [acts], normed_parts, cot_all)
    first = cols_second(first)
    second = cols_first(split_sides(passes[1][1]))
    first, second, gates, grad_d = tie(first, second, gates, grad_d)
    (grad_gu,) = weight_grad(sizes_e, meta, (False, False), [gates, ups], normed_parts, cot_all)
    first = chips_steps(first)
    second = cols_second(second)
    both_d = own_core(grad_d)
    first, second, both_d, moved_s[3:], grad_gu = tie(first, second, both_d, moved_s[3:], grad_gu)
    moved_d = send_slices(both_d)
    first = chips_last(first)
    second = chips_steps(second)
    both_gu = own_core(grad_gu)
    first, second, both_gu = tie(first, second, both_gu)
    second = chips_last(second)
    out_sides = [cols_first(split_sides(parts[0])) for parts in passes]
    moved_gu = send_slices(both_gu)
    normed_grad_2 = jnp.concatenate([first, second], axis=0)
    normed_grad_2, moved_d[1] = tie(normed_grad_2, moved_d[1])
    hidden_part, gain_2_sum = norm_back(normed_grad_2, unit_2, second_scale, gain_2)
    hidden_grad = own_cot.astype(F32) + hidden_part
    attn_grad = col_gather(hidden_grad.astype(BF16), n_c).reshape(span, dim)
    attn_grad, moved_d[2:], moved_gu[1] = tie(attn_grad, moved_d[2:], moved_gu[1])
    gate_s, up_s, down_s = (place_s(value) for value in place_slices(moved_s, 3))
    down_e = place_e(place_slices(moved_d, 1)[0])

    out_grad = dot(attn_grad, mixed, ((0,), (0,)))
    mixed_grad = dot(attn_grad, out_w, ((1,), (1,))).astype(BF16).reshape(head_shape)
    out_sides, mixed_grad = tie(out_sides, mixed_grad)
    out_parts = [cols_second(sides) for sides in out_sides]
    prob_grad = einsum("bqhd,bkhd->bhqk", mixed_grad, value_low)
    value_grad = einsum("bhqk,bqhd->bkhd", prob_low, mixed_grad).astype(BF16)
    center = jnp.sum(prob_grad * probabilities, axis=-1, keepdims=True)
    score_grad = (probabilities * (prob_grad - center) * (1.0 / math.sqrt(HEAD_DIM))).astype(BF16)
    out_parts, score_grad, moved_gu[2:3] = tie(out_parts, score_grad, moved_gu[2:3])
    out_parts = [chips_steps(part) for part in out_parts]
    query_grad = rotate(einsum("bhqk,bkhd->bqhd", score_grad, key_rot), cosine, -sine).astype(BF16)
    key_grad = rotate(einsum("bhqk,bqhd->bkhd", score_grad, query_rot), cosine, -sine).astype(BF16)
    qkv_grad = jnp.concatenate(
        [part.reshape(span, width) for part in (query_grad, key_grad, value_grad)], axis=1
    )
    qkv_grad, out_parts = tie(qkv_grad, out_parts)
    out_rows = jnp.concatenate([chips_last(part) for part in out_parts], axis=0)
    qkv_sum = dot(normed_1, qkv_grad, ((0,), (0,)))
    normed_grad_1 = col_sum(dot(qkv_grad, qkv, ((1,), (1,))), n_c)
    normed_grad_1, out_rows, moved_gu[3:] = tie(normed_grad_1, out_rows, moved_gu[3:])
    gate_e, up_e = (place_e(value) for value in place_slices(moved_gu, 2))
    own_scale = lax.dynamic_slice_in_dim(first_scale, at_c * own_rows, own_rows, 0)
    rows_part, gain_1_sum = norm_back(normed_grad_1, own_inputs * own_scale, own_scale, gain_1)
    token_grad = rows_to_features((hidden_grad + rows_part).astype(BF16), n_c).astype(F32)

    result = rows_to_features((hidden + out_rows).astype(BF16), n_c)

    sums = jnp.stack([gain_1_sum, gain_2_sum, logit_sum]).reshape(3, n_row, d_own)
    sums = jnp.broadcast_to(sums.transpose(1, 0, 2)[:, None], (n_row, n_c, 3, d_own))
    sums = lax.all_to_all(sums.reshape(n_row * n_c, 3, d_own), ALL, 0, 0, tiled=True)
    sums = jnp.sum(sums, axis=0)

    out_w_grad = lax.psum_scatter(out_grad.astype(BF16), ROW, scatter_dimension=0, tiled=True)
    qkv_own = lax.psum_scatter(qkv_sum.astype(BF16), ROW, scatter_dimension=0, tiled=True)
    qkv_own = qkv_own.astype(F32)
    return (
        result,
        token_grad,
        sums[0],
        qkv_own[:, :width],
        qkv_own[:, width : 2 * width],
        qkv_own[:, 2 * width :],
        out_w_grad.T.astype(F32),
        sums[1],
        gate_s.T.astype(F32),
        up_s.T.astype(F32),
        down_s.astype(F32),
        sums[2],
        gate_e.transpose(2, 0, 1).astype(F32),
        up_e.transpose(2, 0, 1).astype(F32),
        down_e.astype(F32),
    )


def solution(mesh):
    n_row, n_col = mesh.shape["row"], mesh.shape["col"]
    inner = Mesh(mesh.devices.reshape(n_row // 2, 2, n_col // 2, 2), ALL)
    return jax.shard_map(
        shards,
        mesh=inner,
        in_specs=(
            P(None, ROW, COL),
            P(None, ROW, None),
            P(None, ROW, None),
            P(None, ROW),
            P(ROW),
            P(ROW, COL),
            P(ROW, COL),
            P(ROW, COL),
            P(COL, ROW),
            P(ROW),
            P(ROW, COL),
            P(ROW, COL),
            P(COL, ROW),
            P(ROW),
            P(ROW, COL, None),
            P(ROW, COL, None),
            P(COL, None, ROW),
            P(None, ROW, COL),
        ),
        out_specs=(
            P(None, ROW, COL),
            P(None, ROW, COL),
            P(ROW),
            P(ROW, COL),
            P(ROW, COL),
            P(ROW, COL),
            P(COL, ROW),
            P(ROW),
            P(ROW, COL),
            P(ROW, COL),
            P(COL, ROW),
            P(ROW),
            P(ROW, COL, None),
            P(ROW, COL, None),
            P(COL, None, ROW),
        ),
        check_vma=False,
    )
```

```python
import functools
import math

import jax
import jax.numpy as jnp
from jax import lax
from jax.experimental import pallas as pl
from jax.experimental.pallas import tpu as pltpu
from jax.sharding import Mesh, PartitionSpec as P

HEAD_DIM = 128
EXPERTS = 8
PROMPTS = 2
CONTS = 2
CONT_LEN = 64
PROMPT_LEN = 64

epsilon = 1e-06
rope_base = 1000000.0
masked_score = -1000000000.0

F32 = jnp.float32
BF16 = jnp.bfloat16
COL = ("y", "x")
ROW = ("g", "k")
ALL = ("g", "k", "y", "x")


def block_layout(groups, row_count):
    token_index = jnp.arange(row_count, dtype=jnp.int32)
    prompt_rows = PROMPTS * PROMPT_LEN
    is_prompt = token_index < prompt_rows
    cont_offset = jnp.maximum(token_index - prompt_rows, 0)
    cont_number = cont_offset // CONT_LEN
    segment = jnp.where(is_prompt, token_index // PROMPT_LEN, PROMPTS + cont_number)
    position = jnp.where(is_prompt, token_index % PROMPT_LEN, PROMPT_LEN + cont_offset % CONT_LEN)
    cont_picks = (cont_number[:, None] == jnp.arange(CONTS, dtype=jnp.int32)[None, :]).astype(
        jnp.int32
    )
    source = jnp.where(
        is_prompt[None], segment[None], jnp.sum(cont_picks[None] * groups[:, None, :], axis=2)
    )
    same_segment = (segment[:, None] == segment[None, :]) & (position[None, :] <= position[:, None])
    context = (
        jnp.logical_not(is_prompt)[None, :, None]
        & is_prompt[None, None, :]
        & (source[:, :, None] == segment[None, None, :])
    )
    return (same_segment[None] | context, position)


def rotary_tables(position):
    half_dim = HEAD_DIM // 2
    frequency = rope_base ** (-(2.0 * jnp.arange(half_dim, dtype=F32)) / HEAD_DIM)
    angles = position.astype(F32)[:, None] * frequency[None, :]
    cosine = jnp.cos(angles)
    sine = jnp.sin(angles)
    return (cosine[None, :, None, :], sine[None, :, None, :])


def rotate(values, cosine, sine):
    first, second = jnp.split(values, 2, axis=-1)
    return jnp.concatenate([first * cosine - second * sine, second * cosine + first * sine], -1)


def dot(left, right, dims):
    return lax.dot_general(left, right, (dims, ((), ())), preferred_element_type=F32)


PARTS = 2
EXTRA = 16


def ffn_kernel(sizes, groups, meta, rows_ref, cot_ref, side_ref, *refs):
    n_g, f_pad, f_one, d_own = sizes
    blocks = refs[: groups * 2 * n_g]
    sums = refs[groups * 2 * n_g : -8]
    out_ref, normed_ref, act_ref, gate_ref, up_ref, w_gu, w_down, sems = refs[-8:]
    g_at, k_at, c_at = meta[0], meta[1], meta[2]
    shared = groups == 1

    @pl.when(pl.program_id(0) == 0)
    def _():
        copies = []
        for half in range(2):
            for shift in range(n_g):
                at = half * n_g + shift
                column = 2 * (g_at ^ shift) + (k_at ^ half)
                lanes = pl.ds(pl.multiple_of(column * d_own, d_own), d_own)
                if shared:
                    both, down = blocks[at].at[: 2 * f_pad], blocks[at].at[2 * f_pad :]
                else:
                    both, down = blocks[at], blocks[2 * n_g + at]
                copies.append(
                    pltpu.make_async_copy(both, w_gu.at[: 2 * f_pad, lanes], sems.at[2 * at])
                )
                copies.append(pltpu.make_async_copy(down, w_down.at[:, lanes], sems.at[2 * at + 1]))
        for copy in copies:
            copy.start()
        if shared:
            w_gu[2 * f_pad :, :] = side_ref[...]
        for copy in copies:
            copy.wait()

    rows = rows_ref[...]
    count = rows.shape[0]
    n_c = cot_ref.shape[0]
    cot = jnp.concatenate(
        [
            jnp.concatenate([cot_ref[c ^ c_at, 0, row ^ c_at] for row in range(n_c)], axis=0)
            for c in range(n_c)
        ],
        axis=1,
    )
    minor = ((1,), (1,))
    pre = dot(w_gu[...], rows, minor)
    down_back = dot(w_down[...], cot, minor)
    gate_pre, up_pre = pre[:f_pad], pre[f_pad : 2 * f_pad]
    if shared:
        prob = jax.nn.sigmoid(pre[2 * f_pad : 2 * f_pad + 1])
        scale = jnp.broadcast_to(prob, (f_pad, count))
    else:
        full = f_pad // f_one
        pieces = [jnp.broadcast_to(side_ref[0, e : e + 1, :], (f_one, count)) for e in range(full)]
        if f_pad > full * f_one:
            pieces.append(jnp.zeros((f_pad - full * f_one, count), F32))
        scale = jnp.concatenate(pieces, axis=0)
    sigma = jax.nn.sigmoid(gate_pre)
    silu = gate_pre * sigma
    act = silu * up_pre
    act_grad = down_back * scale
    act_low = (act * scale).astype(BF16)
    gate_low = (act_grad * up_pre * sigma * (1.0 + gate_pre * (1.0 - sigma))).astype(BF16)
    up_low = (act_grad * silu).astype(BF16)
    act_ref[...] = act_low
    gate_ref[:f_pad, :] = gate_low
    up_ref[...] = up_low
    both = [gate_low, up_low]
    if shared:
        prob_part = jnp.sum(act * down_back, axis=0, keepdims=True)
        logit_part = prob_part * prob * (1.0 - prob)
        logit_high = logit_part.astype(BF16).astype(F32)
        logit_rows = jnp.concatenate(
            [logit_high, logit_part - logit_high, jnp.zeros((EXTRA - 2, count), F32)], axis=0
        ).astype(BF16)
        gate_ref[f_pad:, :] = logit_rows
        both.append(logit_rows)
    major = ((0,), (0,))
    out = dot(act_low, w_down[...], major)
    normed = dot(jnp.concatenate(both, axis=0), w_gu[...], major)
    if sums:
        out = out + sums[0][...].astype(F32)
        normed = normed + sums[1][...].astype(F32)
    out_ref[...] = out.astype(BF16)
    normed_ref[...] = normed.astype(BF16)


def ffn_pass(sizes, meta, rows, cot, side, blocks, sums):
    n_g, f_pad, _, d_own = sizes
    total, dim = rows.shape
    n_c, _, _, sub, cw = cot.shape
    tile = n_c * sub
    groups = len(blocks) // (2 * n_g)
    extra = EXTRA if groups == 1 else 0
    flat = lambda i, m: (i, 0)
    wide = lambda i, m: (0, i)
    if groups == 1:
        side_spec = pl.BlockSpec((EXTRA, dim), lambda i, m: (0, 0))
    else:
        side = side.reshape(-1, tile, 8).transpose(0, 2, 1)
        side_spec = pl.BlockSpec((1, 8, tile), lambda i, m: (i, 0, 0))
    return pl.pallas_call(
        functools.partial(ffn_kernel, sizes, groups),
        grid_spec=pltpu.PrefetchScalarGridSpec(
            num_scalar_prefetch=1,
            grid=(n_g,),
            in_specs=[
                pl.BlockSpec((tile, dim), flat),
                pl.BlockSpec((n_c, 1, n_c, sub, cw), lambda i, m: (0, i, 0, 0, 0)),
                side_spec,
            ]
            + [pl.BlockSpec(memory_space=pl.ANY)] * len(blocks)
            + [pl.BlockSpec((tile, dim), flat)] * len(sums),
            out_specs=[
                pl.BlockSpec((tile, dim), flat),
                pl.BlockSpec((tile, dim), flat),
                pl.BlockSpec((f_pad, tile), wide),
                pl.BlockSpec((f_pad + extra, tile), wide),
                pl.BlockSpec((f_pad, tile), wide),
            ],
            scratch_shapes=[
                pltpu.VMEM((2 * f_pad + extra, dim), BF16),
                pltpu.VMEM((f_pad, dim), BF16),
                pltpu.SemaphoreType.DMA((4 * n_g,)),
            ],
        ),
        out_shape=[
            jax.ShapeDtypeStruct((total, dim), BF16),
            jax.ShapeDtypeStruct((total, dim), BF16),
            jax.ShapeDtypeStruct((f_pad, total), BF16),
            jax.ShapeDtypeStruct((f_pad + extra, total), BF16),
            jax.ShapeDtypeStruct((f_pad, total), BF16),
        ],
        compiler_params=pltpu.CompilerParams(
            dimension_semantics=("arbitrary",), vmem_limit_bytes=60 * 1024 * 1024
        ),
        cost_estimate=pl.CostEstimate(
            flops=12 * total * dim * f_pad,
            bytes_accessed=(8 + 4 * len(sums)) * total * dim + 6 * total * f_pad + 6 * f_pad * dim,
            transcendentals=total * f_pad,
        ),
        name="ffn_pass",
    )(meta, rows, cot, side, *blocks, *sums)


def grad_kernel(parts, kinds, f_pad, meta, *refs):
    lefts, refs = refs[: parts * len(kinds)], refs[parts * len(kinds) :]
    values = {}
    for cot in sorted(set(kinds)):
        rights, refs = refs[:parts], refs[parts:]
        if cot:
            _, n_g, n_c, _, _ = rights[0].shape
            order = [(g, c) for g in range(n_g) for c in range(n_c)]
            values[cot] = [
                jnp.concatenate([right[0, g, c ^ meta[2]] for g, c in order], axis=0)
                for right in rights
            ]
        else:
            values[cot] = [right[...] for right in rights]
    for i, cot in enumerate(kinds):
        total = None
        for left, value in zip(lefts[i * parts : (i + 1) * parts], values[cot]):
            term = dot(left[...], value, ((1,), (0,)))
            total = term if total is None else total + term
        refs[0][0, 0, i * f_pad : (i + 1) * f_pad] = total[:f_pad].astype(BF16)
        if total.shape[0] > f_pad:
            refs[1][...] = jnp.broadcast_to(
                total[f_pad : f_pad + 1] + total[f_pad + 1 : f_pad + 2], refs[1].shape
            )


def weight_grad(sizes, meta, kinds, lefts, normed, cots):
    n_g, f_pad, _, d_own = sizes
    parts = len(normed)
    part_rows, dim = normed[0].shape
    extra = max(value[0].shape[0] for value in lefts) > f_pad
    n_c, _, _, sub, cw = cots[0].shape
    per = cw // d_own
    arrays, specs = [], []
    for values in lefts:
        arrays += values
        specs += [pl.BlockSpec(values[0].shape, lambda j, m: (0, 0))] * parts
    if False in kinds:
        arrays += normed
        specs += [pl.BlockSpec((part_rows, d_own), lambda j, m: (0, j))] * parts
    if True in kinds:
        arrays += cots
        specs += [
            pl.BlockSpec(
                (1, n_g, n_c, sub, d_own), lambda j, m: ((j // per) ^ m[2], 0, 0, 0, j % per)
            )
        ] * parts
    f_out = len(kinds) * f_pad
    out_specs = [
        pl.BlockSpec((1, 1, f_out, d_own), lambda j, m: ((j % 2) ^ m[1], (j // 2) ^ m[0], 0, 0))
    ]
    out_shape = [jax.ShapeDtypeStruct((2, n_g, f_out, d_own), BF16)]
    if extra:
        out_specs.append(pl.BlockSpec((8, d_own), lambda j, m: (0, j)))
        out_shape.append(jax.ShapeDtypeStruct((8, dim), F32))
    return pl.pallas_call(
        functools.partial(grad_kernel, parts, kinds, f_pad),
        grid_spec=pltpu.PrefetchScalarGridSpec(
            num_scalar_prefetch=1, grid=(2 * n_g,), in_specs=specs, out_specs=out_specs
        ),
        out_shape=out_shape,
        compiler_params=pltpu.CompilerParams(
            dimension_semantics=("arbitrary",), vmem_limit_bytes=56 * 1024 * 1024
        ),
        cost_estimate=pl.CostEstimate(
            flops=2 * parts * part_rows * dim * f_out,
            bytes_accessed=2 * parts * part_rows * (dim + f_out) + 2 * f_out * dim,
            transcendentals=0,
        ),
        name="weight_grad",
    )(meta, *arrays)


def tie(*values):
    return lax.optimization_barrier(values)


def norm_back(normed_grad, unit_rows, scale, gain):
    weighted = normed_grad * gain
    rows_grad = scale * (
        weighted - unit_rows * jnp.mean(weighted * unit_rows, axis=-1, keepdims=True)
    )
    return (rows_grad, jnp.sum(normed_grad * unit_rows, axis=0))


def swap(value, axis):
    return lax.ppermute(value, axis, [(0, 1), (1, 0)])


def shift_by(value, axis, shift):
    if shift == 0:
        return value
    return lax.ppermute(value, axis, [(i, i ^ shift) for i in range(lax.axis_size(axis))])


def gather_joined(value, axis, at):
    bit = lax.axis_size(axis) // 2
    while bit:
        shape = value.shape[:at] + (2 * value.shape[at],) + value.shape[at + 1 :]
        value = jnp.stack([value, shift_by(value, axis, bit)], axis=at + 1).reshape(shape)
        bit //= 2
    return value


def halve(value, axis, at, bit, after=None):
    size = value.shape[at]
    shape = value.shape[:at] + (size // 2, 2) + value.shape[at + 1 :]
    pair = value.reshape(shape)
    keep, send = (lax.index_in_dim(pair, i, at + 1, keepdims=False) for i in range(2))
    other = shift_by(send, axis, bit)
    if after is not None:
        keep, _ = tie(keep, after)
    return (keep.astype(F32) + other.astype(F32)).astype(BF16)


def col_gather(value, count):
    spread = jnp.broadcast_to(value[None], (count,) + value.shape)
    return lax.all_to_all(spread, COL, 0, 0, tiled=True)


def col_sum(partial, count):
    parts = partial.astype(BF16).reshape((count, -1) + partial.shape[1:])
    return jnp.sum(lax.all_to_all(parts, COL, 0, 0, tiled=True).astype(F32), axis=0)


def rows_to_features(rows, count):
    row_count, width = rows.shape
    parts = rows.reshape(row_count, count, width // count).transpose(1, 0, 2)
    moved = lax.all_to_all(parts, COL, 0, 0, tiled=True)
    blocks = moved.reshape(2, row_count * count // 2, width // count)
    return lax.all_to_all(blocks, "k", 0, 0, tiled=True)


def shards(
    tokens,
    routes,
    route_weights,
    group_ids,
    first_gain,
    query_weight,
    key_weight,
    value_weight,
    output_weight,
    second_gain,
    shared_gate,
    shared_up,
    shared_down,
    shared_logit,
    expert_gate,
    expert_up,
    expert_down,
    cotangent,
):
    n_g = lax.axis_size("g")
    n_c = lax.axis_size("y") * lax.axis_size("x")
    n_y, n_x = lax.axis_size("y"), lax.axis_size("x")
    n_row = 2 * n_g
    at_g, at_k = lax.axis_index("g"), lax.axis_index("k")
    at_c = lax.axis_index(COL)
    block = tokens.shape[1]
    dim = query_weight.shape[0] * n_row
    d_own = query_weight.shape[0]
    width = query_weight.shape[1]
    heads = width // HEAD_DIM
    local_experts = expert_gate.shape[1]
    span = 2 * block
    total = n_g * span
    own_rows = span // n_c
    pick = lambda array, index, axis=0: lax.dynamic_index_in_dim(array, index, axis, keepdims=False)

    labels = jnp.arange(EXPERTS, dtype=jnp.int32)
    mixing = jnp.sum(
        jnp.where(
            routes[:, None] == labels[None, :, None, None], route_weights[:, None], 0.0
        ),
        axis=-1,
    )
    small = jnp.concatenate(
        [
            mixing.reshape(2 * EXPERTS, block),
            jnp.zeros((8, block), F32)
            .at[0, :d_own].set(first_gain.astype(F32))
            .at[1, :d_own].set(second_gain.astype(F32))
            .at[2, :d_own].set(shared_logit.astype(F32))
            .at[3, : 2 * CONTS].set(group_ids.astype(F32).reshape(-1)),
        ],
        axis=0,
    )
    small_all = lax.all_to_all(
        jnp.broadcast_to(small[None], (n_row,) + small.shape), ROW, 0, 0, tiled=True
    )
    f_shared = shared_gate.shape[1] // n_g
    f_routed = expert_gate.shape[2] // n_g
    f_experts = local_experts * f_routed
    f_one, f_two = -(-f_shared // 16) * 16, -(-f_experts // 16) * 16
    sizes_s = (n_g, f_one, f_shared, d_own)
    sizes_e = (n_g, f_two, f_routed, d_own)
    meta = jnp.stack([at_g, at_k, at_c]).astype(jnp.int32)

    def fill(value, size):
        return jnp.pad(value, ((0, 0), (0, size - value.shape[1]), (0, 0)))

    def slices_s(value):
        return fill(value.reshape(n_g, f_shared, d_own), f_one)

    def slices_e(value):
        value = value.reshape(local_experts, n_g, f_routed, d_own).transpose(1, 0, 2, 3)
        return fill(value.reshape(n_g, f_experts, d_own), f_two)

    weight_slices = [
        jnp.concatenate([slices_s(w) for w in (shared_gate.T, shared_up.T, shared_down)], axis=1),
        jnp.concatenate([slices_e(w.transpose(1, 2, 0)) for w in (expert_gate, expert_up)], axis=1),
        slices_e(expert_down),
    ]
    picked = [[pick(value, at_g ^ shift) for shift in range(n_g)] for value in weight_slices]
    qkv = lax.all_gather(
        jnp.concatenate([query_weight, key_weight, value_weight], axis=1), ROW, axis=0, tiled=True
    )
    out_w = lax.all_gather(output_weight, ROW, axis=1, tiled=True)
    picked[0], qkv, small_all = tie(picked[0], qkv, small_all)
    own_blocks = [
        [shift_by(value, "g", shift) for shift, value in enumerate(values)] for values in picked
    ]

    token_part = lax.all_to_all(tokens, "k", 0, 0, tiled=True).reshape(span, -1)
    cot_part = lax.all_to_all(cotangent, "k", 0, 0, tiled=True).reshape(span, -1)

    sub = own_rows // PARTS
    cot_rows = cot_part.reshape(1, n_c, PARTS, sub, dim // n_c)
    cot_rows = gather_joined(cot_rows, "g", 0)
    cot_rows, qkv = tie(cot_rows, qkv)
    inputs = col_gather(token_part, n_c).reshape(n_c, span, -1).transpose(1, 0, 2)
    inputs = inputs.reshape(span, dim).astype(F32)

    gain_1 = small_all[:, 16, :d_own].reshape(dim)
    gain_2 = small_all[:, 17, :d_own].reshape(dim)
    logit_w = small_all[:, 18, :d_own].reshape(dim)
    groups_all = small_all[:, 19, : 2 * CONTS].reshape(n_g, 2, 2, CONTS)
    groups = pick(pick(groups_all, at_g), at_k, 1).astype(jnp.int32)
    mixing_all = small_all[:, : 2 * EXPERTS].reshape(n_row, 2, EXPERTS, block)
    mixing_own = lax.dynamic_slice_in_dim(
        pick(mixing_all, at_k, 1), at_c * local_experts, local_experts, 1
    )
    mixing_own = mixing_own.transpose(0, 2, 1).reshape(total, local_experts)

    first_scale = lax.rsqrt(jnp.mean(inputs * inputs, axis=-1, keepdims=True) + epsilon)
    normed_1 = (inputs * first_scale * gain_1).astype(BF16)
    projected = dot(normed_1, qkv, ((1,), (0,)))
    allowed, position = block_layout(groups, block)
    cosine, sine = rotary_tables(position)
    head_shape = (2, block, heads, HEAD_DIM)
    query_rot = rotate(projected[:, :width].reshape(head_shape), cosine, sine).astype(BF16)
    key_rot = rotate(projected[:, width : 2 * width].reshape(head_shape), cosine, sine).astype(BF16)
    value_low = projected[:, 2 * width :].reshape(head_shape).astype(BF16)

    def einsum(form, left, right):
        return jnp.einsum(form, left, right, preferred_element_type=F32)

    scores = jnp.where(
        allowed[:, None],
        einsum("bqhd,bkhd->bhqk", query_rot, key_rot) * (1.0 / math.sqrt(HEAD_DIM)),
        masked_score,
    )
    peak = jnp.max(scores, axis=-1, keepdims=True)
    exp_scores = jnp.exp(scores - peak)
    probabilities = exp_scores / jnp.sum(exp_scores, axis=-1, keepdims=True)
    prob_low = probabilities.astype(BF16)
    mixed = einsum("bhqk,bkhd->bqhd", prob_low, value_low).astype(BF16).reshape(span, width)
    cot_all = []
    for part in range(PARTS):
        value = cot_rows[:, :, part][None, None]
        axis = ("x", "y")[1 - part % 2]
        cot_all.append(gather_joined(value, axis, ("y", "x").index(axis)))
    cot_all, mixed, own_blocks[0][1] = tie(cot_all, mixed, own_blocks[0][1])
    for part in range(PARTS):
        axis = ("x", "y")[part % 2]
        value = gather_joined(cot_all[part], axis, ("y", "x").index(axis))
        cot_all[part] = value.reshape(n_c, n_g, n_c, sub, dim // n_c)
    attention = col_sum(dot(mixed, out_w, ((1,), (0,))), n_c)

    own_inputs = lax.dynamic_slice_in_dim(inputs, at_c * own_rows, own_rows, 0)
    own_blocks[0][2:], attention = tie(own_blocks[0][2:], attention)
    hidden = own_inputs + attention
    second_scale = lax.rsqrt(jnp.mean(hidden * hidden, axis=-1, keepdims=True) + epsilon)
    unit_2 = hidden * second_scale
    normed_own = (unit_2 * gain_2).astype(BF16)

    def gather_cols(value):
        sides = []
        for side, order in enumerate((("y", "x"), ("x", "y"))):
            half = value[..., side * (dim // 2) : (side + 1) * (dim // 2)]
            for axis in order:
                half = gather_joined(half, axis, 1 + ("y", "x").index(axis))
            sides.append(half)
        return jnp.concatenate(sides, axis=-1).reshape(-1, dim)

    routed_gu, routed_d = own_blocks[1:]
    normed_own, cot_all = tie(normed_own, cot_all)
    halves = [normed_own[part * sub : (part + 1) * sub][None] for part in range(PARTS)]
    halves[0] = gather_joined(halves[0], "g", 0)
    halves[0], halves[1], routed_gu[1] = tie(halves[0], halves[1], routed_gu[1])
    halves[1] = gather_joined(halves[1], "g", 0)
    normed_parts = [gather_cols(halves[0][:, None, None])]
    normed_parts[0], halves[1], routed_gu[2:3] = tie(normed_parts[0], halves[1], routed_gu[2:3])
    normed_parts.append(gather_cols(halves[1][:, None, None]))
    normed_parts[1], routed_gu[3:], routed_d[1] = tie(
        normed_parts[1], routed_gu[3:], routed_d[1]
    )
    own_cot = [
        lax.dynamic_index_in_dim(cot[:, 0], at_c, 1, keepdims=False) for cot in cot_all
    ]
    own_cot = jnp.concatenate(own_cot, axis=1)
    own_cot = jnp.stack([pick(own_cot, at_c ^ c) for c in range(n_c)], axis=1)
    own_cot = own_cot.reshape(own_rows, dim)

    def own_core(grad, after=None):
        other = swap(grad[1], "k")
        grad = grad[0]
        if after is not None:
            grad, _ = tie(grad, after)
        return (grad.astype(F32) + other.astype(F32)).astype(BF16)

    def send_slices(both):
        return [shift_by(both[shift], "g", shift) for shift in range(n_g)]

    def place_slices(moved, kinds):
        moved = jnp.stack(moved)
        moved = jnp.stack([pick(moved, at_g ^ source) for source in range(n_g)])
        return [
            moved[:, i * (moved.shape[1] // kinds) :][:, : moved.shape[1] // kinds]
            for i in range(kinds)
        ]

    def place_s(value):
        return value[:, :f_shared].reshape(n_g * f_shared, d_own)

    def place_e(value):
        value = value[:, :f_experts].reshape(n_g, local_experts, f_routed, d_own)
        return value.transpose(1, 0, 2, 3).reshape(local_experts, n_g * f_routed, d_own)

    logit_low = jnp.zeros((EXTRA, dim), BF16).at[:2].set(logit_w.astype(BF16)[None])
    mixing_parts = mixing_own.reshape(n_g, n_c, PARTS, sub, local_experts)
    mixing_parts = jnp.stack([pick(mixing_parts, at_g ^ shift) for shift in range(n_g)])
    mixing_parts = jnp.stack([pick(mixing_parts, at_c ^ c, 1) for c in range(n_c)], axis=1)
    mixing_parts = jnp.pad(mixing_parts, ((0, 0),) * 4 + ((0, 8 - local_experts),))
    def blocks_of(values):
        return values + [swap(value, "k") for value in values]

    blocks_s = blocks_of(own_blocks[0])
    passes_s = [
        ffn_pass(sizes_s, meta, normed_parts[part], cot_all[part], logit_low, blocks_s, [])
        for part in range(PARTS)
    ]
    kinds = (False, False, True)
    grad_s, logit_sum = weight_grad(
        sizes_s, meta, kinds, [[p[i] for p in passes_s] for i in (3, 4, 2)], normed_parts, cot_all
    )
    logit_sum = logit_sum[0]
    sums = [[passes_s[part][0], passes_s[part][1]] for part in range(PARTS)]
    sums[0], grad_s = tie(sums[0], grad_s)
    blocks_e = blocks_of(own_blocks[1]) + blocks_of(own_blocks[2])
    passes = []
    for part in range(PARTS):
        if part == 1:
            both_s = own_core(grad_s, passes[0][2][:16, :128])
            sums[1], both_s = tie(sums[1], both_s)
        passes.append(
            ffn_pass(
                sizes_e,
                meta,
                normed_parts[part],
                cot_all[part],
                mixing_parts[:, :, part].reshape(-1, 8),
                blocks_e,
                sums[part],
            )
        )
    moved_s = send_slices(both_s)

    def split_sides(partial):
        part = partial.reshape(n_g, n_y, n_x, sub, dim)
        return [part[..., : dim // 2], part[..., dim // 2 :]]

    def scatter_axis(value, axis, at, after=None):
        bit = 1
        while bit < lax.axis_size(axis):
            value = halve(value, axis, at, bit, after)
            bit *= 2
        return lax.index_in_dim(value, 0, at, keepdims=False)

    def cols_first(sides, after=None):
        return [scatter_axis(sides[0], "x", 2, after), scatter_axis(sides[1], "y", 1, after)]

    def cols_second(sides):
        sides = [scatter_axis(sides[0], "y", 1), scatter_axis(sides[1], "x", 1)]
        return jnp.concatenate(sides, axis=-1)

    def chips_steps(value):
        bit = 1
        while 2 * bit < n_g:
            value = halve(value, "g", 0, bit)
            bit *= 2
        return value

    def chips_last(value):
        other = shift_by(value[1], "g", n_g // 2)
        return value[0].astype(F32) + other.astype(F32)

    acts, gates, ups = ([parts[i] for parts in passes] for i in (2, 3, 4))
    first = cols_first(split_sides(passes[0][1]), passes[1][2][:16, :128])
    first, acts = tie(first, acts)
    (grad_d,) = weight_grad(sizes_e, meta, (True,), [acts], normed_parts, cot_all)
    first = cols_second(first)
    second = cols_first(split_sides(passes[1][1]))
    first, second, gates, grad_d = tie(first, second, gates, grad_d)
    (grad_gu,) = weight_grad(sizes_e, meta, (False, False), [gates, ups], normed_parts, cot_all)
    first = chips_steps(first)
    second = cols_second(second)
    both_d = own_core(grad_d)
    first, second, both_d, moved_s[1:3], grad_gu = tie(first, second, both_d, moved_s[1:3], grad_gu)
    moved_d = send_slices(both_d)
    first = chips_last(first)
    second = chips_steps(second)
    both_gu = own_core(grad_gu)
    out_sides = [cols_first(split_sides(parts[0])) for parts in passes]
    first, second, both_gu, out_sides[0] = tie(first, second, both_gu, out_sides[0])
    second = chips_last(second)
    moved_gu = send_slices(both_gu)
    normed_grad_2 = jnp.concatenate([first, second], axis=0)
    normed_grad_2, moved_s[3:], out_sides[1] = tie(normed_grad_2, moved_s[3:], out_sides[1])
    hidden_part, gain_2_sum = norm_back(normed_grad_2, unit_2, second_scale, gain_2)
    hidden_grad = own_cot.astype(F32) + hidden_part
    attn_grad = col_gather(hidden_grad.astype(BF16), n_c).reshape(span, dim)
    attn_grad, moved_d[1:] = tie(attn_grad, moved_d[1:])
    out_parts = [cols_second(sides) for sides in out_sides]
    gate_s, up_s, down_s = (place_s(value) for value in place_slices(moved_s, 3))
    down_e = place_e(place_slices(moved_d, 1)[0])

    out_grad = dot(attn_grad, mixed, ((0,), (0,)))
    mixed_grad = dot(attn_grad, out_w, ((1,), (1,))).astype(BF16).reshape(head_shape)
    out_parts, mixed_grad, moved_gu[1] = tie(out_parts, mixed_grad, moved_gu[1])
    out_parts = [chips_steps(part) for part in out_parts]
    prob_grad = einsum("bqhd,bkhd->bhqk", mixed_grad, value_low)
    value_grad = einsum("bhqk,bqhd->bkhd", prob_low, mixed_grad).astype(BF16)
    center = jnp.sum(prob_grad * probabilities, axis=-1, keepdims=True)
    score_grad = (probabilities * (prob_grad - center) * (1.0 / math.sqrt(HEAD_DIM))).astype(BF16)
    out_parts, score_grad = tie(out_parts, score_grad)
    out_rows = [chips_last(part) for part in out_parts]
    query_grad = rotate(einsum("bhqk,bkhd->bqhd", score_grad, key_rot), cosine, -sine).astype(BF16)
    key_grad = rotate(einsum("bhqk,bqhd->bkhd", score_grad, query_rot), cosine, -sine).astype(BF16)
    qkv_grad = jnp.concatenate(
        [part.reshape(span, width) for part in (query_grad, key_grad, value_grad)], axis=1
    )
    qkv_grad, out_rows, moved_gu[2:3] = tie(qkv_grad, out_rows, moved_gu[2:3])
    out_rows = jnp.concatenate(out_rows, axis=0)
    qkv_sum = dot(normed_1, qkv_grad, ((0,), (0,)))
    normed_grad_1 = col_sum(dot(qkv_grad, qkv, ((1,), (1,))), n_c)
    normed_grad_1, moved_gu[3:] = tie(normed_grad_1, moved_gu[3:])
    gate_e, up_e = (place_e(value) for value in place_slices(moved_gu, 2))
    own_scale = lax.dynamic_slice_in_dim(first_scale, at_c * own_rows, own_rows, 0)
    rows_part, gain_1_sum = norm_back(normed_grad_1, own_inputs * own_scale, own_scale, gain_1)
    token_grad = rows_to_features((hidden_grad + rows_part).astype(BF16), n_c).astype(F32)

    result = rows_to_features((hidden + out_rows).astype(BF16), n_c)

    sums = jnp.stack([gain_1_sum, gain_2_sum, logit_sum]).reshape(3, n_row, d_own)
    sums = jnp.broadcast_to(sums.transpose(1, 0, 2)[:, None], (n_row, n_c, 3, d_own))
    sums = lax.all_to_all(sums.reshape(n_row * n_c, 3, d_own), ALL, 0, 0, tiled=True)
    sums = jnp.sum(sums, axis=0)

    out_w_grad = lax.psum_scatter(out_grad.astype(BF16), ROW, scatter_dimension=0, tiled=True)
    qkv_own = lax.psum_scatter(qkv_sum.astype(BF16), ROW, scatter_dimension=0, tiled=True)
    qkv_own = qkv_own.astype(F32)
    return (
        result,
        token_grad,
        sums[0],
        qkv_own[:, :width],
        qkv_own[:, width : 2 * width],
        qkv_own[:, 2 * width :],
        out_w_grad.T.astype(F32),
        sums[1],
        gate_s.T.astype(F32),
        up_s.T.astype(F32),
        down_s.astype(F32),
        sums[2],
        gate_e.transpose(2, 0, 1).astype(F32),
        up_e.transpose(2, 0, 1).astype(F32),
        down_e.astype(F32),
    )


def solution(mesh):
    n_row, n_col = mesh.shape["row"], mesh.shape["col"]
    inner = Mesh(mesh.devices.reshape(n_row // 2, 2, n_col // 2, 2), ALL)
    return jax.shard_map(
        shards,
        mesh=inner,
        in_specs=(
            P(None, ROW, COL),
            P(None, ROW, None),
            P(None, ROW, None),
            P(None, ROW),
            P(ROW),
            P(ROW, COL),
            P(ROW, COL),
            P(ROW, COL),
            P(COL, ROW),
            P(ROW),
            P(ROW, COL),
            P(ROW, COL),
            P(COL, ROW),
            P(ROW),
            P(ROW, COL, None),
            P(ROW, COL, None),
            P(COL, None, ROW),
            P(None, ROW, COL),
        ),
        out_specs=(
            P(None, ROW, COL),
            P(None, ROW, COL),
            P(ROW),
            P(ROW, COL),
            P(ROW, COL),
            P(ROW, COL),
            P(COL, ROW),
            P(ROW),
            P(ROW, COL),
            P(ROW, COL),
            P(COL, ROW),
            P(ROW),
            P(ROW, COL, None),
            P(ROW, COL, None),
            P(COL, None, ROW),
        ),
        check_vma=False,
    )
```

```python
import functools
import math

import jax
import jax.numpy as jnp
from jax import lax
from jax.experimental import pallas as pl
from jax.experimental.pallas import tpu as pltpu
from jax.sharding import Mesh, PartitionSpec as P

HEAD_DIM = 128
EXPERTS = 8
PROMPTS = 2
CONTS = 2
CONT_LEN = 64
PROMPT_LEN = 64

epsilon = 1e-06
rope_base = 1000000.0
masked_score = -1000000000.0

F32 = jnp.float32
BF16 = jnp.bfloat16
COL = ("y", "x")
ROW = ("g", "k")
ALL = ("g", "k", "y", "x")


def block_layout(groups, row_count):
    token_index = jnp.arange(row_count, dtype=jnp.int32)
    prompt_rows = PROMPTS * PROMPT_LEN
    is_prompt = token_index < prompt_rows
    cont_offset = jnp.maximum(token_index - prompt_rows, 0)
    cont_number = cont_offset // CONT_LEN
    segment = jnp.where(is_prompt, token_index // PROMPT_LEN, PROMPTS + cont_number)
    position = jnp.where(is_prompt, token_index % PROMPT_LEN, PROMPT_LEN + cont_offset % CONT_LEN)
    cont_picks = (cont_number[:, None] == jnp.arange(CONTS, dtype=jnp.int32)[None, :]).astype(
        jnp.int32
    )
    source = jnp.where(
        is_prompt[None], segment[None], jnp.sum(cont_picks[None] * groups[:, None, :], axis=2)
    )
    same_segment = (segment[:, None] == segment[None, :]) & (position[None, :] <= position[:, None])
    context = (
        jnp.logical_not(is_prompt)[None, :, None]
        & is_prompt[None, None, :]
        & (source[:, :, None] == segment[None, None, :])
    )
    return (same_segment[None] | context, position)


def rotary_tables(position):
    half_dim = HEAD_DIM // 2
    frequency = rope_base ** (-(2.0 * jnp.arange(half_dim, dtype=F32)) / HEAD_DIM)
    angles = position.astype(F32)[:, None] * frequency[None, :]
    cosine = jnp.cos(angles)
    sine = jnp.sin(angles)
    return (cosine[None, :, None, :], sine[None, :, None, :])


def rotate(values, cosine, sine):
    first, second = jnp.split(values, 2, axis=-1)
    return jnp.concatenate([first * cosine - second * sine, second * cosine + first * sine], -1)


def dot(left, right, dims):
    return lax.dot_general(left, right, (dims, ((), ())), preferred_element_type=F32)


PARTS = 2
EXTRA = 16


def ffn_kernel(sizes, groups, meta, rows_ref, cot_ref, side_ref, *refs):
    n_g, f_pad, f_one, d_own = sizes
    blocks = refs[: groups * 2 * n_g]
    sums = refs[groups * 2 * n_g : -8]
    out_ref, normed_ref, act_ref, gate_ref, up_ref, w_gu, w_down, sems = refs[-8:]
    g_at, k_at, c_at = meta[0], meta[1], meta[2]
    shared = groups == 1

    @pl.when(pl.program_id(0) == 0)
    def _():
        copies = []
        for half in range(2):
            for shift in range(n_g):
                at = half * n_g + shift
                column = 2 * (g_at ^ shift) + (k_at ^ half)
                lanes = pl.ds(pl.multiple_of(column * d_own, d_own), d_own)
                if shared:
                    both, down = blocks[at].at[: 2 * f_pad], blocks[at].at[2 * f_pad :]
                else:
                    both, down = blocks[at], blocks[2 * n_g + at]
                copies.append(
                    pltpu.make_async_copy(both, w_gu.at[: 2 * f_pad, lanes], sems.at[2 * at])
                )
                copies.append(pltpu.make_async_copy(down, w_down.at[:, lanes], sems.at[2 * at + 1]))
        for copy in copies:
            copy.start()
        if shared:
            w_gu[2 * f_pad :, :] = side_ref[...]
        for copy in copies:
            copy.wait()

    rows = rows_ref[...]
    count = rows.shape[0]
    n_c = cot_ref.shape[0]
    cot = jnp.concatenate(
        [
            jnp.concatenate([cot_ref[c ^ c_at, 0, row ^ c_at] for row in range(n_c)], axis=0)
            for c in range(n_c)
        ],
        axis=1,
    )
    minor = ((1,), (1,))
    pre = dot(w_gu[...], rows, minor)
    down_back = dot(w_down[...], cot, minor)
    gate_pre, up_pre = pre[:f_pad], pre[f_pad : 2 * f_pad]
    if shared:
        prob = jax.nn.sigmoid(pre[2 * f_pad : 2 * f_pad + 1])
        scale = jnp.broadcast_to(prob, (f_pad, count))
    else:
        full = f_pad // f_one
        pieces = [jnp.broadcast_to(side_ref[0, e : e + 1, :], (f_one, count)) for e in range(full)]
        if f_pad > full * f_one:
            pieces.append(jnp.zeros((f_pad - full * f_one, count), F32))
        scale = jnp.concatenate(pieces, axis=0)
    sigma = jax.nn.sigmoid(gate_pre)
    silu = gate_pre * sigma
    act = silu * up_pre
    act_grad = down_back * scale
    act_low = (act * scale).astype(BF16)
    gate_low = (act_grad * up_pre * sigma * (1.0 + gate_pre * (1.0 - sigma))).astype(BF16)
    up_low = (act_grad * silu).astype(BF16)
    act_ref[...] = act_low
    gate_ref[:f_pad, :] = gate_low
    up_ref[...] = up_low
    both = [gate_low, up_low]
    if shared:
        prob_part = jnp.sum(act * down_back, axis=0, keepdims=True)
        logit_part = prob_part * prob * (1.0 - prob)
        logit_high = logit_part.astype(BF16).astype(F32)
        logit_rows = jnp.concatenate(
            [logit_high, logit_part - logit_high, jnp.zeros((EXTRA - 2, count), F32)], axis=0
        ).astype(BF16)
        gate_ref[f_pad:, :] = logit_rows
        both.append(logit_rows)
    major = ((0,), (0,))
    out = dot(act_low, w_down[...], major)
    normed = dot(jnp.concatenate(both, axis=0), w_gu[...], major)
    if sums:
        out = out + sums[0][...].astype(F32)
        normed = normed + sums[1][...].astype(F32)
    out_ref[...] = out.astype(BF16)
    normed_ref[...] = normed.astype(BF16)


def ffn_pass(sizes, meta, rows, cot, side, blocks, sums):
    n_g, f_pad, _, d_own = sizes
    total, dim = rows.shape
    n_c, _, _, sub, cw = cot.shape
    tile = n_c * sub
    groups = len(blocks) // (2 * n_g)
    extra = EXTRA if groups == 1 else 0
    flat = lambda i, m: (i, 0)
    wide = lambda i, m: (0, i)
    if groups == 1:
        side_spec = pl.BlockSpec((EXTRA, dim), lambda i, m: (0, 0))
    else:
        side = side.reshape(-1, tile, 8).transpose(0, 2, 1)
        side_spec = pl.BlockSpec((1, 8, tile), lambda i, m: (i, 0, 0))
    return pl.pallas_call(
        functools.partial(ffn_kernel, sizes, groups),
        grid_spec=pltpu.PrefetchScalarGridSpec(
            num_scalar_prefetch=1,
            grid=(n_g,),
            in_specs=[
                pl.BlockSpec((tile, dim), flat),
                pl.BlockSpec((n_c, 1, n_c, sub, cw), lambda i, m: (0, i, 0, 0, 0)),
                side_spec,
            ]
            + [pl.BlockSpec(memory_space=pl.ANY)] * len(blocks)
            + [pl.BlockSpec((tile, dim), flat)] * len(sums),
            out_specs=[
                pl.BlockSpec((tile, dim), flat),
                pl.BlockSpec((tile, dim), flat),
                pl.BlockSpec((f_pad, tile), wide),
                pl.BlockSpec((f_pad + extra, tile), wide),
                pl.BlockSpec((f_pad, tile), wide),
            ],
            scratch_shapes=[
                pltpu.VMEM((2 * f_pad + extra, dim), BF16),
                pltpu.VMEM((f_pad, dim), BF16),
                pltpu.SemaphoreType.DMA((4 * n_g,)),
            ],
        ),
        out_shape=[
            jax.ShapeDtypeStruct((total, dim), BF16),
            jax.ShapeDtypeStruct((total, dim), BF16),
            jax.ShapeDtypeStruct((f_pad, total), BF16),
            jax.ShapeDtypeStruct((f_pad + extra, total), BF16),
            jax.ShapeDtypeStruct((f_pad, total), BF16),
        ],
        compiler_params=pltpu.CompilerParams(
            dimension_semantics=("arbitrary",), vmem_limit_bytes=60 * 1024 * 1024
        ),
        cost_estimate=pl.CostEstimate(
            flops=12 * total * dim * f_pad,
            bytes_accessed=(8 + 4 * len(sums)) * total * dim + 6 * total * f_pad + 6 * f_pad * dim,
            transcendentals=total * f_pad,
        ),
        name="ffn_pass",
    )(meta, rows, cot, side, *blocks, *sums)


def grad_kernel(parts, kinds, f_pad, meta, *refs):
    lefts, refs = refs[: parts * len(kinds)], refs[parts * len(kinds) :]
    values = {}
    for cot in sorted(set(kinds)):
        rights, refs = refs[:parts], refs[parts:]
        if cot:
            _, n_g, n_c, _, _ = rights[0].shape
            order = [(g, c) for g in range(n_g) for c in range(n_c)]
            values[cot] = [
                jnp.concatenate([right[0, g, c ^ meta[2]] for g, c in order], axis=0)
                for right in rights
            ]
        else:
            values[cot] = [right[...] for right in rights]
    for i, cot in enumerate(kinds):
        total = None
        for left, value in zip(lefts[i * parts : (i + 1) * parts], values[cot]):
            term = dot(left[...], value, ((1,), (0,)))
            total = term if total is None else total + term
        refs[0][0, 0, i * f_pad : (i + 1) * f_pad] = total[:f_pad].astype(BF16)
        if total.shape[0] > f_pad:
            refs[1][...] = jnp.broadcast_to(
                total[f_pad : f_pad + 1] + total[f_pad + 1 : f_pad + 2], refs[1].shape
            )


def weight_grad(sizes, meta, kinds, lefts, normed, cots):
    n_g, f_pad, _, d_own = sizes
    parts = len(normed)
    part_rows, dim = normed[0].shape
    extra = max(value[0].shape[0] for value in lefts) > f_pad
    n_c, _, _, sub, cw = cots[0].shape
    per = cw // d_own
    arrays, specs = [], []
    for values in lefts:
        arrays += values
        specs += [pl.BlockSpec(values[0].shape, lambda j, m: (0, 0))] * parts
    if False in kinds:
        arrays += normed
        specs += [pl.BlockSpec((part_rows, d_own), lambda j, m: (0, j))] * parts
    if True in kinds:
        arrays += cots
        specs += [
            pl.BlockSpec(
                (1, n_g, n_c, sub, d_own), lambda j, m: ((j // per) ^ m[2], 0, 0, 0, j % per)
            )
        ] * parts
    f_out = len(kinds) * f_pad
    out_specs = [
        pl.BlockSpec((1, 1, f_out, d_own), lambda j, m: ((j % 2) ^ m[1], (j // 2) ^ m[0], 0, 0))
    ]
    out_shape = [jax.ShapeDtypeStruct((2, n_g, f_out, d_own), BF16)]
    if extra:
        out_specs.append(pl.BlockSpec((8, d_own), lambda j, m: (0, j)))
        out_shape.append(jax.ShapeDtypeStruct((8, dim), F32))
    return pl.pallas_call(
        functools.partial(grad_kernel, parts, kinds, f_pad),
        grid_spec=pltpu.PrefetchScalarGridSpec(
            num_scalar_prefetch=1, grid=(2 * n_g,), in_specs=specs, out_specs=out_specs
        ),
        out_shape=out_shape,
        compiler_params=pltpu.CompilerParams(
            dimension_semantics=("arbitrary",), vmem_limit_bytes=56 * 1024 * 1024
        ),
        cost_estimate=pl.CostEstimate(
            flops=2 * parts * part_rows * dim * f_out,
            bytes_accessed=2 * parts * part_rows * (dim + f_out) + 2 * f_out * dim,
            transcendentals=0,
        ),
        name="weight_grad",
    )(meta, *arrays)


def tie(*values):
    return lax.optimization_barrier(values)


def norm_back(normed_grad, unit_rows, scale, gain):
    weighted = normed_grad * gain
    rows_grad = scale * (
        weighted - unit_rows * jnp.mean(weighted * unit_rows, axis=-1, keepdims=True)
    )
    return (rows_grad, jnp.sum(normed_grad * unit_rows, axis=0))


def swap(value, axis):
    return lax.ppermute(value, axis, [(0, 1), (1, 0)])


def shift_by(value, axis, shift):
    if shift == 0:
        return value
    return lax.ppermute(value, axis, [(i, i ^ shift) for i in range(lax.axis_size(axis))])


def gather_joined(value, axis, at):
    bit = lax.axis_size(axis) // 2
    while bit:
        shape = value.shape[:at] + (2 * value.shape[at],) + value.shape[at + 1 :]
        value = jnp.stack([value, shift_by(value, axis, bit)], axis=at + 1).reshape(shape)
        bit //= 2
    return value


def halve(value, axis, at, bit, after=None):
    size = value.shape[at]
    shape = value.shape[:at] + (size // 2, 2) + value.shape[at + 1 :]
    pair = value.reshape(shape)
    keep, send = (lax.index_in_dim(pair, i, at + 1, keepdims=False) for i in range(2))
    other = shift_by(send, axis, bit)
    if after is not None:
        keep, _ = tie(keep, after)
    return (keep.astype(F32) + other.astype(F32)).astype(BF16)


def col_gather(value, count):
    spread = jnp.broadcast_to(value[None], (count,) + value.shape)
    return lax.all_to_all(spread, COL, 0, 0, tiled=True)


def col_sum(partial, count):
    parts = partial.astype(BF16).reshape((count, -1) + partial.shape[1:])
    return jnp.sum(lax.all_to_all(parts, COL, 0, 0, tiled=True).astype(F32), axis=0)


def rows_to_features(rows, count):
    row_count, width = rows.shape
    parts = rows.reshape(row_count, count, width // count).transpose(1, 0, 2)
    moved = lax.all_to_all(parts, COL, 0, 0, tiled=True)
    blocks = moved.reshape(2, row_count * count // 2, width // count)
    return lax.all_to_all(blocks, "k", 0, 0, tiled=True)


def shards(
    tokens,
    routes,
    route_weights,
    group_ids,
    first_gain,
    query_weight,
    key_weight,
    value_weight,
    output_weight,
    second_gain,
    shared_gate,
    shared_up,
    shared_down,
    shared_logit,
    expert_gate,
    expert_up,
    expert_down,
    cotangent,
):
    n_g = lax.axis_size("g")
    n_c = lax.axis_size("y") * lax.axis_size("x")
    n_y, n_x = lax.axis_size("y"), lax.axis_size("x")
    n_row = 2 * n_g
    at_g, at_k = lax.axis_index("g"), lax.axis_index("k")
    at_c = lax.axis_index(COL)
    block = tokens.shape[1]
    dim = query_weight.shape[0] * n_row
    d_own = query_weight.shape[0]
    width = query_weight.shape[1]
    heads = width // HEAD_DIM
    local_experts = expert_gate.shape[1]
    span = 2 * block
    total = n_g * span
    own_rows = span // n_c
    pick = lambda array, index, axis=0: lax.dynamic_index_in_dim(array, index, axis, keepdims=False)

    labels = jnp.arange(EXPERTS, dtype=jnp.int32)
    mixing = jnp.sum(
        jnp.where(
            routes[:, None] == labels[None, :, None, None], route_weights[:, None], 0.0
        ),
        axis=-1,
    )
    small = jnp.concatenate(
        [
            mixing.reshape(2 * EXPERTS, block),
            jnp.zeros((8, block), F32)
            .at[0, :d_own].set(first_gain.astype(F32))
            .at[1, :d_own].set(second_gain.astype(F32))
            .at[2, :d_own].set(shared_logit.astype(F32))
            .at[3, : 2 * CONTS].set(group_ids.astype(F32).reshape(-1)),
        ],
        axis=0,
    )
    small_all = lax.all_to_all(
        jnp.broadcast_to(small[None], (n_row,) + small.shape), ROW, 0, 0, tiled=True
    )
    f_shared = shared_gate.shape[1] // n_g
    f_routed = expert_gate.shape[2] // n_g
    f_experts = local_experts * f_routed
    f_one, f_two = -(-f_shared // 16) * 16, -(-f_experts // 16) * 16
    sizes_s = (n_g, f_one, f_shared, d_own)
    sizes_e = (n_g, f_two, f_routed, d_own)
    meta = jnp.stack([at_g, at_k, at_c]).astype(jnp.int32)

    def fill(value, size):
        return jnp.pad(value, ((0, 0), (0, size - value.shape[1]), (0, 0)))

    def slices_s(value):
        return fill(value.reshape(n_g, f_shared, d_own), f_one)

    def slices_e(value):
        value = value.reshape(local_experts, n_g, f_routed, d_own).transpose(1, 0, 2, 3)
        return fill(value.reshape(n_g, f_experts, d_own), f_two)

    weight_slices = [
        jnp.concatenate([slices_s(w) for w in (shared_gate.T, shared_up.T, shared_down)], axis=1),
        jnp.concatenate([slices_e(w.transpose(1, 2, 0)) for w in (expert_gate, expert_up)], axis=1),
        slices_e(expert_down),
    ]
    picked = [[pick(value, at_g ^ shift) for shift in range(n_g)] for value in weight_slices]
    qkv = lax.all_gather(
        jnp.concatenate([query_weight, key_weight, value_weight], axis=1), ROW, axis=0, tiled=True
    )
    out_w = lax.all_gather(output_weight, ROW, axis=1, tiled=True)
    picked[0], qkv, small_all = tie(picked[0], qkv, small_all)
    own_blocks = [
        [shift_by(value, "g", shift) for shift, value in enumerate(values)] for values in picked
    ]

    token_part = lax.all_to_all(tokens, "k", 0, 0, tiled=True).reshape(span, -1)
    cot_part = lax.all_to_all(cotangent, "k", 0, 0, tiled=True).reshape(span, -1)

    sub = own_rows // PARTS
    cot_rows = cot_part.reshape(1, n_c, PARTS, sub, dim // n_c)
    far = shift_by(cot_rows, "g", n_g // 2)
    cot_rows, far, qkv = tie(cot_rows, far, qkv)
    cot_rows = jnp.concatenate([cot_rows, far], axis=0)
    bit = n_g // 4
    while bit:
        far = shift_by(cot_rows, "g", bit)
        cot_rows = jnp.stack([cot_rows, far], axis=1).reshape((-1,) + cot_rows.shape[1:])
        bit //= 2
    inputs = col_gather(token_part, n_c).reshape(n_c, span, -1).transpose(1, 0, 2)
    inputs = inputs.reshape(span, dim).astype(F32)

    gain_1 = small_all[:, 16, :d_own].reshape(dim)
    gain_2 = small_all[:, 17, :d_own].reshape(dim)
    logit_w = small_all[:, 18, :d_own].reshape(dim)
    groups_all = small_all[:, 19, : 2 * CONTS].reshape(n_g, 2, 2, CONTS)
    groups = pick(pick(groups_all, at_g), at_k, 1).astype(jnp.int32)
    mixing_all = small_all[:, : 2 * EXPERTS].reshape(n_row, 2, EXPERTS, block)
    mixing_own = lax.dynamic_slice_in_dim(
        pick(mixing_all, at_k, 1), at_c * local_experts, local_experts, 1
    )
    mixing_own = mixing_own.transpose(0, 2, 1).reshape(total, local_experts)

    first_scale = lax.rsqrt(jnp.mean(inputs * inputs, axis=-1, keepdims=True) + epsilon)
    normed_1 = (inputs * first_scale * gain_1).astype(BF16)
    projected = dot(normed_1, qkv, ((1,), (0,)))
    allowed, position = block_layout(groups, block)
    cosine, sine = rotary_tables(position)
    head_shape = (2, block, heads, HEAD_DIM)
    query_rot = rotate(projected[:, :width].reshape(head_shape), cosine, sine).astype(BF16)
    key_rot = rotate(projected[:, width : 2 * width].reshape(head_shape), cosine, sine).astype(BF16)
    value_low = projected[:, 2 * width :].reshape(head_shape).astype(BF16)

    def einsum(form, left, right):
        return jnp.einsum(form, left, right, preferred_element_type=F32)

    scores = jnp.where(
        allowed[:, None],
        einsum("bqhd,bkhd->bhqk", query_rot, key_rot) * (1.0 / math.sqrt(HEAD_DIM)),
        masked_score,
    )
    peak = jnp.max(scores, axis=-1, keepdims=True)
    exp_scores = jnp.exp(scores - peak)
    probabilities = exp_scores / jnp.sum(exp_scores, axis=-1, keepdims=True)
    prob_low = probabilities.astype(BF16)
    mixed = einsum("bhqk,bkhd->bqhd", prob_low, value_low).astype(BF16).reshape(span, width)
    cot_rows, mixed, own_blocks[0][1] = tie(cot_rows, mixed, own_blocks[0][1])
    attention = col_sum(dot(mixed, out_w, ((1,), (0,))), n_c)
    cot_all = []
    for part in range(PARTS):
        value = cot_rows[:, :, part][None, None]
        axis = ("x", "y")[1 - part % 2]
        cot_all.append(gather_joined(value, axis, ("y", "x").index(axis)))
    cot_all, attention = tie(cot_all, attention)
    for part in range(PARTS):
        axis = ("x", "y")[part % 2]
        value = gather_joined(cot_all[part], axis, ("y", "x").index(axis))
        cot_all[part] = value.reshape(n_c, n_g, n_c, sub, dim // n_c)

    own_inputs = lax.dynamic_slice_in_dim(inputs, at_c * own_rows, own_rows, 0)
    own_blocks[0][2:], attention = tie(own_blocks[0][2:], attention)
    hidden = own_inputs + attention
    second_scale = lax.rsqrt(jnp.mean(hidden * hidden, axis=-1, keepdims=True) + epsilon)
    unit_2 = hidden * second_scale
    normed_own = (unit_2 * gain_2).astype(BF16)

    def gather_cols(value):
        sides = []
        for side, order in enumerate((("y", "x"), ("x", "y"))):
            half = value[..., side * (dim // 2) : (side + 1) * (dim // 2)]
            for axis in order:
                half = gather_joined(half, axis, 1 + ("y", "x").index(axis))
            sides.append(half)
        return jnp.concatenate(sides, axis=-1).reshape(-1, dim)

    routed_gu, routed_d = own_blocks[1:]
    halves = [normed_own[part * sub : (part + 1) * sub][None] for part in range(PARTS)]
    halves[0] = gather_joined(halves[0], "g", 0)
    halves[0], halves[1], routed_gu[1] = tie(halves[0], halves[1], routed_gu[1])
    halves[1] = gather_joined(halves[1], "g", 0)
    normed_parts = [gather_cols(halves[0][:, None, None])]
    normed_parts[0], halves[1], routed_gu[2:3], cot_all = tie(
        normed_parts[0], halves[1], routed_gu[2:3], cot_all
    )
    normed_parts.append(gather_cols(halves[1][:, None, None]))
    normed_parts[1], routed_gu[3:], routed_d[1] = tie(
        normed_parts[1], routed_gu[3:], routed_d[1]
    )
    own_cot = [
        lax.dynamic_index_in_dim(cot[:, 0], at_c, 1, keepdims=False) for cot in cot_all
    ]
    own_cot = jnp.concatenate(own_cot, axis=1)
    own_cot = jnp.stack([pick(own_cot, at_c ^ c) for c in range(n_c)], axis=1)
    own_cot = own_cot.reshape(own_rows, dim)

    def own_core(grad, after=None):
        other = swap(grad[1], "k")
        grad = grad[0]
        if after is not None:
            grad, _ = tie(grad, after)
        return (grad.astype(F32) + other.astype(F32)).astype(BF16)

    def send_slices(both):
        return [shift_by(both[shift], "g", shift) for shift in range(n_g)]

    def place_slices(moved, kinds):
        moved = jnp.stack(moved)
        moved = jnp.stack([pick(moved, at_g ^ source) for source in range(n_g)])
        return [
            moved[:, i * (moved.shape[1] // kinds) :][:, : moved.shape[1] // kinds]
            for i in range(kinds)
        ]

    def place_s(value):
        return value[:, :f_shared].reshape(n_g * f_shared, d_own)

    def place_e(value):
        value = value[:, :f_experts].reshape(n_g, local_experts, f_routed, d_own)
        return value.transpose(1, 0, 2, 3).reshape(local_experts, n_g * f_routed, d_own)

    logit_low = jnp.zeros((EXTRA, dim), BF16).at[:2].set(logit_w.astype(BF16)[None])
    mixing_parts = mixing_own.reshape(n_g, n_c, PARTS, sub, local_experts)
    mixing_parts = jnp.stack([pick(mixing_parts, at_g ^ shift) for shift in range(n_g)])
    mixing_parts = jnp.stack([pick(mixing_parts, at_c ^ c, 1) for c in range(n_c)], axis=1)
    mixing_parts = jnp.pad(mixing_parts, ((0, 0),) * 4 + ((0, 8 - local_experts),))
    def blocks_of(values):
        return values + [swap(value, "k") for value in values]

    blocks_s = blocks_of(own_blocks[0])
    passes_s = [
        ffn_pass(sizes_s, meta, normed_parts[part], cot_all[part], logit_low, blocks_s, [])
        for part in range(PARTS)
    ]
    kinds = (False, False, True)
    grad_s, logit_sum = weight_grad(
        sizes_s, meta, kinds, [[p[i] for p in passes_s] for i in (3, 4, 2)], normed_parts, cot_all
    )
    logit_sum = logit_sum[0]
    sums = [[passes_s[part][0], passes_s[part][1]] for part in range(PARTS)]
    sums[0], grad_s = tie(sums[0], grad_s)
    own_blocks[2], sums[1] = tie(own_blocks[2], sums[1])
    blocks_e = blocks_of(own_blocks[1]) + blocks_of(own_blocks[2])
    passes = []
    for part in range(PARTS):
        if part == 1:
            both_s = own_core(grad_s, passes[0][2][:16, :128])
            sums[1], both_s = tie(sums[1], both_s)
        passes.append(
            ffn_pass(
                sizes_e,
                meta,
                normed_parts[part],
                cot_all[part],
                mixing_parts[:, :, part].reshape(-1, 8),
                blocks_e,
                sums[part],
            )
        )
    moved_s = send_slices(both_s)

    def split_sides(partial):
        part = partial.reshape(n_g, n_y, n_x, sub, dim)
        return [part[..., : dim // 2], part[..., dim // 2 :]]

    def scatter_axis(value, axis, at, after=None):
        bit = 1
        while bit < lax.axis_size(axis):
            value = halve(value, axis, at, bit, after)
            bit *= 2
        return lax.index_in_dim(value, 0, at, keepdims=False)

    def cols_first(sides, after=None):
        return [scatter_axis(sides[0], "x", 2, after), scatter_axis(sides[1], "y", 1, after)]

    def cols_second(sides):
        sides = [scatter_axis(sides[0], "y", 1), scatter_axis(sides[1], "x", 1)]
        return jnp.concatenate(sides, axis=-1)

    def chips_steps(value):
        bit = 1
        while 2 * bit < n_g:
            value = halve(value, "g", 0, bit)
            bit *= 2
        return value

    def chips_last(value, after=None):
        other = shift_by(value[1], "g", n_g // 2)
        keep = value[0]
        if after is not None:
            keep, _ = tie(keep, after)
        return keep.astype(F32) + other.astype(F32)

    acts, gates, ups = ([parts[i] for parts in passes] for i in (2, 3, 4))
    first = cols_first(split_sides(passes[0][1]), passes[1][2][:16, :128])
    first, acts = tie(first, acts)
    (grad_d,) = weight_grad(sizes_e, meta, (True,), [acts], normed_parts, cot_all)
    first = cols_second(first)
    second = cols_first(split_sides(passes[1][1]))
    first, second, gates, grad_d = tie(first, second, gates, grad_d)
    (grad_gu,) = weight_grad(sizes_e, meta, (False, False), [gates, ups], normed_parts, cot_all)
    first = chips_steps(first)
    second = cols_second(second)
    both_d = own_core(grad_d)
    first, second, both_d, moved_s[1:3], grad_gu = tie(first, second, both_d, moved_s[1:3], grad_gu)
    moved_d = send_slices(both_d)
    first = chips_last(first)
    second = chips_steps(second)
    both_gu = own_core(grad_gu)
    first, second, both_gu = tie(first, second, both_gu)
    second = chips_last(second)
    out_sides = [cols_first(split_sides(parts[0])) for parts in passes]
    moved_gu = send_slices(both_gu)
    normed_grad_2 = jnp.concatenate([first, second], axis=0)
    normed_grad_2, moved_s[3:] = tie(normed_grad_2, moved_s[3:])
    hidden_part, gain_2_sum = norm_back(normed_grad_2, unit_2, second_scale, gain_2)
    hidden_grad = own_cot.astype(F32) + hidden_part
    attn_grad = col_gather(hidden_grad.astype(BF16), n_c).reshape(span, dim)
    attn_grad, moved_d[1:] = tie(attn_grad, moved_d[1:])
    gate_s, up_s, down_s = (place_s(value) for value in place_slices(moved_s, 3))
    down_e = place_e(place_slices(moved_d, 1)[0])

    out_grad = dot(attn_grad, mixed, ((0,), (0,)))
    mixed_grad = dot(attn_grad, out_w, ((1,), (1,))).astype(BF16).reshape(head_shape)
    out_sides, mixed_grad = tie(out_sides, mixed_grad)
    out_parts = [cols_second(sides) for sides in out_sides]
    prob_grad = einsum("bqhd,bkhd->bhqk", mixed_grad, value_low)
    value_grad = einsum("bhqk,bqhd->bkhd", prob_low, mixed_grad).astype(BF16)
    center = jnp.sum(prob_grad * probabilities, axis=-1, keepdims=True)
    score_grad = (probabilities * (prob_grad - center) * (1.0 / math.sqrt(HEAD_DIM))).astype(BF16)
    out_parts, score_grad, moved_gu[1] = tie(out_parts, score_grad, moved_gu[1])
    out_parts = [chips_steps(part) for part in out_parts]
    query_grad = rotate(einsum("bhqk,bkhd->bqhd", score_grad, key_rot), cosine, -sine).astype(BF16)
    key_grad = rotate(einsum("bhqk,bqhd->bkhd", score_grad, query_rot), cosine, -sine).astype(BF16)
    qkv_grad = jnp.concatenate(
        [part.reshape(span, width) for part in (query_grad, key_grad, value_grad)], axis=1
    )
    qkv_grad, out_parts, moved_gu[2:3] = tie(qkv_grad, out_parts, moved_gu[2:3])
    qkv_sum = dot(normed_1, qkv_grad, ((0,), (0,)))
    normed_grad_1 = col_sum(dot(qkv_grad, qkv, ((1,), (1,))), n_c)
    normed_grad_1, moved_gu[3:] = tie(normed_grad_1, moved_gu[3:])
    gate_e, up_e = (place_e(value) for value in place_slices(moved_gu, 2))
    own_scale = lax.dynamic_slice_in_dim(first_scale, at_c * own_rows, own_rows, 0)
    rows_part, gain_1_sum = norm_back(normed_grad_1, own_inputs * own_scale, own_scale, gain_1)
    token_rows = (hidden_grad + rows_part).astype(BF16)
    token_grad = rows_to_features(token_rows, n_c).astype(F32)

    out_rows = [chips_last(part, token_rows[:16, :128]) for part in out_parts]
    out_rows = jnp.concatenate(out_rows, axis=0)
    result = rows_to_features((hidden + out_rows).astype(BF16), n_c)

    sums = jnp.stack([gain_1_sum, gain_2_sum, logit_sum]).reshape(3, n_row, d_own)
    sums = jnp.broadcast_to(sums.transpose(1, 0, 2)[:, None], (n_row, n_c, 3, d_own))
    sums = lax.all_to_all(sums.reshape(n_row * n_c, 3, d_own), ALL, 0, 0, tiled=True)
    sums = jnp.sum(sums, axis=0)

    out_w_grad = lax.psum_scatter(out_grad.astype(BF16), ROW, scatter_dimension=0, tiled=True)
    qkv_own = lax.psum_scatter(qkv_sum.astype(BF16), ROW, scatter_dimension=0, tiled=True)
    qkv_own = qkv_own.astype(F32)
    return (
        result,
        token_grad,
        sums[0],
        qkv_own[:, :width],
        qkv_own[:, width : 2 * width],
        qkv_own[:, 2 * width :],
        out_w_grad.T.astype(F32),
        sums[1],
        gate_s.T.astype(F32),
        up_s.T.astype(F32),
        down_s.astype(F32),
        sums[2],
        gate_e.transpose(2, 0, 1).astype(F32),
        up_e.transpose(2, 0, 1).astype(F32),
        down_e.astype(F32),
    )


def solution(mesh):
    n_row, n_col = mesh.shape["row"], mesh.shape["col"]
    inner = Mesh(mesh.devices.reshape(n_row // 2, 2, n_col // 2, 2), ALL)
    return jax.shard_map(
        shards,
        mesh=inner,
        in_specs=(
            P(None, ROW, COL),
            P(None, ROW, None),
            P(None, ROW, None),
            P(None, ROW),
            P(ROW),
            P(ROW, COL),
            P(ROW, COL),
            P(ROW, COL),
            P(COL, ROW),
            P(ROW),
            P(ROW, COL),
            P(ROW, COL),
            P(COL, ROW),
            P(ROW),
            P(ROW, COL, None),
            P(ROW, COL, None),
            P(COL, None, ROW),
            P(None, ROW, COL),
        ),
        out_specs=(
            P(None, ROW, COL),
            P(None, ROW, COL),
            P(ROW),
            P(ROW, COL),
            P(ROW, COL),
            P(ROW, COL),
            P(COL, ROW),
            P(ROW),
            P(ROW, COL),
            P(ROW, COL),
            P(COL, ROW),
            P(ROW),
            P(ROW, COL, None),
            P(ROW, COL, None),
            P(COL, None, ROW),
        ),
        check_vma=False,
    )
```

```python
import functools
import math

import jax
import jax.numpy as jnp
from jax import lax
from jax.experimental import pallas as pl
from jax.experimental.pallas import tpu as pltpu
from jax.sharding import Mesh, PartitionSpec as P

HEAD_DIM = 128
EXPERTS = 8
PROMPTS = 2
CONTS = 2
CONT_LEN = 64
PROMPT_LEN = 64

epsilon = 1e-06
rope_base = 1000000.0
masked_score = -1000000000.0

F32 = jnp.float32
BF16 = jnp.bfloat16
COL = ("y", "x")
ROW = ("g", "k")
ALL = ("g", "k", "y", "x")


def block_layout(groups, row_count):
    token_index = jnp.arange(row_count, dtype=jnp.int32)
    prompt_rows = PROMPTS * PROMPT_LEN
    is_prompt = token_index < prompt_rows
    cont_offset = jnp.maximum(token_index - prompt_rows, 0)
    cont_number = cont_offset // CONT_LEN
    segment = jnp.where(is_prompt, token_index // PROMPT_LEN, PROMPTS + cont_number)
    position = jnp.where(is_prompt, token_index % PROMPT_LEN, PROMPT_LEN + cont_offset % CONT_LEN)
    cont_picks = (cont_number[:, None] == jnp.arange(CONTS, dtype=jnp.int32)[None, :]).astype(
        jnp.int32
    )
    source = jnp.where(
        is_prompt[None], segment[None], jnp.sum(cont_picks[None] * groups[:, None, :], axis=2)
    )
    same_segment = (segment[:, None] == segment[None, :]) & (position[None, :] <= position[:, None])
    context = (
        jnp.logical_not(is_prompt)[None, :, None]
        & is_prompt[None, None, :]
        & (source[:, :, None] == segment[None, None, :])
    )
    return (same_segment[None] | context, position)


def rotary_tables(position):
    half_dim = HEAD_DIM // 2
    frequency = rope_base ** (-(2.0 * jnp.arange(half_dim, dtype=F32)) / HEAD_DIM)
    angles = position.astype(F32)[:, None] * frequency[None, :]
    cosine = jnp.cos(angles)
    sine = jnp.sin(angles)
    return (cosine[None, :, None, :], sine[None, :, None, :])


def rotate(values, cosine, sine):
    first, second = jnp.split(values, 2, axis=-1)
    return jnp.concatenate([first * cosine - second * sine, second * cosine + first * sine], -1)


def dot(left, right, dims):
    return lax.dot_general(left, right, (dims, ((), ())), preferred_element_type=F32)


PARTS = 2
EXTRA = 16


def ffn_kernel(sizes, groups, meta, rows_ref, cot_ref, side_ref, *refs):
    n_g, f_pad, f_one, d_own = sizes
    blocks = refs[: groups * 2 * n_g]
    sums = refs[groups * 2 * n_g : -8]
    out_ref, normed_ref, act_ref, gate_ref, up_ref, w_gu, w_down, sems = refs[-8:]
    g_at, k_at, c_at = meta[0], meta[1], meta[2]
    shared = groups == 1

    @pl.when(pl.program_id(0) == 0)
    def _():
        copies = []
        for half in range(2):
            for shift in range(n_g):
                at = half * n_g + shift
                column = 2 * (g_at ^ shift) + (k_at ^ half)
                lanes = pl.ds(pl.multiple_of(column * d_own, d_own), d_own)
                if shared:
                    both, down = blocks[at].at[: 2 * f_pad], blocks[at].at[2 * f_pad :]
                else:
                    both, down = blocks[at], blocks[2 * n_g + at]
                copies.append(
                    pltpu.make_async_copy(both, w_gu.at[: 2 * f_pad, lanes], sems.at[2 * at])
                )
                copies.append(pltpu.make_async_copy(down, w_down.at[:, lanes], sems.at[2 * at + 1]))
        for copy in copies:
            copy.start()
        if shared:
            w_gu[2 * f_pad :, :] = side_ref[...]
        for copy in copies:
            copy.wait()

    rows = rows_ref[...]
    count = rows.shape[0]
    n_c = cot_ref.shape[0]
    cot = jnp.concatenate(
        [
            jnp.concatenate([cot_ref[c ^ c_at, 0, row ^ c_at] for row in range(n_c)], axis=0)
            for c in range(n_c)
        ],
        axis=1,
    )
    minor = ((1,), (1,))
    pre = dot(w_gu[...], rows, minor)
    down_back = dot(w_down[...], cot, minor)
    gate_pre, up_pre = pre[:f_pad], pre[f_pad : 2 * f_pad]
    if shared:
        prob = jax.nn.sigmoid(pre[2 * f_pad : 2 * f_pad + 1])
        scale = jnp.broadcast_to(prob, (f_pad, count))
    else:
        full = f_pad // f_one
        pieces = [jnp.broadcast_to(side_ref[0, e : e + 1, :], (f_one, count)) for e in range(full)]
        if f_pad > full * f_one:
            pieces.append(jnp.zeros((f_pad - full * f_one, count), F32))
        scale = jnp.concatenate(pieces, axis=0)
    sigma = jax.nn.sigmoid(gate_pre)
    silu = gate_pre * sigma
    act = silu * up_pre
    act_grad = down_back * scale
    act_low = (act * scale).astype(BF16)
    gate_low = (act_grad * up_pre * sigma * (1.0 + gate_pre * (1.0 - sigma))).astype(BF16)
    up_low = (act_grad * silu).astype(BF16)
    act_ref[...] = act_low
    gate_ref[:f_pad, :] = gate_low
    up_ref[...] = up_low
    both = [gate_low, up_low]
    if shared:
        prob_part = jnp.sum(act * down_back, axis=0, keepdims=True)
        logit_part = prob_part * prob * (1.0 - prob)
        logit_high = logit_part.astype(BF16).astype(F32)
        logit_rows = jnp.concatenate(
            [logit_high, logit_part - logit_high, jnp.zeros((EXTRA - 2, count), F32)], axis=0
        ).astype(BF16)
        gate_ref[f_pad:, :] = logit_rows
        both.append(logit_rows)
    major = ((0,), (0,))
    out = dot(act_low, w_down[...], major)
    normed = dot(jnp.concatenate(both, axis=0), w_gu[...], major)
    if sums:
        out = out + sums[0][...].astype(F32)
        normed = normed + sums[1][...].astype(F32)
    out_ref[...] = out.astype(BF16)
    normed_ref[...] = normed.astype(BF16)


def ffn_pass(sizes, meta, rows, cot, side, blocks, sums):
    n_g, f_pad, _, d_own = sizes
    total, dim = rows.shape
    n_c, _, _, sub, cw = cot.shape
    tile = n_c * sub
    groups = len(blocks) // (2 * n_g)
    extra = EXTRA if groups == 1 else 0
    flat = lambda i, m: (i, 0)
    wide = lambda i, m: (0, i)
    if groups == 1:
        side_spec = pl.BlockSpec((EXTRA, dim), lambda i, m: (0, 0))
    else:
        side = side.reshape(-1, tile, 8).transpose(0, 2, 1)
        side_spec = pl.BlockSpec((1, 8, tile), lambda i, m: (i, 0, 0))
    return pl.pallas_call(
        functools.partial(ffn_kernel, sizes, groups),
        grid_spec=pltpu.PrefetchScalarGridSpec(
            num_scalar_prefetch=1,
            grid=(n_g,),
            in_specs=[
                pl.BlockSpec((tile, dim), flat),
                pl.BlockSpec((n_c, 1, n_c, sub, cw), lambda i, m: (0, i, 0, 0, 0)),
                side_spec,
            ]
            + [pl.BlockSpec(memory_space=pl.ANY)] * len(blocks)
            + [pl.BlockSpec((tile, dim), flat)] * len(sums),
            out_specs=[
                pl.BlockSpec((tile, dim), flat),
                pl.BlockSpec((tile, dim), flat),
                pl.BlockSpec((f_pad, tile), wide),
                pl.BlockSpec((f_pad + extra, tile), wide),
                pl.BlockSpec((f_pad, tile), wide),
            ],
            scratch_shapes=[
                pltpu.VMEM((2 * f_pad + extra, dim), BF16),
                pltpu.VMEM((f_pad, dim), BF16),
                pltpu.SemaphoreType.DMA((4 * n_g,)),
            ],
        ),
        out_shape=[
            jax.ShapeDtypeStruct((total, dim), BF16),
            jax.ShapeDtypeStruct((total, dim), BF16),
            jax.ShapeDtypeStruct((f_pad, total), BF16),
            jax.ShapeDtypeStruct((f_pad + extra, total), BF16),
            jax.ShapeDtypeStruct((f_pad, total), BF16),
        ],
        compiler_params=pltpu.CompilerParams(
            dimension_semantics=("arbitrary",), vmem_limit_bytes=60 * 1024 * 1024
        ),
        cost_estimate=pl.CostEstimate(
            flops=12 * total * dim * f_pad,
            bytes_accessed=(8 + 4 * len(sums)) * total * dim + 6 * total * f_pad + 6 * f_pad * dim,
            transcendentals=total * f_pad,
        ),
        name="ffn_pass",
    )(meta, rows, cot, side, *blocks, *sums)


def grad_kernel(parts, kinds, f_pad, meta, *refs):
    lefts, refs = refs[: parts * len(kinds)], refs[parts * len(kinds) :]
    values = {}
    for cot in sorted(set(kinds)):
        rights, refs = refs[:parts], refs[parts:]
        if cot:
            _, n_g, n_c, _, _ = rights[0].shape
            order = [(g, c) for g in range(n_g) for c in range(n_c)]
            values[cot] = [
                jnp.concatenate([right[0, g, c ^ meta[2]] for g, c in order], axis=0)
                for right in rights
            ]
        else:
            values[cot] = [right[...] for right in rights]
    for i, cot in enumerate(kinds):
        total = None
        for left, value in zip(lefts[i * parts : (i + 1) * parts], values[cot]):
            term = dot(left[...], value, ((1,), (0,)))
            total = term if total is None else total + term
        refs[0][0, 0, i * f_pad : (i + 1) * f_pad] = total[:f_pad].astype(BF16)
        if total.shape[0] > f_pad:
            refs[1][...] = jnp.broadcast_to(
                total[f_pad : f_pad + 1] + total[f_pad + 1 : f_pad + 2], refs[1].shape
            )


def weight_grad(sizes, meta, kinds, lefts, normed, cots):
    n_g, f_pad, _, d_own = sizes
    parts = len(normed)
    part_rows, dim = normed[0].shape
    extra = max(value[0].shape[0] for value in lefts) > f_pad
    n_c, _, _, sub, cw = cots[0].shape
    per = cw // d_own
    arrays, specs = [], []
    for values in lefts:
        arrays += values
        specs += [pl.BlockSpec(values[0].shape, lambda j, m: (0, 0))] * parts
    if False in kinds:
        arrays += normed
        specs += [pl.BlockSpec((part_rows, d_own), lambda j, m: (0, j))] * parts
    if True in kinds:
        arrays += cots
        specs += [
            pl.BlockSpec(
                (1, n_g, n_c, sub, d_own), lambda j, m: ((j // per) ^ m[2], 0, 0, 0, j % per)
            )
        ] * parts
    f_out = len(kinds) * f_pad
    out_specs = [
        pl.BlockSpec((1, 1, f_out, d_own), lambda j, m: ((j % 2) ^ m[1], (j // 2) ^ m[0], 0, 0))
    ]
    out_shape = [jax.ShapeDtypeStruct((2, n_g, f_out, d_own), BF16)]
    if extra:
        out_specs.append(pl.BlockSpec((8, d_own), lambda j, m: (0, j)))
        out_shape.append(jax.ShapeDtypeStruct((8, dim), F32))
    return pl.pallas_call(
        functools.partial(grad_kernel, parts, kinds, f_pad),
        grid_spec=pltpu.PrefetchScalarGridSpec(
            num_scalar_prefetch=1, grid=(2 * n_g,), in_specs=specs, out_specs=out_specs
        ),
        out_shape=out_shape,
        compiler_params=pltpu.CompilerParams(
            dimension_semantics=("arbitrary",), vmem_limit_bytes=56 * 1024 * 1024
        ),
        cost_estimate=pl.CostEstimate(
            flops=2 * parts * part_rows * dim * f_out,
            bytes_accessed=2 * parts * part_rows * (dim + f_out) + 2 * f_out * dim,
            transcendentals=0,
        ),
        name="weight_grad",
    )(meta, *arrays)


def tie(*values):
    return lax.optimization_barrier(values)


def norm_back(normed_grad, unit_rows, scale, gain):
    weighted = normed_grad * gain
    rows_grad = scale * (
        weighted - unit_rows * jnp.mean(weighted * unit_rows, axis=-1, keepdims=True)
    )
    return (rows_grad, jnp.sum(normed_grad * unit_rows, axis=0))


def swap(value, axis):
    return lax.ppermute(value, axis, [(0, 1), (1, 0)])


def shift_by(value, axis, shift):
    if shift == 0:
        return value
    return lax.ppermute(value, axis, [(i, i ^ shift) for i in range(lax.axis_size(axis))])


def gather_joined(value, axis, at):
    bit = lax.axis_size(axis) // 2
    while bit:
        shape = value.shape[:at] + (2 * value.shape[at],) + value.shape[at + 1 :]
        value = jnp.stack([value, shift_by(value, axis, bit)], axis=at + 1).reshape(shape)
        bit //= 2
    return value


def halve(value, axis, at, bit, after=None):
    size = value.shape[at]
    shape = value.shape[:at] + (size // 2, 2) + value.shape[at + 1 :]
    pair = value.reshape(shape)
    keep, send = (lax.index_in_dim(pair, i, at + 1, keepdims=False) for i in range(2))
    other = shift_by(send, axis, bit)
    if after is not None:
        keep, _ = tie(keep, after)
    return (keep.astype(F32) + other.astype(F32)).astype(BF16)


def col_gather(value, count):
    spread = jnp.broadcast_to(value[None], (count,) + value.shape)
    return lax.all_to_all(spread, COL, 0, 0, tiled=True)


def col_sum(partial, count):
    parts = partial.astype(BF16).reshape((count, -1) + partial.shape[1:])
    return jnp.sum(lax.all_to_all(parts, COL, 0, 0, tiled=True).astype(F32), axis=0)


def rows_to_features(rows, count):
    row_count, width = rows.shape
    parts = rows.reshape(row_count, count, width // count).transpose(1, 0, 2)
    moved = lax.all_to_all(parts, COL, 0, 0, tiled=True)
    blocks = moved.reshape(2, row_count * count // 2, width // count)
    return lax.all_to_all(blocks, "k", 0, 0, tiled=True)


def shards(
    tokens,
    routes,
    route_weights,
    group_ids,
    first_gain,
    query_weight,
    key_weight,
    value_weight,
    output_weight,
    second_gain,
    shared_gate,
    shared_up,
    shared_down,
    shared_logit,
    expert_gate,
    expert_up,
    expert_down,
    cotangent,
):
    n_g = lax.axis_size("g")
    n_c = lax.axis_size("y") * lax.axis_size("x")
    n_y, n_x = lax.axis_size("y"), lax.axis_size("x")
    n_row = 2 * n_g
    at_g, at_k = lax.axis_index("g"), lax.axis_index("k")
    at_c = lax.axis_index(COL)
    block = tokens.shape[1]
    dim = query_weight.shape[0] * n_row
    d_own = query_weight.shape[0]
    width = query_weight.shape[1]
    heads = width // HEAD_DIM
    local_experts = expert_gate.shape[1]
    span = 2 * block
    total = n_g * span
    own_rows = span // n_c
    pick = lambda array, index, axis=0: lax.dynamic_index_in_dim(array, index, axis, keepdims=False)

    labels = jnp.arange(EXPERTS, dtype=jnp.int32)
    mixing = jnp.sum(
        jnp.where(
            routes[:, None] == labels[None, :, None, None], route_weights[:, None], 0.0
        ),
        axis=-1,
    )
    small = jnp.concatenate(
        [
            mixing.reshape(2 * EXPERTS, block),
            jnp.zeros((8, block), F32)
            .at[0, :d_own].set(first_gain.astype(F32))
            .at[1, :d_own].set(second_gain.astype(F32))
            .at[2, :d_own].set(shared_logit.astype(F32))
            .at[3, : 2 * CONTS].set(group_ids.astype(F32).reshape(-1)),
        ],
        axis=0,
    )
    small_all = lax.all_to_all(
        jnp.broadcast_to(small[None], (n_row,) + small.shape), ROW, 0, 0, tiled=True
    )
    f_shared = shared_gate.shape[1] // n_g
    f_routed = expert_gate.shape[2] // n_g
    f_experts = local_experts * f_routed
    f_one, f_two = -(-f_shared // 16) * 16, -(-f_experts // 16) * 16
    sizes_s = (n_g, f_one, f_shared, d_own)
    sizes_e = (n_g, f_two, f_routed, d_own)
    meta = jnp.stack([at_g, at_k, at_c]).astype(jnp.int32)

    def fill(value, size):
        return jnp.pad(value, ((0, 0), (0, size - value.shape[1]), (0, 0)))

    def slices_s(value):
        return fill(value.reshape(n_g, f_shared, d_own), f_one)

    def slices_e(value):
        value = value.reshape(local_experts, n_g, f_routed, d_own).transpose(1, 0, 2, 3)
        return fill(value.reshape(n_g, f_experts, d_own), f_two)

    weight_slices = [
        jnp.concatenate([slices_s(w) for w in (shared_gate.T, shared_up.T, shared_down)], axis=1),
        jnp.concatenate([slices_e(w.transpose(1, 2, 0)) for w in (expert_gate, expert_up)], axis=1),
        slices_e(expert_down),
    ]
    picked = [[pick(value, at_g ^ shift) for shift in range(n_g)] for value in weight_slices]
    qkv = lax.all_gather(
        jnp.concatenate([query_weight, key_weight, value_weight], axis=1), ROW, axis=0, tiled=True
    )
    out_w = lax.all_gather(output_weight, ROW, axis=1, tiled=True)
    picked[0], qkv, small_all = tie(picked[0], qkv, small_all)
    own_blocks = [
        [shift_by(value, "g", shift) for shift, value in enumerate(values)] for values in picked
    ]

    token_part = lax.all_to_all(tokens, "k", 0, 0, tiled=True).reshape(span, -1)
    cot_part = lax.all_to_all(cotangent, "k", 0, 0, tiled=True).reshape(span, -1)

    sub = own_rows // PARTS
    cot_rows = cot_part.reshape(1, n_c, PARTS, sub, dim // n_c)
    far = shift_by(cot_rows, "g", n_g // 2)
    cot_rows, far, qkv = tie(cot_rows, far, qkv)
    cot_rows = jnp.concatenate([cot_rows, far], axis=0)
    bit = n_g // 4
    while bit:
        far = shift_by(cot_rows, "g", bit)
        cot_rows = jnp.stack([cot_rows, far], axis=1).reshape((-1,) + cot_rows.shape[1:])
        bit //= 2
    inputs = col_gather(token_part, n_c).reshape(n_c, span, -1).transpose(1, 0, 2)
    inputs = inputs.reshape(span, dim).astype(F32)

    gain_1 = small_all[:, 16, :d_own].reshape(dim)
    gain_2 = small_all[:, 17, :d_own].reshape(dim)
    logit_w = small_all[:, 18, :d_own].reshape(dim)
    groups_all = small_all[:, 19, : 2 * CONTS].reshape(n_g, 2, 2, CONTS)
    groups = pick(pick(groups_all, at_g), at_k, 1).astype(jnp.int32)
    mixing_all = small_all[:, : 2 * EXPERTS].reshape(n_row, 2, EXPERTS, block)
    mixing_own = lax.dynamic_slice_in_dim(
        pick(mixing_all, at_k, 1), at_c * local_experts, local_experts, 1
    )
    mixing_own = mixing_own.transpose(0, 2, 1).reshape(total, local_experts)

    first_scale = lax.rsqrt(jnp.mean(inputs * inputs, axis=-1, keepdims=True) + epsilon)
    normed_1 = (inputs * first_scale * gain_1).astype(BF16)
    projected = dot(normed_1, qkv, ((1,), (0,)))
    allowed, position = block_layout(groups, block)
    cosine, sine = rotary_tables(position)
    head_shape = (2, block, heads, HEAD_DIM)
    query_rot = rotate(projected[:, :width].reshape(head_shape), cosine, sine).astype(BF16)
    key_rot = rotate(projected[:, width : 2 * width].reshape(head_shape), cosine, sine).astype(BF16)
    value_low = projected[:, 2 * width :].reshape(head_shape).astype(BF16)

    def einsum(form, left, right):
        return jnp.einsum(form, left, right, preferred_element_type=F32)

    scores = jnp.where(
        allowed[:, None],
        einsum("bqhd,bkhd->bhqk", query_rot, key_rot) * (1.0 / math.sqrt(HEAD_DIM)),
        masked_score,
    )
    peak = jnp.max(scores, axis=-1, keepdims=True)
    exp_scores = jnp.exp(scores - peak)
    probabilities = exp_scores / jnp.sum(exp_scores, axis=-1, keepdims=True)
    prob_low = probabilities.astype(BF16)
    mixed = einsum("bhqk,bkhd->bqhd", prob_low, value_low).astype(BF16).reshape(span, width)
    cot_rows, mixed, own_blocks[0][1] = tie(cot_rows, mixed, own_blocks[0][1])
    attention = col_sum(dot(mixed, out_w, ((1,), (0,))), n_c)
    cot_all = []
    for part in range(PARTS):
        value = cot_rows[:, :, part][None, None]
        axis = ("x", "y")[1 - part % 2]
        cot_all.append(gather_joined(value, axis, ("y", "x").index(axis)))
    own_inputs = lax.dynamic_slice_in_dim(inputs, at_c * own_rows, own_rows, 0)
    own_blocks[0][2:], attention = tie(own_blocks[0][2:], attention)
    hidden = own_inputs + attention
    second_scale = lax.rsqrt(jnp.mean(hidden * hidden, axis=-1, keepdims=True) + epsilon)
    unit_2 = hidden * second_scale
    normed_own = (unit_2 * gain_2).astype(BF16)

    def gather_cols(value):
        sides = []
        for side, order in enumerate((("y", "x"), ("x", "y"))):
            half = value[..., side * (dim // 2) : (side + 1) * (dim // 2)]
            for axis in order:
                half = gather_joined(half, axis, 1 + ("y", "x").index(axis))
            sides.append(half)
        return jnp.concatenate(sides, axis=-1).reshape(-1, dim)

    routed_gu, routed_d = own_blocks[1:]
    halves = [normed_own[part * sub : (part + 1) * sub][None] for part in range(PARTS)]
    halves[0] = gather_joined(halves[0], "g", 0)
    halves[0], halves[1], routed_gu[1], cot_all = tie(
        halves[0], halves[1], routed_gu[1], cot_all
    )
    for part in range(PARTS):
        axis = ("x", "y")[part % 2]
        value = gather_joined(cot_all[part], axis, ("y", "x").index(axis))
        cot_all[part] = value.reshape(n_c, n_g, n_c, sub, dim // n_c)
    halves[1] = gather_joined(halves[1], "g", 0)
    normed_parts = [gather_cols(halves[0][:, None, None])]
    normed_parts[0], halves[1], routed_gu[2:3], cot_all = tie(
        normed_parts[0], halves[1], routed_gu[2:3], cot_all
    )
    normed_parts.append(gather_cols(halves[1][:, None, None]))
    normed_parts[1], routed_gu[3:], routed_d[1] = tie(
        normed_parts[1], routed_gu[3:], routed_d[1]
    )
    own_cot = [
        lax.dynamic_index_in_dim(cot[:, 0], at_c, 1, keepdims=False) for cot in cot_all
    ]
    own_cot = jnp.concatenate(own_cot, axis=1)
    own_cot = jnp.stack([pick(own_cot, at_c ^ c) for c in range(n_c)], axis=1)
    own_cot = own_cot.reshape(own_rows, dim)

    def own_core(grad, after=None):
        other = swap(grad[1], "k")
        grad = grad[0]
        if after is not None:
            grad, _ = tie(grad, after)
        return (grad.astype(F32) + other.astype(F32)).astype(BF16)

    def send_slices(both):
        return [shift_by(both[shift], "g", shift) for shift in range(n_g)]

    def place_slices(moved, kinds):
        moved = jnp.stack(moved)
        moved = jnp.stack([pick(moved, at_g ^ source) for source in range(n_g)])
        return [
            moved[:, i * (moved.shape[1] // kinds) :][:, : moved.shape[1] // kinds]
            for i in range(kinds)
        ]

    def place_s(value):
        return value[:, :f_shared].reshape(n_g * f_shared, d_own)

    def place_e(value):
        value = value[:, :f_experts].reshape(n_g, local_experts, f_routed, d_own)
        return value.transpose(1, 0, 2, 3).reshape(local_experts, n_g * f_routed, d_own)

    logit_low = jnp.zeros((EXTRA, dim), BF16).at[:2].set(logit_w.astype(BF16)[None])
    mixing_parts = mixing_own.reshape(n_g, n_c, PARTS, sub, local_experts)
    mixing_parts = jnp.stack([pick(mixing_parts, at_g ^ shift) for shift in range(n_g)])
    mixing_parts = jnp.stack([pick(mixing_parts, at_c ^ c, 1) for c in range(n_c)], axis=1)
    mixing_parts = jnp.pad(mixing_parts, ((0, 0),) * 4 + ((0, 8 - local_experts),))
    def blocks_of(values):
        return values + [swap(value, "k") for value in values]

    blocks_s = blocks_of(own_blocks[0])
    passes_s = [
        ffn_pass(sizes_s, meta, normed_parts[part], cot_all[part], logit_low, blocks_s, [])
        for part in range(PARTS)
    ]
    kinds = (False, False, True)
    grad_s, logit_sum = weight_grad(
        sizes_s, meta, kinds, [[p[i] for p in passes_s] for i in (3, 4, 2)], normed_parts, cot_all
    )
    logit_sum = logit_sum[0]
    sums = [[passes_s[part][0], passes_s[part][1]] for part in range(PARTS)]
    sums[0], grad_s = tie(sums[0], grad_s)
    own_blocks[2], sums[1] = tie(own_blocks[2], sums[1])
    blocks_e = blocks_of(own_blocks[1]) + blocks_of(own_blocks[2])
    passes = []
    for part in range(PARTS):
        if part == 1:
            both_s = own_core(grad_s, passes[0][2][:16, :128])
            sums[1], both_s = tie(sums[1], both_s)
        passes.append(
            ffn_pass(
                sizes_e,
                meta,
                normed_parts[part],
                cot_all[part],
                mixing_parts[:, :, part].reshape(-1, 8),
                blocks_e,
                sums[part],
            )
        )
    moved_s = send_slices(both_s)

    def split_sides(partial):
        part = partial.reshape(n_g, n_y, n_x, sub, dim)
        return [part[..., : dim // 2], part[..., dim // 2 :]]

    def scatter_axis(value, axis, at, after=None):
        bit = 1
        while bit < lax.axis_size(axis):
            value = halve(value, axis, at, bit, after)
            bit *= 2
        return lax.index_in_dim(value, 0, at, keepdims=False)

    def cols_first(sides, after=None):
        return [scatter_axis(sides[0], "x", 2, after), scatter_axis(sides[1], "y", 1, after)]

    def cols_second(sides):
        sides = [scatter_axis(sides[0], "y", 1), scatter_axis(sides[1], "x", 1)]
        return jnp.concatenate(sides, axis=-1)

    def chips_steps(value):
        bit = 1
        while 2 * bit < n_g:
            value = halve(value, "g", 0, bit)
            bit *= 2
        return value

    def chips_last(value, after=None):
        other = shift_by(value[1], "g", n_g // 2)
        keep = value[0]
        if after is not None:
            keep, _ = tie(keep, after)
        return keep.astype(F32) + other.astype(F32)

    acts, gates, ups = ([parts[i] for parts in passes] for i in (2, 3, 4))
    first = cols_first(split_sides(passes[0][1]), passes[1][2][:16, :128])
    first, acts = tie(first, acts)
    (grad_d,) = weight_grad(sizes_e, meta, (True,), [acts], normed_parts, cot_all)
    first = cols_second(first)
    second = cols_first(split_sides(passes[1][1]))
    first, second, gates, grad_d = tie(first, second, gates, grad_d)
    (grad_gu,) = weight_grad(sizes_e, meta, (False, False), [gates, ups], normed_parts, cot_all)
    first = chips_steps(first)
    second = cols_second(second)
    both_d = own_core(grad_d)
    first, second, both_d, moved_s[1:3], grad_gu = tie(first, second, both_d, moved_s[1:3], grad_gu)
    moved_d = send_slices(both_d)
    first = chips_last(first)
    second = chips_steps(second)
    both_gu = own_core(grad_gu)
    first, second, both_gu = tie(first, second, both_gu)
    second = chips_last(second)
    out_sides = [cols_first(split_sides(parts[0])) for parts in passes]
    moved_gu = send_slices(both_gu)
    normed_grad_2 = jnp.concatenate([first, second], axis=0)
    normed_grad_2, moved_s[3:] = tie(normed_grad_2, moved_s[3:])
    hidden_part, gain_2_sum = norm_back(normed_grad_2, unit_2, second_scale, gain_2)
    hidden_grad = own_cot.astype(F32) + hidden_part
    attn_grad = col_gather(hidden_grad.astype(BF16), n_c).reshape(span, dim)
    attn_grad, moved_d[1:] = tie(attn_grad, moved_d[1:])
    gate_s, up_s, down_s = (place_s(value) for value in place_slices(moved_s, 3))
    down_e = place_e(place_slices(moved_d, 1)[0])

    out_grad = dot(attn_grad, mixed, ((0,), (0,)))
    mixed_grad = dot(attn_grad, out_w, ((1,), (1,))).astype(BF16).reshape(head_shape)
    out_sides, mixed_grad = tie(out_sides, mixed_grad)
    out_parts = [cols_second(sides) for sides in out_sides]
    prob_grad = einsum("bqhd,bkhd->bhqk", mixed_grad, value_low)
    value_grad = einsum("bhqk,bqhd->bkhd", prob_low, mixed_grad).astype(BF16)
    center = jnp.sum(prob_grad * probabilities, axis=-1, keepdims=True)
    score_grad = (probabilities * (prob_grad - center) * (1.0 / math.sqrt(HEAD_DIM))).astype(BF16)
    out_parts, score_grad, moved_gu[1] = tie(out_parts, score_grad, moved_gu[1])
    out_parts = [chips_steps(part) for part in out_parts]
    query_grad = rotate(einsum("bhqk,bkhd->bqhd", score_grad, key_rot), cosine, -sine).astype(BF16)
    key_grad = rotate(einsum("bhqk,bqhd->bkhd", score_grad, query_rot), cosine, -sine).astype(BF16)
    qkv_grad = jnp.concatenate(
        [part.reshape(span, width) for part in (query_grad, key_grad, value_grad)], axis=1
    )
    qkv_grad, moved_gu[2:3] = tie(qkv_grad, moved_gu[2:3])
    qkv_sum = dot(normed_1, qkv_grad, ((0,), (0,)))
    normed_grad_1 = col_sum(dot(qkv_grad, qkv, ((1,), (1,))), n_c)
    normed_grad_1, moved_gu[3:], out_parts = tie(normed_grad_1, moved_gu[3:], out_parts)
    gate_e, up_e = (place_e(value) for value in place_slices(moved_gu, 2))
    own_scale = lax.dynamic_slice_in_dim(first_scale, at_c * own_rows, own_rows, 0)
    rows_part, gain_1_sum = norm_back(normed_grad_1, own_inputs * own_scale, own_scale, gain_1)
    token_rows = (hidden_grad + rows_part).astype(BF16)
    token_moved = rows_to_features(token_rows, n_c)
    token_grad = token_moved.astype(F32)

    sums = jnp.stack([gain_1_sum, gain_2_sum, logit_sum]).reshape(3, n_row, d_own)
    sums = jnp.broadcast_to(sums.transpose(1, 0, 2)[:, None], (n_row, n_c, 3, d_own))
    sums = lax.all_to_all(sums.reshape(n_row * n_c, 3, d_own), ALL, 0, 0, tiled=True)
    sums = jnp.sum(sums, axis=0)

    out_rows = [chips_last(part, (token_moved[:, :16, :128], sums[:, :128])) for part in out_parts]
    out_rows = jnp.concatenate(out_rows, axis=0)
    result = rows_to_features((hidden + out_rows).astype(BF16), n_c)

    out_w_grad = lax.psum_scatter(out_grad.astype(BF16), ROW, scatter_dimension=0, tiled=True)
    qkv_own = lax.psum_scatter(qkv_sum.astype(BF16), ROW, scatter_dimension=0, tiled=True)
    qkv_own = qkv_own.astype(F32)
    return (
        result,
        token_grad,
        sums[0],
        qkv_own[:, :width],
        qkv_own[:, width : 2 * width],
        qkv_own[:, 2 * width :],
        out_w_grad.T.astype(F32),
        sums[1],
        gate_s.T.astype(F32),
        up_s.T.astype(F32),
        down_s.astype(F32),
        sums[2],
        gate_e.transpose(2, 0, 1).astype(F32),
        up_e.transpose(2, 0, 1).astype(F32),
        down_e.astype(F32),
    )


def solution(mesh):
    n_row, n_col = mesh.shape["row"], mesh.shape["col"]
    inner = Mesh(mesh.devices.reshape(n_row // 2, 2, n_col // 2, 2), ALL)
    return jax.shard_map(
        shards,
        mesh=inner,
        in_specs=(
            P(None, ROW, COL),
            P(None, ROW, None),
            P(None, ROW, None),
            P(None, ROW),
            P(ROW),
            P(ROW, COL),
            P(ROW, COL),
            P(ROW, COL),
            P(COL, ROW),
            P(ROW),
            P(ROW, COL),
            P(ROW, COL),
            P(COL, ROW),
            P(ROW),
            P(ROW, COL, None),
            P(ROW, COL, None),
            P(COL, None, ROW),
            P(None, ROW, COL),
        ),
        out_specs=(
            P(None, ROW, COL),
            P(None, ROW, COL),
            P(ROW),
            P(ROW, COL),
            P(ROW, COL),
            P(ROW, COL),
            P(COL, ROW),
            P(ROW),
            P(ROW, COL),
            P(ROW, COL),
            P(COL, ROW),
            P(ROW),
            P(ROW, COL, None),
            P(ROW, COL, None),
            P(COL, None, ROW),
        ),
        check_vma=False,
    )
```

```python
import functools
import math

import jax
import jax.numpy as jnp
from jax import lax
from jax.experimental import pallas as pl
from jax.experimental.pallas import tpu as pltpu
from jax.sharding import Mesh, PartitionSpec as P

HEAD_DIM = 128
EXPERTS = 8
PROMPTS = 2
CONTS = 2
CONT_LEN = 64
PROMPT_LEN = 64

epsilon = 1e-06
rope_base = 1000000.0
masked_score = -1000000000.0

F32 = jnp.float32
BF16 = jnp.bfloat16
COL = ("y", "x")
ROW = ("g", "k")
ALL = ("g", "k", "y", "x")


def block_layout(groups, row_count):
    token_index = jnp.arange(row_count, dtype=jnp.int32)
    prompt_rows = PROMPTS * PROMPT_LEN
    is_prompt = token_index < prompt_rows
    cont_offset = jnp.maximum(token_index - prompt_rows, 0)
    cont_number = cont_offset // CONT_LEN
    segment = jnp.where(is_prompt, token_index // PROMPT_LEN, PROMPTS + cont_number)
    position = jnp.where(is_prompt, token_index % PROMPT_LEN, PROMPT_LEN + cont_offset % CONT_LEN)
    cont_picks = (cont_number[:, None] == jnp.arange(CONTS, dtype=jnp.int32)[None, :]).astype(
        jnp.int32
    )
    source = jnp.where(
        is_prompt[None], segment[None], jnp.sum(cont_picks[None] * groups[:, None, :], axis=2)
    )
    same_segment = (segment[:, None] == segment[None, :]) & (position[None, :] <= position[:, None])
    context = (
        jnp.logical_not(is_prompt)[None, :, None]
        & is_prompt[None, None, :]
        & (source[:, :, None] == segment[None, None, :])
    )
    return (same_segment[None] | context, position)


def rotary_tables(position):
    half_dim = HEAD_DIM // 2
    frequency = rope_base ** (-(2.0 * jnp.arange(half_dim, dtype=F32)) / HEAD_DIM)
    angles = position.astype(F32)[:, None] * frequency[None, :]
    cosine = jnp.cos(angles)
    sine = jnp.sin(angles)
    return (cosine[None, :, None, :], sine[None, :, None, :])


def rotate(values, cosine, sine):
    first, second = jnp.split(values, 2, axis=-1)
    return jnp.concatenate([first * cosine - second * sine, second * cosine + first * sine], -1)


def dot(left, right, dims):
    return lax.dot_general(left, right, (dims, ((), ())), preferred_element_type=F32)


PARTS = 2
EXTRA = 16


def ffn_kernel(sizes, groups, meta, rows_ref, cot_ref, side_ref, *refs):
    n_g, f_pad, f_one, d_own = sizes
    blocks = refs[: groups * 2 * n_g]
    sums = refs[groups * 2 * n_g : -8]
    out_ref, normed_ref, act_ref, gate_ref, up_ref, w_gu, w_down, sems = refs[-8:]
    g_at, k_at, c_at = meta[0], meta[1], meta[2]
    shared = groups == 1

    @pl.when(pl.program_id(0) == 0)
    def _():
        copies = []
        for half in range(2):
            for shift in range(n_g):
                at = half * n_g + shift
                column = 2 * (g_at ^ shift) + (k_at ^ half)
                lanes = pl.ds(pl.multiple_of(column * d_own, d_own), d_own)
                if shared:
                    both, down = blocks[at].at[: 2 * f_pad], blocks[at].at[2 * f_pad :]
                else:
                    both, down = blocks[at], blocks[2 * n_g + at]
                copies.append(
                    pltpu.make_async_copy(both, w_gu.at[: 2 * f_pad, lanes], sems.at[2 * at])
                )
                copies.append(pltpu.make_async_copy(down, w_down.at[:, lanes], sems.at[2 * at + 1]))
        for copy in copies:
            copy.start()
        if shared:
            w_gu[2 * f_pad :, :] = side_ref[...]
        for copy in copies:
            copy.wait()

    rows = rows_ref[...]
    count = rows.shape[0]
    n_c = cot_ref.shape[0]
    cot = jnp.concatenate(
        [
            jnp.concatenate([cot_ref[c ^ c_at, 0, row ^ c_at] for row in range(n_c)], axis=0)
            for c in range(n_c)
        ],
        axis=1,
    )
    minor = ((1,), (1,))
    pre = dot(w_gu[...], rows, minor)
    down_back = dot(w_down[...], cot, minor)
    gate_pre, up_pre = pre[:f_pad], pre[f_pad : 2 * f_pad]
    if shared:
        prob = jax.nn.sigmoid(pre[2 * f_pad : 2 * f_pad + 1])
        scale = jnp.broadcast_to(prob, (f_pad, count))
    else:
        full = f_pad // f_one
        pieces = [jnp.broadcast_to(side_ref[0, e : e + 1, :], (f_one, count)) for e in range(full)]
        if f_pad > full * f_one:
            pieces.append(jnp.zeros((f_pad - full * f_one, count), F32))
        scale = jnp.concatenate(pieces, axis=0)
    sigma = jax.nn.sigmoid(gate_pre)
    silu = gate_pre * sigma
    act = silu * up_pre
    act_grad = down_back * scale
    act_low = (act * scale).astype(BF16)
    gate_low = (act_grad * up_pre * sigma * (1.0 + gate_pre * (1.0 - sigma))).astype(BF16)
    up_low = (act_grad * silu).astype(BF16)
    act_ref[...] = act_low
    gate_ref[:f_pad, :] = gate_low
    up_ref[...] = up_low
    both = [gate_low, up_low]
    if shared:
        prob_part = jnp.sum(act * down_back, axis=0, keepdims=True)
        logit_part = prob_part * prob * (1.0 - prob)
        logit_high = logit_part.astype(BF16).astype(F32)
        logit_rows = jnp.concatenate(
            [logit_high, logit_part - logit_high, jnp.zeros((EXTRA - 2, count), F32)], axis=0
        ).astype(BF16)
        gate_ref[f_pad:, :] = logit_rows
        both.append(logit_rows)
    major = ((0,), (0,))
    out = dot(act_low, w_down[...], major)
    normed = dot(jnp.concatenate(both, axis=0), w_gu[...], major)
    if sums:
        out = out + sums[0][...].astype(F32)
        normed = normed + sums[1][...].astype(F32)
    out_ref[...] = out.astype(BF16)
    normed_ref[...] = normed.astype(BF16)


def ffn_pass(sizes, meta, rows, cot, side, blocks, sums):
    n_g, f_pad, _, d_own = sizes
    total, dim = rows.shape
    n_c, _, _, sub, cw = cot.shape
    tile = n_c * sub
    groups = len(blocks) // (2 * n_g)
    extra = EXTRA if groups == 1 else 0
    flat = lambda i, m: (i, 0)
    wide = lambda i, m: (0, i)
    if groups == 1:
        side_spec = pl.BlockSpec((EXTRA, dim), lambda i, m: (0, 0))
    else:
        side = side.reshape(-1, tile, 8).transpose(0, 2, 1)
        side_spec = pl.BlockSpec((1, 8, tile), lambda i, m: (i, 0, 0))
    return pl.pallas_call(
        functools.partial(ffn_kernel, sizes, groups),
        grid_spec=pltpu.PrefetchScalarGridSpec(
            num_scalar_prefetch=1,
            grid=(n_g,),
            in_specs=[
                pl.BlockSpec((tile, dim), flat),
                pl.BlockSpec((n_c, 1, n_c, sub, cw), lambda i, m: (0, i, 0, 0, 0)),
                side_spec,
            ]
            + [pl.BlockSpec(memory_space=pl.ANY)] * len(blocks)
            + [pl.BlockSpec((tile, dim), flat)] * len(sums),
            out_specs=[
                pl.BlockSpec((tile, dim), flat),
                pl.BlockSpec((tile, dim), flat),
                pl.BlockSpec((f_pad, tile), wide),
                pl.BlockSpec((f_pad + extra, tile), wide),
                pl.BlockSpec((f_pad, tile), wide),
            ],
            scratch_shapes=[
                pltpu.VMEM((2 * f_pad + extra, dim), BF16),
                pltpu.VMEM((f_pad, dim), BF16),
                pltpu.SemaphoreType.DMA((4 * n_g,)),
            ],
        ),
        out_shape=[
            jax.ShapeDtypeStruct((total, dim), BF16),
            jax.ShapeDtypeStruct((total, dim), BF16),
            jax.ShapeDtypeStruct((f_pad, total), BF16),
            jax.ShapeDtypeStruct((f_pad + extra, total), BF16),
            jax.ShapeDtypeStruct((f_pad, total), BF16),
        ],
        compiler_params=pltpu.CompilerParams(
            dimension_semantics=("arbitrary",), vmem_limit_bytes=60 * 1024 * 1024
        ),
        cost_estimate=pl.CostEstimate(
            flops=12 * total * dim * f_pad,
            bytes_accessed=(8 + 4 * len(sums)) * total * dim + 6 * total * f_pad + 6 * f_pad * dim,
            transcendentals=total * f_pad,
        ),
        name="ffn_pass",
    )(meta, rows, cot, side, *blocks, *sums)


def grad_kernel(parts, kinds, f_pad, meta, *refs):
    lefts, refs = refs[: parts * len(kinds)], refs[parts * len(kinds) :]
    values = {}
    for cot in sorted(set(kinds)):
        rights, refs = refs[:parts], refs[parts:]
        if cot:
            _, n_g, n_c, _, _ = rights[0].shape
            order = [(g, c) for g in range(n_g) for c in range(n_c)]
            values[cot] = [
                jnp.concatenate([right[0, g, c ^ meta[2]] for g, c in order], axis=0)
                for right in rights
            ]
        else:
            values[cot] = [right[...] for right in rights]
    for i, cot in enumerate(kinds):
        total = None
        for left, value in zip(lefts[i * parts : (i + 1) * parts], values[cot]):
            term = dot(left[...], value, ((1,), (0,)))
            total = term if total is None else total + term
        refs[0][0, 0, i * f_pad : (i + 1) * f_pad] = total[:f_pad].astype(BF16)
        if total.shape[0] > f_pad:
            refs[1][...] = jnp.broadcast_to(
                total[f_pad : f_pad + 1] + total[f_pad + 1 : f_pad + 2], refs[1].shape
            )


def weight_grad(sizes, meta, kinds, lefts, normed, cots):
    n_g, f_pad, _, d_own = sizes
    parts = len(normed)
    part_rows, dim = normed[0].shape
    extra = max(value[0].shape[0] for value in lefts) > f_pad
    n_c, _, _, sub, cw = cots[0].shape
    per = cw // d_own
    arrays, specs = [], []
    for values in lefts:
        arrays += values
        specs += [pl.BlockSpec(values[0].shape, lambda j, m: (0, 0))] * parts
    if False in kinds:
        arrays += normed
        specs += [pl.BlockSpec((part_rows, d_own), lambda j, m: (0, j))] * parts
    if True in kinds:
        arrays += cots
        specs += [
            pl.BlockSpec(
                (1, n_g, n_c, sub, d_own), lambda j, m: ((j // per) ^ m[2], 0, 0, 0, j % per)
            )
        ] * parts
    f_out = len(kinds) * f_pad
    out_specs = [
        pl.BlockSpec((1, 1, f_out, d_own), lambda j, m: ((j % 2) ^ m[1], (j // 2) ^ m[0], 0, 0))
    ]
    out_shape = [jax.ShapeDtypeStruct((2, n_g, f_out, d_own), BF16)]
    if extra:
        out_specs.append(pl.BlockSpec((8, d_own), lambda j, m: (0, j)))
        out_shape.append(jax.ShapeDtypeStruct((8, dim), F32))
    return pl.pallas_call(
        functools.partial(grad_kernel, parts, kinds, f_pad),
        grid_spec=pltpu.PrefetchScalarGridSpec(
            num_scalar_prefetch=1, grid=(2 * n_g,), in_specs=specs, out_specs=out_specs
        ),
        out_shape=out_shape,
        compiler_params=pltpu.CompilerParams(
            dimension_semantics=("arbitrary",), vmem_limit_bytes=56 * 1024 * 1024
        ),
        cost_estimate=pl.CostEstimate(
            flops=2 * parts * part_rows * dim * f_out,
            bytes_accessed=2 * parts * part_rows * (dim + f_out) + 2 * f_out * dim,
            transcendentals=0,
        ),
        name="weight_grad",
    )(meta, *arrays)


def tie(*values):
    return lax.optimization_barrier(values)


def norm_back(normed_grad, unit_rows, scale, gain):
    weighted = normed_grad * gain
    rows_grad = scale * (
        weighted - unit_rows * jnp.mean(weighted * unit_rows, axis=-1, keepdims=True)
    )
    return (rows_grad, jnp.sum(normed_grad * unit_rows, axis=0))


def swap(value, axis):
    return lax.ppermute(value, axis, [(0, 1), (1, 0)])


def shift_by(value, axis, shift):
    if shift == 0:
        return value
    return lax.ppermute(value, axis, [(i, i ^ shift) for i in range(lax.axis_size(axis))])


def gather_joined(value, axis, at):
    bit = lax.axis_size(axis) // 2
    while bit:
        shape = value.shape[:at] + (2 * value.shape[at],) + value.shape[at + 1 :]
        value = jnp.stack([value, shift_by(value, axis, bit)], axis=at + 1).reshape(shape)
        bit //= 2
    return value


def halve(value, axis, at, bit, after=None):
    size = value.shape[at]
    shape = value.shape[:at] + (size // 2, 2) + value.shape[at + 1 :]
    pair = value.reshape(shape)
    keep, send = (lax.index_in_dim(pair, i, at + 1, keepdims=False) for i in range(2))
    other = shift_by(send, axis, bit)
    if after is not None:
        keep, _ = tie(keep, after)
    return (keep.astype(F32) + other.astype(F32)).astype(BF16)


def col_gather(value, count):
    spread = jnp.broadcast_to(value[None], (count,) + value.shape)
    return lax.all_to_all(spread, COL, 0, 0, tiled=True)


def col_sum(partial, count):
    parts = partial.astype(BF16).reshape((count, -1) + partial.shape[1:])
    return jnp.sum(lax.all_to_all(parts, COL, 0, 0, tiled=True).astype(F32), axis=0)


def rows_to_features(rows, count):
    row_count, width = rows.shape
    parts = rows.reshape(row_count, count, width // count).transpose(1, 0, 2)
    moved = lax.all_to_all(parts, COL, 0, 0, tiled=True)
    blocks = moved.reshape(2, row_count * count // 2, width // count)
    return lax.all_to_all(blocks, "k", 0, 0, tiled=True)


def shards(
    tokens,
    routes,
    route_weights,
    group_ids,
    first_gain,
    query_weight,
    key_weight,
    value_weight,
    output_weight,
    second_gain,
    shared_gate,
    shared_up,
    shared_down,
    shared_logit,
    expert_gate,
    expert_up,
    expert_down,
    cotangent,
):
    n_g = lax.axis_size("g")
    n_c = lax.axis_size("y") * lax.axis_size("x")
    n_y, n_x = lax.axis_size("y"), lax.axis_size("x")
    n_row = 2 * n_g
    at_g, at_k = lax.axis_index("g"), lax.axis_index("k")
    at_c = lax.axis_index(COL)
    block = tokens.shape[1]
    dim = query_weight.shape[0] * n_row
    d_own = query_weight.shape[0]
    width = query_weight.shape[1]
    heads = width // HEAD_DIM
    local_experts = expert_gate.shape[1]
    span = 2 * block
    total = n_g * span
    own_rows = span // n_c
    pick = lambda array, index, axis=0: lax.dynamic_index_in_dim(array, index, axis, keepdims=False)

    labels = jnp.arange(EXPERTS, dtype=jnp.int32)
    mixing = jnp.sum(
        jnp.where(
            routes[:, None] == labels[None, :, None, None], route_weights[:, None], 0.0
        ),
        axis=-1,
    )
    small = jnp.concatenate(
        [
            mixing.reshape(2 * EXPERTS, block),
            jnp.zeros((8, block), F32)
            .at[0, :d_own].set(first_gain.astype(F32))
            .at[1, :d_own].set(second_gain.astype(F32))
            .at[2, :d_own].set(shared_logit.astype(F32))
            .at[3, : 2 * CONTS].set(group_ids.astype(F32).reshape(-1)),
        ],
        axis=0,
    )
    small_all = lax.all_to_all(
        jnp.broadcast_to(small[None], (n_row,) + small.shape), ROW, 0, 0, tiled=True
    )
    f_shared = shared_gate.shape[1] // n_g
    f_routed = expert_gate.shape[2] // n_g
    f_experts = local_experts * f_routed
    f_one, f_two = -(-f_shared // 16) * 16, -(-f_experts // 16) * 16
    sizes_s = (n_g, f_one, f_shared, d_own)
    sizes_e = (n_g, f_two, f_routed, d_own)
    meta = jnp.stack([at_g, at_k, at_c]).astype(jnp.int32)

    def fill(value, size):
        return jnp.pad(value, ((0, 0), (0, size - value.shape[1]), (0, 0)))

    def slices_s(value):
        return fill(value.reshape(n_g, f_shared, d_own), f_one)

    def slices_e(value):
        value = value.reshape(local_experts, n_g, f_routed, d_own).transpose(1, 0, 2, 3)
        return fill(value.reshape(n_g, f_experts, d_own), f_two)

    weight_slices = [
        jnp.concatenate([slices_s(w) for w in (shared_gate.T, shared_up.T, shared_down)], axis=1),
        jnp.concatenate([slices_e(w.transpose(1, 2, 0)) for w in (expert_gate, expert_up)], axis=1),
        slices_e(expert_down),
    ]
    picked = [[pick(value, at_g ^ shift) for shift in range(n_g)] for value in weight_slices]
    qkv = lax.all_gather(
        jnp.concatenate([query_weight, key_weight, value_weight], axis=1), ROW, axis=0, tiled=True
    )
    out_w = lax.all_gather(output_weight, ROW, axis=1, tiled=True)
    picked[0], qkv, small_all = tie(picked[0], qkv, small_all)
    own_blocks = [
        [shift_by(value, "g", shift) for shift, value in enumerate(values)] for values in picked
    ]

    token_part = lax.all_to_all(tokens, "k", 0, 0, tiled=True).reshape(span, -1)
    cot_part = lax.all_to_all(cotangent, "k", 0, 0, tiled=True).reshape(span, -1)

    sub = own_rows // PARTS
    cot_rows = cot_part.reshape(1, n_c, PARTS, sub, dim // n_c)
    far = shift_by(cot_rows, "g", n_g // 2)
    cot_rows, far, qkv = tie(cot_rows, far, qkv)
    cot_rows = jnp.concatenate([cot_rows, far], axis=0)
    bit = n_g // 4
    while bit:
        far = shift_by(cot_rows, "g", bit)
        cot_rows = jnp.stack([cot_rows, far], axis=1).reshape((-1,) + cot_rows.shape[1:])
        bit //= 2
    inputs = col_gather(token_part, n_c).reshape(n_c, span, -1).transpose(1, 0, 2)
    inputs = inputs.reshape(span, dim).astype(F32)

    gain_1 = small_all[:, 16, :d_own].reshape(dim)
    gain_2 = small_all[:, 17, :d_own].reshape(dim)
    logit_w = small_all[:, 18, :d_own].reshape(dim)
    groups_all = small_all[:, 19, : 2 * CONTS].reshape(n_g, 2, 2, CONTS)
    groups = pick(pick(groups_all, at_g), at_k, 1).astype(jnp.int32)
    mixing_all = small_all[:, : 2 * EXPERTS].reshape(n_row, 2, EXPERTS, block)
    mixing_own = lax.dynamic_slice_in_dim(
        pick(mixing_all, at_k, 1), at_c * local_experts, local_experts, 1
    )
    mixing_own = mixing_own.transpose(0, 2, 1).reshape(total, local_experts)

    first_scale = lax.rsqrt(jnp.mean(inputs * inputs, axis=-1, keepdims=True) + epsilon)
    normed_1 = (inputs * first_scale * gain_1).astype(BF16)
    projected = dot(normed_1, qkv, ((1,), (0,)))
    allowed, position = block_layout(groups, block)
    cosine, sine = rotary_tables(position)
    head_shape = (2, block, heads, HEAD_DIM)
    query_rot = rotate(projected[:, :width].reshape(head_shape), cosine, sine).astype(BF16)
    key_rot = rotate(projected[:, width : 2 * width].reshape(head_shape), cosine, sine).astype(BF16)
    value_low = projected[:, 2 * width :].reshape(head_shape).astype(BF16)

    def einsum(form, left, right):
        return jnp.einsum(form, left, right, preferred_element_type=F32)

    scores = jnp.where(
        allowed[:, None],
        einsum("bqhd,bkhd->bhqk", query_rot, key_rot) * (1.0 / math.sqrt(HEAD_DIM)),
        masked_score,
    )
    peak = jnp.max(scores, axis=-1, keepdims=True)
    exp_scores = jnp.exp(scores - peak)
    probabilities = exp_scores / jnp.sum(exp_scores, axis=-1, keepdims=True)
    prob_low = probabilities.astype(BF16)
    mixed = einsum("bhqk,bkhd->bqhd", prob_low, value_low).astype(BF16).reshape(span, width)
    cot_rows, mixed, own_blocks[0][1] = tie(cot_rows, mixed, own_blocks[0][1])
    attention = col_sum(dot(mixed, out_w, ((1,), (0,))), n_c)
    cot_all = []
    for part in range(PARTS):
        value = cot_rows[:, :, part][None, None]
        axis = ("x", "y")[1 - part % 2]
        cot_all.append(gather_joined(value, axis, ("y", "x").index(axis)))
    cot_all, attention = tie(cot_all, attention)
    for part in range(PARTS):
        axis = ("x", "y")[part % 2]
        value = gather_joined(cot_all[part], axis, ("y", "x").index(axis))
        cot_all[part] = value.reshape(n_c, n_g, n_c, sub, dim // n_c)
    own_inputs = lax.dynamic_slice_in_dim(inputs, at_c * own_rows, own_rows, 0)
    own_blocks[0][2:], attention = tie(own_blocks[0][2:], attention)
    hidden = own_inputs + attention
    second_scale = lax.rsqrt(jnp.mean(hidden * hidden, axis=-1, keepdims=True) + epsilon)
    unit_2 = hidden * second_scale
    normed_own = (unit_2 * gain_2).astype(BF16)

    def gather_cols(value):
        sides = []
        for side, order in enumerate((("y", "x"), ("x", "y"))):
            half = value[..., side * (dim // 2) : (side + 1) * (dim // 2)]
            for axis in order:
                half = gather_joined(half, axis, 1 + ("y", "x").index(axis))
            sides.append(half)
        return jnp.concatenate(sides, axis=-1).reshape(-1, dim)

    routed_gu, routed_d = own_blocks[1:]
    halves = [normed_own[part * sub : (part + 1) * sub][None] for part in range(PARTS)]
    halves[0] = gather_joined(halves[0], "g", 0)
    halves[0], halves[1], routed_gu[1] = tie(halves[0], halves[1], routed_gu[1])
    halves[1] = gather_joined(halves[1], "g", 0)
    normed_parts = [gather_cols(halves[0][:, None, None])]
    normed_parts[0], halves[1], routed_gu[2:3], cot_all = tie(
        normed_parts[0], halves[1], routed_gu[2:3], cot_all
    )
    normed_parts.append(gather_cols(halves[1][:, None, None]))
    normed_parts[1], routed_gu[3:], routed_d[1] = tie(
        normed_parts[1], routed_gu[3:], routed_d[1]
    )
    own_cot = [
        lax.dynamic_index_in_dim(cot[:, 0], at_c, 1, keepdims=False) for cot in cot_all
    ]
    own_cot = jnp.concatenate(own_cot, axis=1)
    own_cot = jnp.stack([pick(own_cot, at_c ^ c) for c in range(n_c)], axis=1)
    own_cot = own_cot.reshape(own_rows, dim)

    def own_core(grad, after=None):
        other = swap(grad[1], "k")
        grad = grad[0]
        if after is not None:
            grad, _ = tie(grad, after)
        return (grad.astype(F32) + other.astype(F32)).astype(BF16)

    def send_slices(both):
        return [shift_by(both[shift], "g", shift) for shift in range(n_g)]

    def place_slices(moved, kinds):
        moved = jnp.stack(moved)
        moved = jnp.stack([pick(moved, at_g ^ source) for source in range(n_g)])
        return [
            moved[:, i * (moved.shape[1] // kinds) :][:, : moved.shape[1] // kinds]
            for i in range(kinds)
        ]

    def place_s(value):
        return value[:, :f_shared].reshape(n_g * f_shared, d_own)

    def place_e(value):
        value = value[:, :f_experts].reshape(n_g, local_experts, f_routed, d_own)
        return value.transpose(1, 0, 2, 3).reshape(local_experts, n_g * f_routed, d_own)

    logit_low = jnp.zeros((EXTRA, dim), BF16).at[:2].set(logit_w.astype(BF16)[None])
    mixing_parts = mixing_own.reshape(n_g, n_c, PARTS, sub, local_experts)
    mixing_parts = jnp.stack([pick(mixing_parts, at_g ^ shift) for shift in range(n_g)])
    mixing_parts = jnp.stack([pick(mixing_parts, at_c ^ c, 1) for c in range(n_c)], axis=1)
    mixing_parts = jnp.pad(mixing_parts, ((0, 0),) * 4 + ((0, 8 - local_experts),))
    def blocks_of(values):
        return values + [swap(value, "k") for value in values]

    blocks_s = blocks_of(own_blocks[0])
    passes_s = [
        ffn_pass(sizes_s, meta, normed_parts[part], cot_all[part], logit_low, blocks_s, [])
        for part in range(PARTS)
    ]
    kinds = (False, False, True)
    grad_s, logit_sum = weight_grad(
        sizes_s, meta, kinds, [[p[i] for p in passes_s] for i in (3, 4, 2)], normed_parts, cot_all
    )
    logit_sum = logit_sum[0]
    sums = [[passes_s[part][0], passes_s[part][1]] for part in range(PARTS)]
    sums[0], grad_s = tie(sums[0], grad_s)
    own_blocks[2], sums[1] = tie(own_blocks[2], sums[1])
    blocks_e = blocks_of(own_blocks[1]) + blocks_of(own_blocks[2])
    passes = []
    for part in range(PARTS):
        if part == 1:
            both_s = own_core(grad_s, passes[0][2][:16, :128])
            sums[1], both_s = tie(sums[1], both_s)
        passes.append(
            ffn_pass(
                sizes_e,
                meta,
                normed_parts[part],
                cot_all[part],
                mixing_parts[:, :, part].reshape(-1, 8),
                blocks_e,
                sums[part],
            )
        )
    moved_s = send_slices(both_s)

    def split_sides(partial):
        part = partial.reshape(n_g, n_y, n_x, sub, dim)
        return [part[..., : dim // 2], part[..., dim // 2 :]]

    def scatter_axis(value, axis, at, after=None):
        bit = 1
        while bit < lax.axis_size(axis):
            value = halve(value, axis, at, bit, after)
            bit *= 2
        return lax.index_in_dim(value, 0, at, keepdims=False)

    def cols_first(sides, after=None):
        return [scatter_axis(sides[0], "x", 2, after), scatter_axis(sides[1], "y", 1, after)]

    def cols_second(sides):
        sides = [scatter_axis(sides[0], "y", 1), scatter_axis(sides[1], "x", 1)]
        return jnp.concatenate(sides, axis=-1)

    def chips_steps(value):
        bit = 1
        while 2 * bit < n_g:
            value = halve(value, "g", 0, bit)
            bit *= 2
        return value

    def chips_last(value, after=None):
        other = shift_by(value[1], "g", n_g // 2)
        keep = value[0]
        if after is not None:
            keep, _ = tie(keep, after)
        return keep.astype(F32) + other.astype(F32)

    acts, gates, ups = ([parts[i] for parts in passes] for i in (2, 3, 4))
    first = cols_first(split_sides(passes[0][1]), passes[1][2][:16, :128])
    first, acts = tie(first, acts)
    (grad_d,) = weight_grad(sizes_e, meta, (True,), [acts], normed_parts, cot_all)
    first = cols_second(first)
    second = cols_first(split_sides(passes[1][1]))
    first, second, gates, grad_d = tie(first, second, gates, grad_d)
    (grad_gu,) = weight_grad(sizes_e, meta, (False, False), [gates, ups], normed_parts, cot_all)
    first = chips_steps(first)
    second = cols_second(second)
    both_d = own_core(grad_d)
    first, second, both_d, moved_s[1:3], grad_gu = tie(first, second, both_d, moved_s[1:3], grad_gu)
    moved_d = send_slices(both_d)
    first = chips_last(first)
    second = chips_steps(second)
    both_gu = own_core(grad_gu)
    first, second, both_gu = tie(first, second, both_gu)
    second = chips_last(second)
    out_sides = [cols_first(split_sides(parts[0])) for parts in passes]
    moved_gu = send_slices(both_gu)
    normed_grad_2 = jnp.concatenate([first, second], axis=0)
    normed_grad_2, moved_s[3:] = tie(normed_grad_2, moved_s[3:])
    hidden_part, gain_2_sum = norm_back(normed_grad_2, unit_2, second_scale, gain_2)
    hidden_grad = own_cot.astype(F32) + hidden_part
    attn_grad = col_gather(hidden_grad.astype(BF16), n_c).reshape(span, dim)
    attn_grad, moved_d[1:] = tie(attn_grad, moved_d[1:])
    gate_s, up_s, down_s = (place_s(value) for value in place_slices(moved_s, 3))
    down_e = place_e(place_slices(moved_d, 1)[0])

    out_grad = dot(attn_grad, mixed, ((0,), (0,)))
    mixed_grad = dot(attn_grad, out_w, ((1,), (1,))).astype(BF16).reshape(head_shape)
    out_sides, mixed_grad = tie(out_sides, mixed_grad)
    out_parts = [cols_second(sides) for sides in out_sides]
    prob_grad = einsum("bqhd,bkhd->bhqk", mixed_grad, value_low)
    value_grad = einsum("bhqk,bqhd->bkhd", prob_low, mixed_grad).astype(BF16)
    center = jnp.sum(prob_grad * probabilities, axis=-1, keepdims=True)
    score_grad = (probabilities * (prob_grad - center) * (1.0 / math.sqrt(HEAD_DIM))).astype(BF16)
    out_parts, score_grad, moved_gu[1] = tie(out_parts, score_grad, moved_gu[1])
    out_parts = [chips_steps(part) for part in out_parts]
    query_grad = rotate(einsum("bhqk,bkhd->bqhd", score_grad, key_rot), cosine, -sine).astype(BF16)
    key_grad = rotate(einsum("bhqk,bqhd->bkhd", score_grad, query_rot), cosine, -sine).astype(BF16)
    qkv_grad = jnp.concatenate(
        [part.reshape(span, width) for part in (query_grad, key_grad, value_grad)], axis=1
    )
    qkv_grad, moved_gu[2:3] = tie(qkv_grad, moved_gu[2:3])
    qkv_sum = dot(normed_1, qkv_grad, ((0,), (0,)))
    normed_grad_1 = col_sum(dot(qkv_grad, qkv, ((1,), (1,))), n_c)
    normed_grad_1, moved_gu[3:], out_parts = tie(normed_grad_1, moved_gu[3:], out_parts)
    gate_e, up_e = (place_e(value) for value in place_slices(moved_gu, 2))
    own_scale = lax.dynamic_slice_in_dim(first_scale, at_c * own_rows, own_rows, 0)
    rows_part, gain_1_sum = norm_back(normed_grad_1, own_inputs * own_scale, own_scale, gain_1)
    token_rows = (hidden_grad + rows_part).astype(BF16)
    token_moved = rows_to_features(token_rows, n_c)
    token_grad = token_moved.astype(F32)

    out_rows = [chips_last(part, token_moved[:, :16, :128]) for part in out_parts]
    out_rows = jnp.concatenate(out_rows, axis=0)
    result = rows_to_features((hidden + out_rows).astype(BF16), n_c)

    sums = jnp.stack([gain_1_sum, gain_2_sum, logit_sum]).reshape(3, n_row, d_own)
    sums, result = tie(sums, result)
    sums = jnp.broadcast_to(sums.transpose(1, 0, 2)[:, None], (n_row, n_c, 3, d_own))
    sums = lax.all_to_all(sums.reshape(n_row * n_c, 3, d_own), ALL, 0, 0, tiled=True)
    sums = jnp.sum(sums, axis=0)

    out_w_grad = lax.psum_scatter(out_grad.astype(BF16), ROW, scatter_dimension=0, tiled=True)
    qkv_own = lax.psum_scatter(qkv_sum.astype(BF16), ROW, scatter_dimension=0, tiled=True)
    qkv_own = qkv_own.astype(F32)
    return (
        result,
        token_grad,
        sums[0],
        qkv_own[:, :width],
        qkv_own[:, width : 2 * width],
        qkv_own[:, 2 * width :],
        out_w_grad.T.astype(F32),
        sums[1],
        gate_s.T.astype(F32),
        up_s.T.astype(F32),
        down_s.astype(F32),
        sums[2],
        gate_e.transpose(2, 0, 1).astype(F32),
        up_e.transpose(2, 0, 1).astype(F32),
        down_e.astype(F32),
    )


def solution(mesh):
    n_row, n_col = mesh.shape["row"], mesh.shape["col"]
    inner = Mesh(mesh.devices.reshape(n_row // 2, 2, n_col // 2, 2), ALL)
    return jax.shard_map(
        shards,
        mesh=inner,
        in_specs=(
            P(None, ROW, COL),
            P(None, ROW, None),
            P(None, ROW, None),
            P(None, ROW),
            P(ROW),
            P(ROW, COL),
            P(ROW, COL),
            P(ROW, COL),
            P(COL, ROW),
            P(ROW),
            P(ROW, COL),
            P(ROW, COL),
            P(COL, ROW),
            P(ROW),
            P(ROW, COL, None),
            P(ROW, COL, None),
            P(COL, None, ROW),
            P(None, ROW, COL),
        ),
        out_specs=(
            P(None, ROW, COL),
            P(None, ROW, COL),
            P(ROW),
            P(ROW, COL),
            P(ROW, COL),
            P(ROW, COL),
            P(COL, ROW),
            P(ROW),
            P(ROW, COL),
            P(ROW, COL),
            P(COL, ROW),
            P(ROW),
            P(ROW, COL, None),
            P(ROW, COL, None),
            P(COL, None, ROW),
        ),
        check_vma=False,
    )
```
